32 devices in a mesh: clu: 8 (over z, x), col: 4 (over y, core).
Axes of the slice: x: 2, y: 2, z: 4, core: 2. Of those that a mesh axis runs over, the one named last changes fastest.
Arguments:
- features: bfloat16 [65536, 2048], P('clu', 'col'), may hold values from -6 to 6
- weight: bfloat16 [2048, 2048], P(None, 'col'), may hold values from -0.125 to 0.125
- bias: bfloat16 [2048], P('col'), may hold values from -3 to 3
- adjacency: int32 [65536, 128], P('clu'), may hold values from 0 to 1, as said below
- segments: int32 [512, 128], P('clu'), may hold values from 0 to 3, never falling along the last dimension, each value on 1 to 48 neighbouring positions
- cotangent: bfloat16 [65536, 2048], P('clu', 'col'), may hold values from -6 to 6
Outputs:
- activations: bfloat16 [65536, 2048], P('clu', 'col')
- grad_features: float32 [65536, 2048], P('clu', 'col')
- grad_weight: float32 [2048, 2048], P(None, 'col')
- grad_bias: float32 [2048], P('col')
The draws below stay inside these ranges and needn't reach their ends.
Inputs may be any that keep to these rules, and one draw needn't show every extreme that they name: `adjacency`: 0 or 1; within each block of 128 nodes the links are symmetric and a node has no link to itself.
All inputs are finite; a program needn't handle non-finite values.
Results may differ from the reference program's by a relative error of at most 0.0065.
The reference program's roundings to bfloat16 on the way count: a program that leaves them out, or rounds other values in their place, can miss the bound.
Values may be sent and summed in bfloat16 or wider, within the bound.
A program may use at most 256 MiB of HBM per device.

```python
import math
import jax
import jax.numpy as jnp
import numpy as np
from jax import lax

D = 2048
BLOCK = 128
CLUSTERS = 4
MOST = 48
NODES = 65536
BLOCKS = 512


def draw_adjacency(key, part):
    first, second = jax.random.split(jax.random.fold_in(key, 7))
    chance = jax.random.randint(first, (BLOCKS, 1, 1), 4, 40)
    rolls = jax.random.randint(second, (BLOCKS, BLOCK, BLOCK), 0, 100)
    places = jnp.arange(BLOCK)
    upper = (places[None, :, None] < places[None, None, :]) & (rolls < chance)
    linked = upper | jnp.swapaxes(upper, 1, 2)
    return linked.astype(jnp.int32).reshape(BLOCKS * BLOCK, BLOCK)


def shard_levels(key, extent, cuts, low, largest):
    loudness, own = 1.0, jax.random.fold_in(key, 6)
    for position, blocks in cuts:
        heights = jnp.exp(jax.random.uniform(jax.random.fold_in(own, position), (blocks,), jnp.float32, low / len(cuts), largest / len(cuts)))
        loudness = loudness * jnp.repeat(heights, extent[position] // blocks).reshape([-1 if axis == position else 1 for axis in range(len(extent))])
    return loudness


def profile(count, total, limit, slope):
    portions = [(1 << 20) // math.isqrt(standing ** slope) + 1 for standing in range(2, count + 1)]
    rest, given = total - limit - (count - 1), [1] * (count - 1)
    while rest > 0:
        movable = [i for i in range(count - 1) if given[i] < limit]
        mass, left = sum([portions[i] for i in movable]), rest
        for i in movable:
            extra = min(limit - given[i], max(1, left * portions[i] // mass), rest)
            given[i] = given[i] + extra
            rest = rest - extra
    return np.array([limit] + given)


def ragged_sizes(stream_key, number_of, total, reach, lean):
    if number_of == 2:
        one = jax.random.randint(stream_key, (), max(1, total - reach), min(reach, total - 1) + 1)
        return jnp.stack([one, total - one])
    sizes = jnp.asarray(profile(number_of, total, reach, lean), jnp.int32)
    twos = (number_of - 1) // 2
    donor, receiver = sizes[1:1 + 2 * twos:2], sizes[2:2 + 2 * twos:2]
    margin = jnp.minimum(donor - 1, reach - receiver)
    moved = jax.random.randint(jax.random.fold_in(stream_key, 1), (twos,), 0, 1 << 20) % (margin + 1)
    sizes = sizes.at[1:1 + 2 * twos:2].set(donor - moved).at[2:2 + 2 * twos:2].set(receiver + moved)
    return sizes[jax.random.permutation(jax.random.fold_in(stream_key, 2), number_of)]


def bell_draw(stream_key, shape, width, limit, shards=(), held_as=jnp.bfloat16):
    level = shard_levels(stream_key, shape, shards, -0.22, 0.18) if shards else 1.0
    array = jax.random.normal(stream_key, shape, jnp.float32) * width * level
    return jnp.minimum(jnp.maximum(array, -limit), limit).astype(held_as)


def setup_inputs(seed: int = 0) -> dict:
    seeds = jax.random.split(jax.random.key(seed), 7)
    return {
        "features": bell_draw(seeds[0], (NODES, D), 1.0, 6.0, ((0, 8), (1, 4))),
        "weight": bell_draw(seeds[1], (D, D), D ** -0.5, 0.125, ((1, 4),)),
        "bias": bell_draw(seeds[2], (D,), 0.5, 3.0, ((0, 4),)),
        "adjacency": draw_adjacency(jax.random.fold_in(seeds[6], 71), 0),
        "segments": jax.vmap(lambda own: jnp.searchsorted(jnp.cumsum(ragged_sizes(own, CLUSTERS, BLOCK, MOST, 2)), jnp.arange(BLOCK), side="right"))(jax.random.split(seeds[4], BLOCKS)).reshape((BLOCKS, BLOCK)).astype(jnp.int32),
        "cotangent": bell_draw(seeds[5], (NODES, D), 1.0, 6.0, ((0, 8), (1, 4))),
    }


@jax.custom_vjp
def low(v):
    return lax.optimization_barrier(v.astype(jnp.bfloat16)).astype(jnp.float32)

@jax.custom_vjp
def low_back(v):
    return v

def low_keep(v):
    return (low(v), None)

def low_pass(kept, grad):
    return (grad,)

def back_keep(v):
    return (v, None)

def back_low(kept, grad):
    return (low(grad),)
low.defvjp(low_keep, low_pass)
low_back.defvjp(back_keep, back_low)

def build_stencil(adjacency, segments):
    blocks = segments.shape[0]
    linked = adjacency.reshape(blocks, BLOCK, BLOCK).astype(jnp.float32)
    same_cluster = segments[:, :, None] == segments[:, None, :]
    links = jnp.where(same_cluster, linked, jnp.float32(0.0))
    degree = lax.optimization_barrier(jnp.sum(links, axis=-1))
    eye = jnp.eye(BLOCK, dtype=jnp.float32)
    stencil = links + 2.0 * eye[None, :, :]
    inverse = (1.0 / (degree + 1.0)).reshape(-1)
    return (stencil, inverse)

def reference(features, weight, bias, adjacency, segments, cotangent):
    stencil, inverse = build_stencil(adjacency, segments)
    blocks = stencil.shape[0]

    def forward(feats, weights, biases):
        grouped = feats.reshape(blocks, BLOCK, D)
        summed = jnp.einsum('bij,bjf->bif', stencil, grouped, precision=lax.Precision.HIGHEST).reshape(-1, D)
        summed = low_back(summed)
        aggregated = low_back(low(summed * inverse[:, None]))
        preact = jnp.dot(aggregated, weights, precision=lax.Precision.HIGHEST) + biases[None, :]
        return jnp.maximum(low_back(preact), 0.0)
    output, pullback = jax.vjp(forward, features.astype(jnp.float32), weight.astype(jnp.float32), bias.astype(jnp.float32))
    grad_feats, grad_weights, grad_biases = pullback(cotangent.astype(jnp.float32))
    return (output.astype(jnp.bfloat16), grad_feats, grad_weights, grad_biases)
```

```python
import functools

import jax
import jax.numpy as jnp
from jax import lax
from jax.experimental import pallas as pl
from jax.experimental.pallas import tpu as pltpu
from jax.sharding import PartitionSpec as P

BLOCK = 128
F32 = jnp.float32
BF16 = jnp.bfloat16
ANY = pl.BlockSpec(memory_space=pl.ANY)


def params(mib):
    return pltpu.CompilerParams(dimension_semantics=("arbitrary",), vmem_limit_bytes=mib << 20)


def whole(shape):
    return pl.BlockSpec(shape, lambda *_: (0,) * len(shape))


def stencil_of(adjacency, segment):
    columns = jnp.broadcast_to(segment, (BLOCK, BLOCK))
    links = jnp.where(columns == columns.T, adjacency, 0).astype(F32)
    inverse = 1.0 / (jnp.sum(links, axis=1, keepdims=True) + 1.0)
    row = lax.broadcasted_iota(jnp.int32, (BLOCK, BLOCK), 0)
    column = lax.broadcasted_iota(jnp.int32, (BLOCK, BLOCK), 1)
    return (links + jnp.where(row == column, 2.0, 0.0)).astype(BF16), inverse


def aggregate_kernel(first, tile, features, adjacency, segments, out):
    step = pl.program_id(0)
    for b in range(tile // BLOCK):
        rows = pl.ds(b * BLOCK, BLOCK)
        index = first // BLOCK + step * (tile // BLOCK) + b
        stencil, inverse = stencil_of(adjacency[rows, :], segments[pl.ds(index, 1), :])
        summed = jnp.dot(stencil, features[rows, :], preferred_element_type=F32)
        out[rows, :] = (summed * inverse).astype(BF16)


def aggregate(features, adjacency, segments, first, size):
    width, tile = features.shape[1], min(size, 512)
    offset = first // tile
    return pl.pallas_call(
        functools.partial(aggregate_kernel, first, tile),
        grid=(size // tile,),
        in_specs=[
            pl.BlockSpec((tile, width), lambda i: (offset + i, 0)),
            pl.BlockSpec((tile, BLOCK), lambda i: (offset + i, 0)),
            whole(segments.shape),
        ],
        out_specs=pl.BlockSpec((tile, width), lambda i: (i, 0)),
        out_shape=jax.ShapeDtypeStruct((size, width), BF16),
        cost_estimate=pl.CostEstimate(
            flops=2 * size * BLOCK * width, bytes_accessed=size * (4 * width + 4 * BLOCK), transcendentals=0
        ),
        compiler_params=params(32),
    )(features, adjacency, segments)


def forward_kernel(n, start, tile, order, *refs):
    pieces, (weight, bias, cotangent) = refs[:n], refs[n : n + 3]
    if start:
        out, grad, total, total_bias = refs[n + 3 :]
        total_in = total_bias_in = None
    else:
        total_in, total_bias_in, _, out, grad, total, total_bias = refs[n + 3 :]
    width = weight.shape[1]

    @pl.when(pl.program_id(0) == 0)
    def _():
        total[...] = jnp.zeros_like(total) if start else total_in[...]
        total_bias[...] = jnp.zeros_like(total_bias) if start else total_bias_in[...]

    preact = None
    for p in range(n):
        rows = pl.ds(pl.multiple_of(order[p] * width, width), width)
        term = jnp.dot(pieces[p][...], weight[rows, :], preferred_element_type=F32)
        preact = term if preact is None else preact + term
    preact = preact + bias[...].astype(F32)
    out[...] = jnp.maximum(preact, 0.0).astype(BF16)
    grad_preact = jnp.where(preact > 0.0, cotangent[...].astype(F32), 0.0)
    total_bias[...] += jnp.sum(grad_preact.reshape(tile // 8, 8, width), axis=0)
    grad_preact = grad_preact.astype(BF16)
    grad[...] = grad_preact
    for p in range(n):
        rows = pl.ds(pl.multiple_of(order[p] * width, width), width)
        total[rows, :] += lax.dot_general(
            pieces[p][...], grad_preact, (((0,), (0,)), ((), ())), preferred_element_type=F32
        )


def forward(order, pieces, weight, bias, cotangent, carried, first):
    n, (size, width) = len(pieces), pieces[0].shape
    rows, depth = cotangent.shape[0], weight.shape[0]
    tile = min(size, 512)
    offset = first // tile
    start = carried is None
    small = lambda shape: pl.BlockSpec(shape, lambda i, order: (0,) * len(shape))
    here = pl.BlockSpec((tile, width), lambda i, order: (i, 0))
    there = pl.BlockSpec((tile, width), lambda i, order: (offset + i, 0))
    in_specs = [here] * n + [small((depth, width)), small((1, width)), there]
    operands = list(pieces) + [weight, bias, cotangent]
    aliases = {}
    if not start:
        in_specs += [small((depth, width)), small((8, width)), ANY]
        operands += list(carried)
        aliases = {n + 4: 2, n + 5: 3, n + 6: 0}
    out, grad, total, total_bias = pl.pallas_call(
        functools.partial(forward_kernel, n, start, tile),
        grid_spec=pltpu.PrefetchScalarGridSpec(
            num_scalar_prefetch=1,
            grid=(size // tile,),
            in_specs=in_specs,
            out_specs=[there, here, small((depth, width)), small((8, width))],
        ),
        out_shape=[
            jax.ShapeDtypeStruct((rows, width), BF16),
            jax.ShapeDtypeStruct((size, width), BF16),
            jax.ShapeDtypeStruct((depth, width), F32),
            jax.ShapeDtypeStruct((8, width), F32),
        ],
        input_output_aliases=aliases,
        cost_estimate=pl.CostEstimate(
            flops=4 * size * depth * width,
            bytes_accessed=size * (2 * depth + 6 * width) + depth * width * 10,
            transcendentals=0,
        ),
        compiler_params=params(44),
    )(order, *operands)
    return grad, (total, total_bias, out)


def backward_kernel(n, first, tile, *refs):
    grads, weights, (adjacency, segments), out = refs[:n], refs[n : 2 * n], refs[2 * n : 2 * n + 2], refs[-1]
    step = pl.program_id(0)
    grad = None
    for p in range(n):
        term = lax.dot_general(
            grads[p][...], weights[p][...], (((1,), (1,)), ((), ())), preferred_element_type=F32
        )
        grad = term if grad is None else grad + term
    grad = grad.astype(BF16)
    for b in range(tile // BLOCK):
        rows = pl.ds(b * BLOCK, BLOCK)
        index = first // BLOCK + step * (tile // BLOCK) + b
        stencil, inverse = stencil_of(adjacency[rows, :], segments[pl.ds(index, 1), :])
        summed = (grad[b * BLOCK : (b + 1) * BLOCK].astype(F32) * inverse).astype(BF16)
        out[rows, :] = jnp.dot(stencil, summed, preferred_element_type=F32)


def backward(grads, weights, adjacency, segments, carried, first):
    n, (size, width) = len(grads), grads[0].shape
    rows = adjacency.shape[0]
    tile = min(size, 512)
    offset = first // tile
    here = pl.BlockSpec((tile, width), lambda i: (i, 0))
    in_specs = (
        [here] * n
        + [whole(w.shape) for w in weights]
        + [pl.BlockSpec((tile, BLOCK), lambda i: (offset + i, 0)), whole(segments.shape)]
    )
    operands = list(grads) + list(weights) + [adjacency, segments]
    aliases = {}
    if carried is not None:
        in_specs.append(ANY)
        aliases = {len(operands): 0}
        operands.append(carried)
    return pl.pallas_call(
        functools.partial(backward_kernel, n, first, tile),
        grid=(size // tile,),
        in_specs=in_specs,
        out_specs=pl.BlockSpec((tile, width), lambda i: (offset + i, 0)),
        out_shape=jax.ShapeDtypeStruct((rows, width), F32),
        input_output_aliases=aliases,
        cost_estimate=pl.CostEstimate(
            flops=2 * size * width * (n * width + BLOCK),
            bytes_accessed=size * (2 * n * width + 4 * width + 4 * BLOCK) + n * width * width * 2,
            transcendentals=0,
        ),
        compiler_params=params(32),
    )(*operands)


def chunk_sizes(rows):
    sizes = [512] + [1024] * ((rows - 1024) // 1024) + [256, 256]
    return sizes if sum(sizes) == rows else [rows]


def build(n, clusters):
    outer = n // 2

    def device(chip, core):
        return (chip % outer) * 2 + core

    def from_chip(x, shift):
        pairs = [(device(chip + shift, core), device(chip, core)) for chip in range(outer) for core in range(2)]
        return lax.ppermute(x, "col", pairs)

    def from_sibling(x):
        return lax.ppermute(x, "col", [(i, i ^ 1) for i in range(n)])

    def after(x, *others):
        return lax.optimization_barrier((x,) + others)[0]

    def sum_clusters(x):
        if clusters & (clusters - 1):
            return lax.psum(x, "clu")
        step = 1
        while step < clusters:
            x = x + lax.ppermute(x, "clu", [(i, i ^ step) for i in range(clusters)])
            step *= 2
        return x

    def gather_weight(weight, order, width):
        me = lax.axis_index("col")
        chip, core = me // 2, me % 2
        mine = lambda c: lax.dynamic_slice_in_dim(weight, c * width, width, 0)
        blocks = [mine(me), from_sibling(mine(me ^ 1))]
        part = 2 * width // clusters
        for shift in range(1, outer):
            base = ((chip - shift + outer) % outer) * 2 * width + lax.axis_index("clu") * part
            piece = from_chip(lax.dynamic_slice_in_dim(weight, base, part, 0), shift)
            rows = lax.all_gather(piece, "clu", axis=0, tiled=True)
            own = lax.dynamic_slice_in_dim(rows, core * width, width, 0)
            other = lax.dynamic_slice_in_dim(rows, (1 - core) * width, width, 0)
            blocks += [own, from_sibling(other)]
        return blocks

    def local(features, weight, bias, adjacency, segments, cotangent):
        rows, width = features.shape
        me = lax.axis_index("col")
        chip, core = me // 2, me % 2
        order = jnp.stack(
            [((chip + p // 2) % outer) * 2 + (core if p % 2 == 0 else 1 - core) for p in range(n)]
        ).astype(jnp.int32)
        bias = bias.reshape(1, width)
        sizes = chunk_sizes(rows)
        starts = [sum(sizes[:k]) for k in range(len(sizes))]
        window = 3
        arrived = []

        def send(x):
            if len(arrived) >= window:
                x = after(x, *arrived[-window])
            got = [from_chip(x, shift) for shift in range(1, outer)]
            arrived.append(got)
            return got

        def spread(own, got):
            pieces = []
            for x in [own] + got:
                pieces += [x, from_sibling(x)]
            return pieces

        aggregated, received = [], []
        for first, size in zip(starts, sizes):
            aggregated.append(aggregate(features, adjacency, segments, first, size))
            received.append(send(aggregated[-1]))
        own_weights = gather_weight(weight, order, width)
        grads, carried = [], None
        for k, first in enumerate(starts):
            grad, carried = forward(
                order, spread(aggregated[k], received[k]), weight, bias, cotangent, carried, first
            )
            grads.append(grad)
        total, total_bias, out = carried
        grad_weight = lax.psum(total, "clu")
        grad_bias = sum_clusters(jnp.sum(total_bias, axis=0))
        grad_features = None
        received = [send(grad) for grad in grads]
        for k, first in enumerate(starts):
            grad_features = backward(
                spread(grads[k], received[k]), own_weights, adjacency, segments, grad_features, first
            )
        return (out, grad_features, grad_weight, grad_bias)

    return local


def solution(mesh):
    return jax.shard_map(
        build(mesh.shape["col"], mesh.shape["clu"]),
        mesh=mesh,
        in_specs=(
            P("clu", "col"),
            P(None, "col"),
            P("col"),
            P("clu", None),
            P("clu", None),
            P("clu", "col"),
        ),
        out_specs=(P("clu", "col"), P("clu", "col"), P(None, "col"), P("col")),
        check_vma=False,
    )
```

```python
import functools

import jax
import jax.numpy as jnp
from jax import lax
from jax.experimental import pallas as pl
from jax.experimental.pallas import tpu as pltpu
from jax.sharding import PartitionSpec as P

BLOCK = 128
F32 = jnp.float32
BF16 = jnp.bfloat16
MESH = pl.DeviceIdType.MESH
SMALL = pl.CostEstimate(flops=1000, bytes_accessed=1000, transcendentals=0)
ANY = pl.BlockSpec(memory_space=pl.ANY)


def params():
    return pltpu.CompilerParams(dimension_semantics=("arbitrary",), vmem_limit_bytes=56 << 20)


def whole(shape):
    return pl.BlockSpec(shape, lambda *_: (0,) * len(shape))


def stencil_of(adjacency, segment):
    columns = jnp.broadcast_to(segment, (BLOCK, BLOCK))
    links = jnp.where(columns == columns.T, adjacency, 0).astype(F32)
    inverse = 1.0 / (jnp.sum(links, axis=1, keepdims=True) + 1.0)
    row = lax.broadcasted_iota(jnp.int32, (BLOCK, BLOCK), 0)
    column = lax.broadcasted_iota(jnp.int32, (BLOCK, BLOCK), 1)
    return (links + jnp.where(row == column, 2.0, 0.0)).astype(BF16), inverse


class cluster_sum:
    PARTS = 4
    BACK = (5, 7, 8, 9)
    rounds = 10

    def __init__(self, total, result, half_in, quarter_in, bias_in, sems, clusters):
        self.result = result
        self.total, self.half_in, self.quarter_in, self.bias_in, self.sems = total, half_in, quarter_in, bias_in, sems
        self.clusters, self.high = clusters, clusters // 2
        self.depth = total.shape[0] - 8
        self.half = self.depth // self.PARTS // 2
        self.quarter = self.half // self.high
        self.me = lax.axis_index("clu")
        self.z, self.x = self.me // 2, lax.rem(self.me, 2)
        self.others = [lax.rem(self.me + d, clusters) for d in range(1, clusters)]
        self.levels = [lax.rem(self.z + d, self.high) for d in range(1, self.high)]

    def rows_of_half(self, c, x):
        return pl.ds(pl.multiple_of(c * 2 * self.half + x * self.half, self.half), self.half)

    def rows_of_quarter(self, c, q):
        start = c * 2 * self.half + self.x * self.half + q * self.quarter
        return pl.ds(pl.multiple_of(start, self.quarter), self.quarter)

    def copy(self, source, target, kind, send, recv, device):
        return pltpu.make_async_remote_copy(
            src_ref=source, dst_ref=target, send_sem=self.sems[2 * kind].at[send],
            recv_sem=self.sems[2 * kind + 1].at[recv], device_id={"clu": device}, device_id_type=MESH,
        )

    def give_half(self, c):
        rows = self.rows_of_half(c, 1 - self.x)
        return self.copy(self.total.at[rows], self.half_in.at[c], 0, c, c, self.z * 2 + 1 - self.x)

    def give_quarter(self, c, source, target):
        rows = self.rows_of_quarter(c, target)
        return self.copy(
            self.total.at[rows], self.quarter_in.at[c, source], 1, (c, target), (c, source), target * 2 + self.x
        )

    def return_quarter(self, c, source, target):
        rows = self.rows_of_quarter(c, source)
        return self.copy(
            self.result.at[rows], self.result.at[rows], 2, (c, target), (c, source), target * 2 + self.x
        )

    def return_half(self, c, x):
        rows = self.rows_of_half(c, x)
        return self.copy(self.result.at[rows], self.result.at[rows], 3, c, c, self.z * 2 + 1 - self.x)

    def give_bias(self, source, target):
        return self.copy(
            self.total.at[pl.ds(self.depth, 8)], self.bias_in.at[source], 4, target, source, target
        )

    def start(self):
        for c in range(self.PARTS):
            self.give_half(c).start()
        for other in self.others:
            self.give_bias(self.me, other).start()

    def advance(self, k):
        total = self.total
        if k < self.PARTS:
            self.give_half(k).wait_recv()
            total[self.rows_of_half(k, self.x), :] += self.half_in[k]
            for level in self.levels:
                self.give_quarter(k, self.z, level).start()
        c = k - 2
        if 0 <= c < self.PARTS:
            rows = self.rows_of_quarter(c, self.z)
            for level in self.levels:
                self.give_quarter(c, level, self.z).wait_recv()
            value = total[rows, :]
            for level in self.levels:
                value = value + self.quarter_in[c, level]
            self.result[rows, :] = value
            for level in self.levels:
                self.return_quarter(c, self.z, level).start()
        if k in self.BACK:
            c = self.BACK.index(k)
            for level in self.levels:
                self.return_quarter(c, level, self.z).wait_recv()
            self.return_half(c, self.x).start()

    def finish(self):
        for c in range(self.PARTS):
            self.give_half(c).wait_send()
            for level in self.levels:
                self.give_quarter(c, self.z, level).wait_send()
                self.return_quarter(c, self.z, level).wait_send()
            self.return_half(c, self.x).wait_send()
            self.return_half(c, 1 - self.x).wait_recv()
        for other in self.others:
            self.give_bias(self.me, other).wait_send()
            self.give_bias(other, self.me).wait_recv()
        value = self.total[pl.ds(self.depth, 8), :]
        for other in self.others:
            value = value + self.bias_in[other]
        self.result[pl.ds(self.depth, 8), :] = value


def exchange_kernel(
    n, clusters, groups, tile, features, adjacency, cotangent, segments, weight, bias,
    out, total_out, blocks_out, *rest,
):
    grads, rest = rest[: len(groups)], rest[len(groups) :]
    landing = (None,) + rest[: n - 1]
    (pieces, feat, adj, cot, act, grad, seg, mat, vec, total, shares, load_sem, cot_sem, out_sem, grad_sem,
     fixed_sem, send_sem, recv_sem, early_send, early_recv, share_send, share_recv, spread_send, spread_recv,
     block_send, block_recv, summed_total, half_in, quarter_in, bias_in, sum_sems) = rest[n - 1 :]
    outer = n // 2
    early = groups[0]
    ends = [sum(groups[: i + 1]) for i in range(len(groups))]
    rows, width = features.shape
    depth = mat.shape[0]
    count = rows // tile
    me, cluster = lax.axis_index("col"), lax.axis_index("clu")
    chip, core = me // 2, lax.rem(me, 2)
    sibling = chip * 2 + 1 - core
    part = 2 * width // clusters

    def chip_at(shift):
        return lax.rem(chip + shift + outer, outer) * 2 + core

    def at(k):
        return pl.ds(pl.multiple_of(k * tile, tile), tile)

    def loads(k):
        slot = lax.rem(k, 2)
        return (
            pltpu.make_async_copy(features.at[at(k)], feat.at[slot], load_sem.at[0, slot]),
            pltpu.make_async_copy(adjacency.at[at(k)], adj.at[slot], load_sem.at[1, slot]),
        )

    def load_cot(k):
        slot = lax.rem(k, 2)
        return pltpu.make_async_copy(cotangent.at[at(k)], cot.at[slot], cot_sem.at[slot])

    def store_out(k):
        slot = lax.rem(k, 2)
        return pltpu.make_async_copy(act.at[slot], out.at[at(k)], out_sem.at[slot])

    def store_grad(k, act_on):
        slot = lax.rem(k, 2)
        for start, end, target in zip([0] + ends, ends, grads):

            @pl.when((k >= start) & (k < end))
            def _():
                act_on(pltpu.make_async_copy(grad.at[slot], target.at[at(k - start)], grad_sem.at[slot]))

    def remote(source, target, send, recv, device, axis="col"):
        return pltpu.make_async_remote_copy(
            src_ref=source, dst_ref=target, send_sem=send, recv_sem=recv,
            device_id={axis: device}, device_id_type=MESH,
        )

    def hop(p, k):
        source = 0 if p % 2 == 0 else p - 1
        device = chip_at(-(p // 2)) if p % 2 == 0 else sibling
        return remote(pieces.at[source, at(k)], pieces.at[p, at(k)], send_sem.at[p, k], recv_sem.at[p, k], device)

    def early_hop(p, k):
        source = grads[0] if p < 2 or p % 2 == 0 else landing[p - 1]
        device = chip_at(-(p // 2)) if p % 2 == 0 else sibling
        return remote(source.at[at(k)], landing[p].at[at(k)], early_send.at[p, k], early_recv.at[p, k], device)

    def share(shift):
        owner = lax.rem(chip - shift + outer, outer)
        rows = pl.ds(pl.multiple_of(owner * 2 * width + cluster * part, part), part)
        mine = pl.ds(pl.multiple_of(cluster * part, part), part)
        return remote(
            weight.at[rows], shares.at[shift, mine], share_send.at[shift], share_recv.at[shift], chip_at(-shift)
        )

    def spread(shift, source, peer):
        rows = pl.ds(pl.multiple_of(source * part, part), part)
        return remote(
            shares.at[shift, rows], shares.at[shift, rows],
            spread_send.at[shift, peer], spread_recv.at[shift, source], peer, "clu",
        )

    def block(p):
        half = core if p % 2 == 0 else 1 - core
        if p < 2:
            source = weight.at[pl.ds(pl.multiple_of((chip * 2 + half) * width, width), width)]
        else:
            source = shares.at[p // 2, pl.ds(pl.multiple_of(half * width, width), width)]
        if p % 2 == 0:
            return pltpu.make_async_copy(source, blocks_out.at[p], block_recv.at[p])
        return remote(source, blocks_out.at[p], block_send.at[p], block_recv.at[p], sibling)

    others = [lax.rem(cluster + d, clusters) for d in range(1, clusters)]
    for copy in loads(0):
        copy.start()
    fixed = [
        pltpu.make_async_copy(source, target, fixed_sem.at[i])
        for i, (source, target) in enumerate([(segments, seg), (weight, mat), (bias, vec)])
    ]
    for copy in fixed:
        copy.start()
    load_cot(0).start()

    barrier = pltpu.get_barrier_semaphore()
    peers = [("col", sibling)] + [("col", chip_at(shift)) for shift in range(1, outer)]
    peers += [("clu", peer) for peer in others]
    for axis, peer in peers:
        pl.semaphore_signal(barrier, inc=1, device_id={axis: peer}, device_id_type=MESH)
    pl.semaphore_wait(barrier, len(peers))
    for shift in range(1, outer):
        share(shift).start()
    block(0).start()
    block(1).start()
    fixed[0].wait()

    def aggregate_tile(k, carry):
        slot = lax.rem(k, 2)
        for copy in loads(k):
            copy.wait()

        @pl.when(k + 1 < count)
        def _():
            for copy in loads(k + 1):
                copy.start()

        for b in range(tile // BLOCK):
            part = pl.ds(b * BLOCK, BLOCK)
            stencil, inverse = stencil_of(adj[slot, part, :], seg[pl.ds(k * (tile // BLOCK) + b, 1), :])
            summed = jnp.dot(stencil, feat[slot, part, :], preferred_element_type=F32)
            target = pl.ds(pl.multiple_of(k * tile + b * BLOCK, BLOCK), BLOCK)
            pieces[0, target, :] = (summed * inverse).astype(BF16)
        for shift in range(1, outer):
            hop(2 * shift, k).start()
        hop(1, k).start()
        return carry

    lax.fori_loop(0, count, aggregate_tile, 0)
    total[...] = jnp.zeros_like(total)
    fixed[1].wait()
    fixed[2].wait()
    blocks = [lax.rem(chip + p // 2, outer) * 2 + (core if p % 2 == 0 else 1 - core) for p in range(n)]

    def forward_tile(k):
        slot = lax.rem(k, 2)
        load_cot(k).wait()

        @pl.when(k + 1 < count)
        def _():
            load_cot(k + 1).start()

        hop(1, k).wait_recv()
        for shift in range(1, outer):
            hop(2 * shift + 1, k).wait_recv()

        @pl.when(k >= 2)
        def _():
            store_out(k - 2).wait()
            store_grad(k - 2, lambda copy: copy.wait())

            @pl.when(k - 2 < early)
            def _():
                for shift in range(1, outer):
                    early_hop(2 * shift, k - 2).start()
                early_hop(1, k - 2).start()

        preact = None
        for p in range(n):
            source = pl.ds(pl.multiple_of(blocks[p] * width, width), width)
            term = jnp.dot(pieces[p, at(k), :], mat[source, :], preferred_element_type=F32)
            preact = term if preact is None else preact + term
        preact = preact + vec[...].astype(F32)
        act[slot] = jnp.maximum(preact, 0.0).astype(BF16)
        grad_preact = jnp.where(preact > 0.0, cot[slot].astype(F32), 0.0)
        total[pl.ds(depth, 8), :] += jnp.sum(grad_preact.reshape(tile // 8, 8, width), axis=0)
        grad_preact = grad_preact.astype(BF16)
        grad[slot] = grad_preact
        store_out(k).start()
        store_grad(k, lambda copy: copy.start())
        for p in range(n):
            target = pl.ds(pl.multiple_of(blocks[p] * width, width), width)
            total[target, :] += lax.dot_general(
                pieces[p, at(k), :], grad_preact, (((0,), (0,)), ((), ())), preferred_element_type=F32
            )

    def step(k, carry):
        @pl.when(k < count)
        def _():
            for shift in range(1, outer):
                hop(2 * shift, k).wait_recv()
                hop(2 * shift + 1, k).start()

        @pl.when(k == 1)
        def _():
            for shift in range(1, outer):
                share(shift).wait_recv()
                for peer in others:
                    spread(shift, cluster, peer).start()

        @pl.when(k == 4)
        def _():
            for shift in range(1, outer):
                for peer in others:
                    spread(shift, peer, cluster).wait_recv()
                block(2 * shift).start()
                block(2 * shift + 1).start()

        @pl.when(k >= 1)
        def _():
            forward_tile(k - 1)

        return carry

    lax.fori_loop(0, count + 1, step, 0)
    sums = cluster_sum(total, summed_total, half_in, quarter_in, bias_in, sum_sems, clusters)
    sums.start()
    for k in (count - 2, count - 1):
        store_out(k).wait()
        store_grad(k, lambda copy: copy.wait())

    def finish_early(k, carry):
        for p in range(1, n):
            if p == 1 or p % 2:
                early_hop(p, k).wait_recv()
            early_hop(p, k).wait_send()
        return carry

    def finish(k, carry):
        for p in range(1, n):
            hop(p, k).wait_send()
        return carry

    lax.fori_loop(0, count, finish, 0)
    for p in range(n):
        if p % 2:
            block(p).wait_send()
            block(p).wait_recv()
        else:
            block(p).wait()
    for shift in range(1, outer):
        share(shift).wait_send()
        for peer in others:
            spread(shift, cluster, peer).wait_send()
    for k in range(max(early, sums.rounds)):
        if k < early:
            for shift in range(1, outer):
                early_hop(2 * shift, k).wait_recv()
                early_hop(2 * shift + 1, k).start()
        sums.advance(k)
    sums.finish()
    result = pltpu.make_async_copy(summed_total, total_out, fixed_sem.at[3])
    result.start()
    lax.fori_loop(0, early, finish_early, 0)
    result.wait()


def exchange(features, adjacency, cotangent, segments, weight, bias, n, clusters, groups, tile):
    rows, width = features.shape
    depth = weight.shape[0]
    count, outer = rows // tile, n // 2
    early = groups[0]
    parts, high = cluster_sum.PARTS, clusters // 2
    dma = pltpu.SemaphoreType.DMA
    array = jax.ShapeDtypeStruct
    return pl.pallas_call(
        functools.partial(exchange_kernel, n, clusters, groups, tile),
        in_specs=[ANY] * 6,
        out_specs=[ANY] * (2 + n + len(groups)),
        out_shape=[array((rows, width), BF16), array((depth + 8, width), F32), array((n, width, width), BF16)]
        + [array((group * tile, width), BF16) for group in groups]
        + [array((early * tile, width), BF16)] * (n - 1),
        scratch_shapes=[
            pltpu.VMEM((n, rows, width), BF16),
            pltpu.VMEM((2, tile, width), BF16),
            pltpu.VMEM((2, tile, BLOCK), jnp.int32),
            pltpu.VMEM((2, tile, width), BF16),
            pltpu.VMEM((2, tile, width), BF16),
            pltpu.VMEM((2, tile, width), BF16),
            pltpu.VMEM(segments.shape, jnp.int32),
            pltpu.VMEM((depth, width), BF16),
            pltpu.VMEM((1, width), BF16),
            pltpu.VMEM((depth + 8, width), F32),
            pltpu.VMEM((outer, 2 * width, width), BF16),
            dma((2, 2)),
            dma((2,)),
            dma((2,)),
            dma((2,)),
            dma((4,)),
            dma((n, count)),
            dma((n, count)),
            dma((n, early)),
            dma((n, early)),
            dma((outer,)),
            dma((outer,)),
            dma((outer, clusters)),
            dma((outer, clusters)),
            dma((n,)),
            dma((n,)),
            pltpu.VMEM((depth + 8, width), F32),
            pltpu.VMEM((parts, depth // parts // 2, width), F32),
            pltpu.VMEM((parts, high, depth // parts // 2 // high, width), F32),
            pltpu.VMEM((clusters, 8, width), F32),
            [
                dma((parts,)), dma((parts,)), dma((parts, high)), dma((parts, high)), dma((parts, high)),
                dma((parts, high)), dma((parts,)), dma((parts,)), dma((clusters,)), dma((clusters,)),
            ],
        ],
        compiler_params=pltpu.CompilerParams(
            collective_id=0, has_side_effects=True, vmem_limit_bytes=62 << 20
        ),
    )(features, adjacency, cotangent, segments, weight, bias)


def backward_kernel(n, first, tile, *refs):
    grads, (weights, adjacency, segments), out = refs[:n], refs[n : n + 3], refs[-2]
    refs[-1][...] = jnp.zeros_like(refs[-1])
    step = pl.program_id(0)
    grad = None
    for p in range(n):
        term = lax.dot_general(
            grads[p][...], weights[p], (((1,), (1,)), ((), ())), preferred_element_type=F32
        )
        grad = term if grad is None else grad + term
    grad = grad.astype(BF16)
    for b in range(tile // BLOCK):
        rows = pl.ds(b * BLOCK, BLOCK)
        index = first // BLOCK + step * (tile // BLOCK) + b
        stencil, inverse = stencil_of(adjacency[rows, :], segments[pl.ds(index, 1), :])
        summed = (grad[b * BLOCK : (b + 1) * BLOCK].astype(F32) * inverse).astype(BF16)
        out[rows, :] = jnp.dot(stencil, summed, preferred_element_type=F32)


def backward(grads, weights, adjacency, segments, carried, first, size, *earlier):
    n, width = len(grads), weights.shape[1]
    rows = adjacency.shape[0]
    tile = min(size, 512)
    offset = first // tile

    def rows_from(base):
        return pl.BlockSpec((tile, width), lambda i: (base // tile + i, 0))

    in_specs = (
        [rows_from(base) for _, base in grads]
        + [whole(weights.shape)]
        + [pl.BlockSpec((tile, BLOCK), lambda i: (offset + i, 0)), whole(segments.shape)]
    )
    operands = [x for x, _ in grads] + [weights, adjacency, segments]
    aliases = {}
    if carried is not None:
        in_specs.append(ANY)
        aliases = {len(operands): 0}
        operands.append(carried)
    in_specs += [ANY] * len(earlier)
    operands += earlier
    return pl.pallas_call(
        functools.partial(backward_kernel, n, first, tile),
        grid=(size // tile,),
        in_specs=in_specs,
        out_specs=[pl.BlockSpec((tile, width), lambda i: (offset + i, 0)), whole((8, BLOCK))],
        out_shape=[jax.ShapeDtypeStruct((rows, width), F32), jax.ShapeDtypeStruct((8, BLOCK), F32)],
        input_output_aliases=aliases,
        cost_estimate=SMALL,
        compiler_params=params(),
    )(*operands)


def copy_kernel(source, earlier, target):
    target[...] = source[...]


def copied(x, earlier):
    rows, width = x.shape
    spec = pl.BlockSpec((1024, width), lambda i: (i, 0))
    return pl.pallas_call(
        copy_kernel,
        grid=(rows // 1024,),
        in_specs=[spec, ANY],
        out_specs=spec,
        out_shape=jax.ShapeDtypeStruct(x.shape, x.dtype),
        cost_estimate=SMALL,
        compiler_params=params(),
    )(x, earlier)


def tie_kernel(*refs):
    pass


def tie(x, *earlier):
    return pl.pallas_call(
        tie_kernel,
        in_specs=[ANY] * (1 + len(earlier)),
        out_specs=ANY,
        out_shape=jax.ShapeDtypeStruct(x.shape, x.dtype),
        input_output_aliases={0: 0},
        cost_estimate=SMALL,
    )(x, *earlier)


def split_kernel(total, earlier, grad_weight, grad_bias):
    depth, width = grad_weight.shape
    grad_weight[...] = total[pl.ds(0, depth), :]
    grad_bias[...] = jnp.broadcast_to(jnp.sum(total[pl.ds(depth, 8), :], axis=0, keepdims=True), (8, width))


def split(total, earlier):
    rows, width = total.shape
    return pl.pallas_call(
        split_kernel,
        grid=(1,),
        in_specs=[whole(total.shape), ANY],
        out_specs=[whole((rows - 8, width)), whole((8, width))],
        out_shape=[jax.ShapeDtypeStruct((rows - 8, width), F32), jax.ShapeDtypeStruct((8, width), F32)],
        cost_estimate=SMALL,
        compiler_params=params(),
    )(total, earlier)


def tile_groups(count):
    return [count - 5, 3, 1, 1]


def build(n, clusters):
    outer = n // 2

    def device(chip, core):
        return (chip % outer) * 2 + core

    def from_chip(x, shift):
        pairs = [(device(chip + shift, core), device(chip, core)) for chip in range(outer) for core in range(2)]
        return lax.ppermute(x, "col", pairs)

    def from_sibling(x):
        return lax.ppermute(x, "col", [(i, i ^ 1) for i in range(n)])

    def local(features, weight, bias, adjacency, segments, cotangent):
        rows, width = features.shape
        tile = 512
        groups = tile_groups(rows // tile)
        out, total, blocks, *rest = exchange(
            features, adjacency, cotangent, segments, weight, bias.reshape(1, width), n, clusters, groups, tile
        )
        grads, landing = rest[: len(groups)], rest[len(groups) :]
        own = grads[1:-1] + [grads[-1][: tile // 2], grads[-1][tile // 2 :]]
        near, far = [], []
        for k, x in enumerate(own):
            if k:
                x = own[k] = tie(x, near[-1])
            near.append(from_sibling(x))
            far.append([from_chip(x, shift) for shift in range(1, outer)])
        out = copied(out, near[-1])
        grad_weight, grad_bias = split(total, out)
        first = groups[0] * tile
        grad_features, token = backward(
            [(x, 0) for x in [grads[0]] + landing], blocks, adjacency, segments, None, 0, first, grad_bias
        )
        for k, x in enumerate(own):
            parts = [(x, 0), (near[k], 0)]
            for y in far[k]:
                y = tie(y, token)
                parts += [(y, 0), (from_sibling(y), 0)]
            size = x.shape[0]
            grad_features, token = backward(parts, blocks, adjacency, segments, grad_features, first, size)
            first += size
        return (out, grad_features, grad_weight, grad_bias[0])

    return local


def solution(mesh):
    return jax.shard_map(
        build(mesh.shape["col"], mesh.shape["clu"]),
        mesh=mesh,
        in_specs=(
            P("clu", "col"),
            P(None, "col"),
            P("col"),
            P("clu", None),
            P("clu", None),
            P("clu", "col"),
        ),
        out_specs=(P("clu", "col"), P("clu", "col"), P(None, "col"), P("col")),
        check_vma=False,
    )
```

```python
import functools

import jax
import jax.numpy as jnp
from jax import lax
from jax.experimental import pallas as pl
from jax.experimental.pallas import tpu as pltpu
from jax.sharding import PartitionSpec as P

BLOCK = 128
F32 = jnp.float32
BF16 = jnp.bfloat16
MESH = pl.DeviceIdType.MESH
SMALL = pl.CostEstimate(flops=1000, bytes_accessed=1000, transcendentals=0)
ANY = pl.BlockSpec(memory_space=pl.ANY)


def params():
    return pltpu.CompilerParams(dimension_semantics=("arbitrary",), vmem_limit_bytes=56 << 20)


def whole(shape):
    return pl.BlockSpec(shape, lambda *_: (0,) * len(shape))


def stencil_of(adjacency, segment):
    columns = jnp.broadcast_to(segment, (BLOCK, BLOCK))
    links = jnp.where(columns == columns.T, adjacency, 0).astype(F32)
    inverse = 1.0 / (jnp.sum(links, axis=1, keepdims=True) + 1.0)
    row = lax.broadcasted_iota(jnp.int32, (BLOCK, BLOCK), 0)
    column = lax.broadcasted_iota(jnp.int32, (BLOCK, BLOCK), 1)
    return (links + jnp.where(row == column, 2.0, 0.0)).astype(BF16), inverse


class cluster_sum:
    PARTS = 4
    BACK = (5, 7, 8, 9)
    rounds = 10
    last = 12

    def __init__(self, total, result, half_in, quarter_in, bias_in, sems, clusters):
        self.result = result
        self.total, self.half_in, self.quarter_in, self.bias_in, self.sems = total, half_in, quarter_in, bias_in, sems
        self.clusters, self.high = clusters, clusters // 2
        self.depth = total.shape[0] - 8
        self.half = self.depth // self.PARTS // 2
        self.quarter = self.half // self.high
        self.me = lax.axis_index("clu")
        self.z, self.x = self.me // 2, lax.rem(self.me, 2)
        self.others = [lax.rem(self.me + d, clusters) for d in range(1, clusters)]
        self.levels = [lax.rem(self.z + d, self.high) for d in range(1, self.high)]

    def rows_of_half(self, c, x):
        return pl.ds(pl.multiple_of(c * 2 * self.half + x * self.half, self.half), self.half)

    def rows_of_quarter(self, c, q):
        start = c * 2 * self.half + self.x * self.half + q * self.quarter
        return pl.ds(pl.multiple_of(start, self.quarter), self.quarter)

    def copy(self, source, target, kind, send, recv, device):
        return pltpu.make_async_remote_copy(
            src_ref=source, dst_ref=target, send_sem=self.sems[2 * kind].at[send],
            recv_sem=self.sems[2 * kind + 1].at[recv], device_id={"clu": device}, device_id_type=MESH,
        )

    def give_half(self, c):
        rows = self.rows_of_half(c, 1 - self.x)
        return self.copy(self.total.at[rows], self.half_in.at[c], 0, c, c, self.z * 2 + 1 - self.x)

    def give_quarter(self, c, source, target):
        rows = self.rows_of_quarter(c, target)
        return self.copy(
            self.total.at[rows], self.quarter_in.at[c, source], 1, (c, target), (c, source), target * 2 + self.x
        )

    def return_quarter(self, c, source, target):
        rows = self.rows_of_quarter(c, source)
        return self.copy(
            self.result.at[rows], self.result.at[rows], 2, (c, target), (c, source), target * 2 + self.x
        )

    def return_half(self, c, x):
        rows = self.rows_of_half(c, x)
        return self.copy(self.result.at[rows], self.result.at[rows], 3, c, c, self.z * 2 + 1 - self.x)

    def give_bias(self, source, target):
        return self.copy(
            self.total.at[pl.ds(self.depth, 8)], self.bias_in.at[source], 4, target, source, target
        )

    def start(self):
        for c in range(self.PARTS):
            self.give_half(c).start()
        for other in self.others:
            self.give_bias(self.me, other).start()

    def advance(self, k):
        total = self.total
        if k < self.PARTS:
            self.give_half(k).wait_recv()
            total[self.rows_of_half(k, self.x), :] += self.half_in[k]
            for level in self.levels:
                self.give_quarter(k, self.z, level).start()
        c = k - 2
        if 0 <= c < self.PARTS:
            rows = self.rows_of_quarter(c, self.z)
            for level in self.levels:
                self.give_quarter(c, level, self.z).wait_recv()
            value = total[rows, :]
            for level in self.levels:
                value = value + self.quarter_in[c, level]
            self.result[rows, :] = value
            for level in self.levels:
                self.return_quarter(c, self.z, level).start()
        if k in self.BACK:
            c = self.BACK.index(k)
            for level in self.levels:
                self.return_quarter(c, level, self.z).wait_recv()
            self.return_half(c, self.x).start()

    def finish(self):
        for c in range(self.PARTS):
            self.give_half(c).wait_send()
            for level in self.levels:
                self.give_quarter(c, self.z, level).wait_send()
                self.return_quarter(c, self.z, level).wait_send()
            self.return_half(c, self.x).wait_send()
            self.return_half(c, 1 - self.x).wait_recv()
        for other in self.others:
            self.give_bias(self.me, other).wait_send()
            self.give_bias(other, self.me).wait_recv()
        value = self.total[pl.ds(self.depth, 8), :]
        for other in self.others:
            value = value + self.bias_in[other]
        self.result[pl.ds(self.depth, 8), :] = value


def exchange_kernel(
    n, clusters, early, tile, features, adjacency, cotangent, segments, weight, bias,
    out, total_out, blocks_out, stencil_out, back_out, grads, late_grads, late_near, *rest,
):
    landing = (None,) + rest[: n - 1]
    (pieces, feat, adj, cot, act, grad, seg, sten, mat, vec, total, shares, back, load_sem, cot_sem, out_sem, grad_sem,
     fixed_sem, send_sem, recv_sem, early_send, early_recv, back_sem, share_send, share_recv, spread_send, spread_recv,
     block_send, block_recv, summed_total, half_in, quarter_in, bias_in, sum_sems) = rest[n - 1 :]
    outer = n // 2
    rows, width = features.shape
    depth = mat.shape[0]
    count = rows // tile
    me, cluster = lax.axis_index("col"), lax.axis_index("clu")
    chip, core = me // 2, lax.rem(me, 2)
    sibling = chip * 2 + 1 - core
    part = 2 * width // clusters

    def chip_at(shift):
        return lax.rem(chip + shift + outer, outer) * 2 + core

    def at(k):
        return pl.ds(pl.multiple_of(k * tile, tile), tile)

    def loads(k):
        slot = lax.rem(k, 2)
        return (
            pltpu.make_async_copy(features.at[at(k)], feat.at[slot], load_sem.at[0, slot]),
            pltpu.make_async_copy(adjacency.at[at(k)], adj.at[slot], load_sem.at[1, slot]),
        )

    def load_cot(k):
        slot = lax.rem(k, 2)
        return pltpu.make_async_copy(cotangent.at[at(k)], cot.at[slot], cot_sem.at[slot])

    def store_out(k):
        slot = lax.rem(k, 2)
        return pltpu.make_async_copy(act.at[slot], out.at[at(k)], out_sem.at[slot])

    def store_grad(k, then):
        slot = lax.rem(k, 2)

        @pl.when(k < early)
        def _():
            then(pltpu.make_async_copy(grad.at[slot], grads.at[at(k)], grad_sem.at[slot]))

        if early < count:

            @pl.when(k >= early)
            def _():
                then(pltpu.make_async_copy(grad.at[slot], late_grads.at[at(k - early)], grad_sem.at[slot]))

    def remote(source, target, send, recv, device, axis="col"):
        return pltpu.make_async_remote_copy(
            src_ref=source, dst_ref=target, send_sem=send, recv_sem=recv,
            device_id={axis: device}, device_id_type=MESH,
        )

    def hop(p, k):
        source = 0 if p % 2 == 0 else p - 1
        device = chip_at(-(p // 2)) if p % 2 == 0 else sibling
        return remote(pieces.at[source, at(k)], pieces.at[p, at(k)], send_sem.at[p, k], recv_sem.at[p, k], device)

    def early_hop(p, k):
        source = grads if p < 2 or p % 2 == 0 else landing[p - 1]
        device = chip_at(-(p // 2)) if p % 2 == 0 else sibling
        return remote(source.at[at(k)], landing[p].at[at(k)], early_send.at[p, k], early_recv.at[p, k], device)

    def late_hop(k):
        return remote(
            late_grads.at[at(k - early)], late_near.at[at(k - early)], early_send.at[1, k], early_recv.at[1, k], sibling
        )

    def send_grad(k):
        @pl.when(k < early)
        def _():
            for shift in range(1, outer):
                early_hop(2 * shift, k).start()
            early_hop(1, k).start()

        if early < count:

            @pl.when(k >= early)
            def _():
                late_hop(k).start()

    def load_piece(p, k):
        slot = lax.rem(k, 2)
        source = landing[p] if p else grads
        return pltpu.make_async_copy(source.at[at(k)], back.at[slot, p], back_sem.at[slot, p])

    def store_back(k):
        slot = lax.rem(k, 2)
        return pltpu.make_async_copy(act.at[slot], back_out.at[at(k)], out_sem.at[slot])

    def share(shift):
        owner = lax.rem(chip - shift + outer, outer)
        rows = pl.ds(pl.multiple_of(owner * 2 * width + cluster * part, part), part)
        mine = pl.ds(pl.multiple_of(cluster * part, part), part)
        return remote(
            weight.at[rows], shares.at[shift, mine], share_send.at[shift], share_recv.at[shift], chip_at(-shift)
        )

    def spread(shift, source, peer):
        rows = pl.ds(pl.multiple_of(source * part, part), part)
        return remote(
            shares.at[shift, rows], shares.at[shift, rows],
            spread_send.at[shift, peer], spread_recv.at[shift, source], peer, "clu",
        )

    def block(p):
        half = core if p % 2 == 0 else 1 - core
        if p < 2:
            source = weight.at[pl.ds(pl.multiple_of((chip * 2 + half) * width, width), width)]
        else:
            source = shares.at[p // 2, pl.ds(pl.multiple_of(half * width, width), width)]
        if p % 2 == 0:
            return pltpu.make_async_copy(source, blocks_out.at[p], block_recv.at[p])
        return remote(source, blocks_out.at[p], block_send.at[p], block_recv.at[p], sibling)

    others = [lax.rem(cluster + d, clusters) for d in range(1, clusters)]
    for copy in loads(0):
        copy.start()
    fixed = [
        pltpu.make_async_copy(source, target, fixed_sem.at[i])
        for i, (source, target) in enumerate([(segments, seg), (weight, mat), (bias, vec)])
    ]
    for copy in fixed:
        copy.start()
    load_cot(0).start()

    barrier = pltpu.get_barrier_semaphore()
    peers = [("col", sibling)] + [("col", chip_at(shift)) for shift in range(1, outer)]
    peers += [("clu", peer) for peer in others]
    for axis, peer in peers:
        pl.semaphore_signal(barrier, inc=1, device_id={axis: peer}, device_id_type=MESH)
    pl.semaphore_wait(barrier, len(peers))
    for shift in range(1, outer):
        share(shift).start()
    block(0).start()
    block(1).start()
    fixed[0].wait()

    def aggregate_tile(k, carry):
        slot = lax.rem(k, 2)
        for copy in loads(k):
            copy.wait()

        @pl.when(k + 1 < count)
        def _():
            for copy in loads(k + 1):
                copy.start()

        for b in range(tile // BLOCK):
            part = pl.ds(b * BLOCK, BLOCK)
            stencil, inverse = stencil_of(adj[slot, part, :], seg[pl.ds(k * (tile // BLOCK) + b, 1), :])
            summed = jnp.dot(stencil, feat[slot, part, :], preferred_element_type=F32)
            target = pl.ds(pl.multiple_of(k * tile + b * BLOCK, BLOCK), BLOCK)
            sten[target, :] = stencil
            pieces[0, target, :] = (summed * inverse).astype(BF16)
        for shift in range(1, outer):
            hop(2 * shift, k).start()
        hop(1, k).start()
        return carry

    lax.fori_loop(0, count, aggregate_tile, 0)
    stencil_copy = pltpu.make_async_copy(sten, stencil_out, fixed_sem.at[4])
    stencil_copy.start()
    total[...] = jnp.zeros_like(total)
    fixed[1].wait()
    fixed[2].wait()
    blocks = [lax.rem(chip + p // 2, outer) * 2 + (core if p % 2 == 0 else 1 - core) for p in range(n)]

    def forward_tile(k):
        slot = lax.rem(k, 2)
        load_cot(k).wait()

        @pl.when(k + 1 < count)
        def _():
            load_cot(k + 1).start()

        hop(1, k).wait_recv()
        for shift in range(1, outer):
            hop(2 * shift + 1, k).wait_recv()

        @pl.when(k >= 2)
        def _():
            store_out(k - 2).wait()
            store_grad(k - 2, lambda copy: copy.wait())
            send_grad(k - 2)

        preact = None
        for p in range(n):
            source = pl.ds(pl.multiple_of(blocks[p] * width, width), width)
            term = jnp.dot(pieces[p, at(k), :], mat[source, :], preferred_element_type=F32)
            preact = term if preact is None else preact + term
        preact = preact + vec[...].astype(F32)
        act[slot] = jnp.maximum(preact, 0.0).astype(BF16)
        grad_preact = jnp.where(preact > 0.0, cot[slot].astype(F32), 0.0)
        total[pl.ds(depth, 8), :] += jnp.sum(grad_preact.reshape(tile // 8, 8, width), axis=0)
        grad_preact = grad_preact.astype(BF16)
        grad[slot] = grad_preact
        store_out(k).start()
        store_grad(k, lambda copy: copy.start())
        for p in range(n):
            target = pl.ds(pl.multiple_of(blocks[p] * width, width), width)
            total[target, :] += lax.dot_general(
                pieces[p, at(k), :], grad_preact, (((0,), (0,)), ((), ())), preferred_element_type=F32
            )

    def step(k, carry):
        @pl.when(k < count)
        def _():
            for shift in range(1, outer):
                hop(2 * shift, k).wait_recv()
                hop(2 * shift + 1, k).start()

        @pl.when(k == 1)
        def _():
            for shift in range(1, outer):
                share(shift).wait_recv()
                for peer in others:
                    spread(shift, cluster, peer).start()

        @pl.when(k == 4)
        def _():
            for shift in range(1, outer):
                for peer in others:
                    spread(shift, peer, cluster).wait_recv()
                block(2 * shift).start()
                block(2 * shift + 1).start()

        @pl.when(k >= 1)
        def _():
            forward_tile(k - 1)

        return carry

    lax.fori_loop(0, count + 1, step, 0)
    sums = cluster_sum(total, summed_total, half_in, quarter_in, bias_in, sum_sems, clusters)
    sums.start()
    for k in (count - 2, count - 1):
        store_out(k).wait()
        store_grad(k, lambda copy: copy.wait())
        send_grad(k)
    for p in range(n):
        if p % 2:
            block(p).wait_recv()
        else:
            block(p).wait()
    copies = [
        pltpu.make_async_copy(blocks_out.at[p], mat.at[pl.ds(p * width, width)], block_send.at[p - p % 2])
        for p in range(0, n, 2)
    ] + [
        pltpu.make_async_copy(blocks_out.at[p], mat.at[pl.ds(p * width, width)], block_recv.at[p])
        for p in range(1, n, 2)
    ]
    for copy in copies:
        copy.start()
    for copy in copies:
        copy.wait()

    def backward_tile(k):
        slot = lax.rem(k, 2)
        for p in range(n):
            load_piece(p, k).wait()

        @pl.when(k >= 2)
        def _():
            store_back(k - 2).wait()

        value = None
        for p in range(n):
            term = lax.dot_general(
                back[slot, p], mat[pl.ds(p * width, width), :], (((1,), (1,)), ((), ())), preferred_element_type=F32
            )
            value = term if value is None else value + term
        inverse = 1.0 / (jnp.sum(sten[at(k), :].astype(F32), axis=1, keepdims=True) - 1.0)
        act[slot] = (value.astype(BF16).astype(F32) * inverse).astype(BF16)
        store_back(k).start()

    result = pltpu.make_async_copy(summed_total, total_out, fixed_sem.at[3])

    def finish_sums():
        sums.finish()
        result.start()

    def moment(r):
        return max(r * 512 // tile, 0)

    def back_step(k, carry):
        @pl.when(k >= 1)
        def _():
            backward_tile(k - 1)

        @pl.when(k < early)
        def _():
            for shift in range(1, outer):
                early_hop(2 * shift, k).wait_recv()
                early_hop(2 * shift + 1, k).start()
            early_hop(1, k).wait_recv()
            for shift in range(1, outer):
                early_hop(2 * shift + 1, k).wait_recv()
            for p in range(n):
                load_piece(p, k).start()

        for r in range(sums.rounds):
            if moment(r) <= early:
                pl.when(k == moment(r))(functools.partial(sums.advance, r))
        if moment(sums.last) <= early:
            pl.when(k == moment(sums.last))(finish_sums)
        return carry

    lax.fori_loop(0, early + 1, back_step, 0)
    for r in range(sums.rounds):
        if moment(r) > early:
            sums.advance(r)
    if moment(sums.last) > early:
        finish_sums()
    for k in (early - 2, early - 1):
        store_back(k).wait()

    def finish(k, carry):
        for p in range(1, n):
            hop(p, k).wait_send()

        @pl.when(k < early)
        def _():
            for p in range(1, n):
                early_hop(p, k).wait_send()

        if early < count:

            @pl.when(k >= early)
            def _():
                late_hop(k).wait()

        return carry

    lax.fori_loop(0, count, finish, 0)
    for p in range(1, n, 2):
        block(p).wait_send()
    for shift in range(1, outer):
        share(shift).wait_send()
        for peer in others:
            spread(shift, cluster, peer).wait_send()
    stencil_copy.wait()
    result.wait()


def exchange(features, adjacency, cotangent, segments, weight, bias, n, clusters, early, tile):
    rows, width = features.shape
    depth = weight.shape[0]
    count, outer = rows // tile, n // 2
    late = max(count - early, 1)
    parts, high = cluster_sum.PARTS, clusters // 2
    dma = pltpu.SemaphoreType.DMA
    array = jax.ShapeDtypeStruct
    return pl.pallas_call(
        functools.partial(exchange_kernel, n, clusters, early, tile),
        in_specs=[ANY] * 6,
        out_specs=[ANY] * (7 + n),
        out_shape=[
            array((rows, width), BF16),
            array((depth + 8, width), F32),
            array((n, width, width), BF16),
            array((rows, BLOCK), BF16),
            array((early * tile, width), BF16),
            array((early * tile, width), BF16),
            array((late * tile, width), BF16),
            array((late * tile, width), BF16),
        ]
        + [array((early * tile, width), BF16)] * (n - 1),
        scratch_shapes=[
            pltpu.VMEM((n, rows, width), BF16),
            pltpu.VMEM((2, tile, width), BF16),
            pltpu.VMEM((2, tile, BLOCK), jnp.int32),
            pltpu.VMEM((2, tile, width), BF16),
            pltpu.VMEM((2, tile, width), BF16),
            pltpu.VMEM((2, tile, width), BF16),
            pltpu.VMEM(segments.shape, jnp.int32),
            pltpu.VMEM((rows, BLOCK), BF16),
            pltpu.VMEM((depth, width), BF16),
            pltpu.VMEM((1, width), BF16),
            pltpu.VMEM((depth + 8, width), F32),
            pltpu.VMEM((outer, 2 * width, width), BF16),
            pltpu.VMEM((2, n, tile, width), BF16),
            dma((2, 2)),
            dma((2,)),
            dma((2,)),
            dma((2,)),
            dma((5,)),
            dma((n, count)),
            dma((n, count)),
            dma((n, count)),
            dma((n, count)),
            dma((2, n)),
            dma((outer,)),
            dma((outer,)),
            dma((outer, clusters)),
            dma((outer, clusters)),
            dma((n,)),
            dma((n,)),
            pltpu.VMEM((depth + 8, width), F32),
            pltpu.VMEM((parts, depth // parts // 2, width), F32),
            pltpu.VMEM((parts, high, depth // parts // 2 // high, width), F32),
            pltpu.VMEM((clusters, 8, width), F32),
            [
                dma((parts,)), dma((parts,)), dma((parts, high)), dma((parts, high)), dma((parts, high)),
                dma((parts, high)), dma((parts,)), dma((parts,)), dma((clusters,)), dma((clusters,)),
            ],
        ],
        compiler_params=pltpu.CompilerParams(
            collective_id=0, has_side_effects=True, vmem_limit_bytes=63 << 20
        ),
    )(features, adjacency, cotangent, segments, weight, bias)


def finish_kernel(steps, stencil, back, out_in, total, bias, grad_features, out, grad_weight, grad_bias):
    @pl.when(pl.program_id(0) < steps)
    def _():
        for b in range(back.shape[0] // BLOCK):
            rows = pl.ds(b * BLOCK, BLOCK)
            grad_features[rows, :] = jnp.dot(stencil[rows, :], back[rows, :], preferred_element_type=F32)

    out[...] = out_in[...]
    grad_weight[...] = total[...]
    grad_bias[...] = jnp.broadcast_to(jnp.sum(bias[...], axis=0, keepdims=True), bias.shape)


def finish(stencil, back, out, total):
    rows, width = out.shape
    depth = total.shape[0] - 8
    tile = 1024
    steps, grid = back.shape[0] // tile, rows // tile
    part = depth // grid
    every = lambda size: pl.BlockSpec((size, width), lambda i: (i, 0))
    first = lambda size: pl.BlockSpec((tile, size), lambda i: (jnp.minimum(i, steps - 1), 0))
    fixed = lambda index: pl.BlockSpec((8, width), lambda i: (index, 0))
    return pl.pallas_call(
        functools.partial(finish_kernel, steps),
        grid=(grid,),
        in_specs=[first(BLOCK), first(width), every(tile), every(part), fixed(depth // 8)],
        out_specs=[first(width), every(tile), every(part), fixed(0)],
        out_shape=[
            jax.ShapeDtypeStruct((rows, width), F32),
            jax.ShapeDtypeStruct((rows, width), BF16),
            jax.ShapeDtypeStruct((depth, width), F32),
            jax.ShapeDtypeStruct((8, width), F32),
        ],
        cost_estimate=pl.CostEstimate(
            flops=2 * rows * BLOCK * width, bytes_accessed=10 * rows * width + 8 * depth * width, transcendentals=0
        ),
        compiler_params=params(),
    )(stencil, back, out, total, total)


def build(n, clusters):
    outer = n // 2

    def device(chip, core):
        return (chip % outer) * 2 + core

    def from_chip(x, shift):
        pairs = [(device(chip + shift, core), device(chip, core)) for chip in range(outer) for core in range(2)]
        return lax.ppermute(x, "col", pairs)

    def from_sibling(x):
        return lax.ppermute(x, "col", [(i, i ^ 1) for i in range(n)])

    def local(features, weight, bias, adjacency, segments, cotangent):
        rows, width = features.shape
        tile = 256 if n <= 4 else 512
        early = rows // tile
        out, total, blocks, stencil, back, *rest = exchange(
            features, adjacency, cotangent, segments, weight, bias.reshape(1, width), n, clusters, early, tile
        )
        grad_features, out, grad_weight, grad_bias = finish(stencil, back, out, total)
        return (out, grad_features, grad_weight, grad_bias[0])

    return local


def solution(mesh):
    return jax.shard_map(
        build(mesh.shape["col"], mesh.shape["clu"]),
        mesh=mesh,
        in_specs=(
            P("clu", "col"),
            P(None, "col"),
            P("col"),
            P("clu", None),
            P("clu", None),
            P("clu", "col"),
        ),
        out_specs=(P("clu", "col"), P("clu", "col"), P(None, "col"), P("col")),
        check_vma=False,
    )
```

```python
import functools

import jax
import jax.numpy as jnp
from jax import lax
from jax.experimental import pallas as pl
from jax.experimental.pallas import tpu as pltpu
from jax.sharding import PartitionSpec as P

BLOCK = 128
SLOTS = 4
F32 = jnp.float32
BF16 = jnp.bfloat16
MESH = pl.DeviceIdType.MESH
HBM = pl.BlockSpec(memory_space=pltpu.HBM)
VMEM = pl.BlockSpec(memory_space=pltpu.VMEM)


def stencil_of(adjacency, segment):
    columns = jnp.broadcast_to(segment, (BLOCK, BLOCK))
    links = jnp.where(columns == columns.T, adjacency, 0).astype(F32)
    inverse = 1.0 / (jnp.sum(links, axis=1, keepdims=True) + 1.0)
    row = lax.broadcasted_iota(jnp.int32, (BLOCK, BLOCK), 0)
    column = lax.broadcasted_iota(jnp.int32, (BLOCK, BLOCK), 1)
    return (links + jnp.where(row == column, 2.0, 0.0)).astype(BF16), inverse


class cluster_sum:
    PARTS = 4
    BACK = (5, 7, 8, 9)
    rounds = 10
    last = 12

    def __init__(self, total, result, half_in, quarter_in, bias_in, sems, clusters):
        self.result = result
        self.total, self.half_in, self.quarter_in, self.bias_in, self.sems = total, half_in, quarter_in, bias_in, sems
        self.clusters, self.high = clusters, clusters // 2
        self.depth = total.shape[0] - 8
        self.half = self.depth // self.PARTS // 2
        self.quarter = self.half // self.high
        self.me = lax.axis_index("clu")
        self.z, self.x = self.me // 2, lax.rem(self.me, 2)
        self.others = [lax.rem(self.me + d, clusters) for d in range(1, clusters)]
        self.levels = [lax.rem(self.z + d, self.high) for d in range(1, self.high)]

    def rows_of_half(self, c, x):
        return pl.ds(pl.multiple_of(c * 2 * self.half + x * self.half, self.half), self.half)

    def rows_of_quarter(self, c, q):
        start = c * 2 * self.half + self.x * self.half + q * self.quarter
        return pl.ds(pl.multiple_of(start, self.quarter), self.quarter)

    def copy(self, source, target, kind, send, recv, device):
        return pltpu.make_async_remote_copy(
            src_ref=source, dst_ref=target, send_sem=self.sems[2 * kind].at[send],
            recv_sem=self.sems[2 * kind + 1].at[recv], device_id={"clu": device}, device_id_type=MESH,
        )

    def give_half(self, c):
        rows = self.rows_of_half(c, 1 - self.x)
        return self.copy(self.total.at[rows], self.half_in.at[c], 0, c, c, self.z * 2 + 1 - self.x)

    def give_quarter(self, c, source, target):
        rows = self.rows_of_quarter(c, target)
        return self.copy(
            self.total.at[rows], self.quarter_in.at[c, source], 1, (c, target), (c, source), target * 2 + self.x
        )

    def return_quarter(self, c, source, target):
        rows = self.rows_of_quarter(c, source)
        return self.copy(
            self.result.at[rows], self.result.at[rows], 2, (c, target), (c, source), target * 2 + self.x
        )

    def return_half(self, c, x):
        rows = self.rows_of_half(c, x)
        return self.copy(self.result.at[rows], self.result.at[rows], 3, c, c, self.z * 2 + 1 - self.x)

    def give_bias(self, source, target):
        return self.copy(
            self.total.at[pl.ds(self.depth, 8)], self.bias_in.at[source], 4, target, source, target
        )

    def start(self):
        for c in range(self.PARTS):
            self.give_half(c).start()
        for other in self.others:
            self.give_bias(self.me, other).start()

    def advance(self, k):
        total = self.total
        if k < self.PARTS:
            self.give_half(k).wait_recv()
            total[self.rows_of_half(k, self.x), :] += self.half_in[k]
            for level in self.levels:
                self.give_quarter(k, self.z, level).start()
        c = k - 2
        if 0 <= c < self.PARTS:
            rows = self.rows_of_quarter(c, self.z)
            for level in self.levels:
                self.give_quarter(c, level, self.z).wait_recv()
            value = total[rows, :]
            for level in self.levels:
                value = value + self.quarter_in[c, level]
            self.result[rows, :] = value
            for level in self.levels:
                self.return_quarter(c, self.z, level).start()
        if k in self.BACK:
            c = self.BACK.index(k)
            for level in self.levels:
                self.return_quarter(c, level, self.z).wait_recv()
            self.return_half(c, self.x).start()

    def finish(self):
        for c in range(self.PARTS):
            self.give_half(c).wait_send()
            for level in self.levels:
                self.give_quarter(c, self.z, level).wait_send()
                self.return_quarter(c, self.z, level).wait_send()
            self.return_half(c, self.x).wait_send()
            self.return_half(c, 1 - self.x).wait_recv()
        for other in self.others:
            self.give_bias(self.me, other).wait_send()
            self.give_bias(other, self.me).wait_recv()
        value = self.total[pl.ds(self.depth, 8), :]
        for other in self.others:
            value = value + self.bias_in[other]
        self.result[pl.ds(self.depth, 8), :] = value


def exchange_kernel(
    n, clusters, tile, features, adjacency, cotangent, segments, weight, bias,
    activations, scaled, summed_total, sten, blocks_out, grads, *rest,
):
    landing = (None,) + rest[: n - 1]
    pieces = list(rest[n - 1 : 2 * n - 3])
    pieces = pieces[:1] + [activations] + pieces[1:] + [scaled]
    (feat, adj, cot, grad, seg, mat, vec, total, shares, back, load_sem, cot_sem, grad_sem,
     fixed_sem, send_sem, recv_sem, grad_out, grad_in, back_sem, share_send, share_recv, spread_send, spread_recv,
     block_send, block_recv, half_in, quarter_in, bias_in, sum_sems) = rest[2 * n - 3 :]
    outer = n // 2
    rows, width = features.shape
    depth = mat.shape[0]
    count = rows // tile
    me, cluster = lax.axis_index("col"), lax.axis_index("clu")
    chip, core = me // 2, lax.rem(me, 2)
    sibling = chip * 2 + 1 - core
    part = 2 * width // clusters

    def chip_at(shift):
        return lax.rem(chip + shift + outer, outer) * 2 + core

    def at(k):
        return pl.ds(pl.multiple_of(k * tile, tile), tile)

    def loads(k):
        slot = lax.rem(k, 2)
        return (
            pltpu.make_async_copy(features.at[at(k)], feat.at[slot], load_sem.at[0, slot]),
            pltpu.make_async_copy(adjacency.at[at(k)], adj.at[slot], load_sem.at[1, slot]),
        )

    def load_cot(k):
        slot = lax.rem(k, 2)
        return pltpu.make_async_copy(cotangent.at[at(k)], cot.at[slot], cot_sem.at[slot])

    def store_grad(k):
        slot = lax.rem(k, 2)
        return pltpu.make_async_copy(grad.at[slot], grads.at[at(k)], grad_sem.at[slot])

    def remote(source, target, send, recv, device, axis="col"):
        return pltpu.make_async_remote_copy(
            src_ref=source, dst_ref=target, send_sem=send, recv_sem=recv,
            device_id={axis: device}, device_id_type=MESH,
        )

    def hop(p, k):
        source = 0 if p % 2 == 0 else p - 1
        device = chip_at(-(p // 2)) if p % 2 == 0 else sibling
        return remote(pieces[source].at[at(k)], pieces[p].at[at(k)], send_sem.at[p, k], recv_sem.at[p, k], device)

    def grad_hop(p, k):
        source = grads if p < 2 or p % 2 == 0 else landing[p - 1]
        device = chip_at(-(p // 2)) if p % 2 == 0 else sibling
        return remote(source.at[at(k)], landing[p].at[at(k)], grad_out.at[p, k], grad_in.at[p, k], device)

    def send_grad(k):
        for shift in range(1, outer):
            grad_hop(2 * shift, k).start()
        grad_hop(1, k).start()

    def load_piece(p, k):
        slot = lax.rem(k, 2)
        source = landing[p] if p else grads
        return pltpu.make_async_copy(source.at[at(k)], back.at[slot, p], back_sem.at[slot, p])

    def share(shift):
        owner = lax.rem(chip - shift + outer, outer)
        rows = pl.ds(pl.multiple_of(owner * 2 * width + cluster * part, part), part)
        mine = pl.ds(pl.multiple_of(cluster * part, part), part)
        return remote(
            weight.at[rows], shares.at[shift, mine], share_send.at[shift], share_recv.at[shift], chip_at(-shift)
        )

    def spread(shift, source, peer):
        rows = pl.ds(pl.multiple_of(source * part, part), part)
        return remote(
            shares.at[shift, rows], shares.at[shift, rows],
            spread_send.at[shift, peer], spread_recv.at[shift, source], peer, "clu",
        )

    def block(p):
        half = core if p % 2 == 0 else 1 - core
        if p < 2:
            source = weight.at[pl.ds(pl.multiple_of((chip * 2 + half) * width, width), width)]
        else:
            source = shares.at[p // 2, pl.ds(pl.multiple_of(half * width, width), width)]
        if p % 2 == 0:
            return pltpu.make_async_copy(source, blocks_out.at[p], block_recv.at[p])
        return remote(source, blocks_out.at[p], block_send.at[p], block_recv.at[p], sibling)

    others = [lax.rem(cluster + d, clusters) for d in range(1, clusters)]
    for copy in loads(0):
        copy.start()
    fixed = [
        pltpu.make_async_copy(source, target, fixed_sem.at[i])
        for i, (source, target) in enumerate([(segments, seg), (weight, mat), (bias, vec)])
    ]
    for copy in fixed:
        copy.start()
    load_cot(0).start()

    barrier = pltpu.get_barrier_semaphore()
    peers = [("col", sibling)] + [("col", chip_at(shift)) for shift in range(1, outer)]
    peers += [("clu", peer) for peer in others]
    for axis, peer in peers:
        pl.semaphore_signal(barrier, inc=1, device_id={axis: peer}, device_id_type=MESH)
    pl.semaphore_wait(barrier, len(peers))
    for shift in range(1, outer):
        share(shift).start()
    block(0).start()
    block(1).start()
    fixed[0].wait()

    def aggregate_tile(k, carry):
        slot = lax.rem(k, 2)
        for copy in loads(k):
            copy.wait()

        @pl.when(k + 1 < count)
        def _():
            for copy in loads(k + 1):
                copy.start()

        for b in range(tile // BLOCK):
            part = pl.ds(b * BLOCK, BLOCK)
            stencil, inverse = stencil_of(adj[slot, part, :], seg[pl.ds(k * (tile // BLOCK) + b, 1), :])
            summed = jnp.dot(stencil, feat[slot, part, :], preferred_element_type=F32)
            target = pl.ds(pl.multiple_of(k * tile + b * BLOCK, BLOCK), BLOCK)
            sten[target, :] = stencil
            pieces[0][target, :] = (summed * inverse).astype(BF16)
        for shift in range(1, outer):
            hop(2 * shift, k).start()
        hop(1, k).start()
        return carry

    lax.fori_loop(0, count, aggregate_tile, 0)
    total[...] = jnp.zeros_like(total)
    fixed[1].wait()
    fixed[2].wait()
    blocks = [lax.rem(chip + p // 2, outer) * 2 + (core if p % 2 == 0 else 1 - core) for p in range(n)]

    def forward_tile(k):
        slot = lax.rem(k, 2)
        load_cot(k).wait()

        @pl.when(k + 1 < count)
        def _():
            load_cot(k + 1).start()

        hop(1, k).wait_recv()
        for shift in range(1, outer):
            hop(2 * shift + 1, k).wait_recv()

        @pl.when(k >= 2)
        def _():
            store_grad(k - 2).wait()
            send_grad(k - 2)

        preact = None
        for p in range(n):
            source = pl.ds(pl.multiple_of(blocks[p] * width, width), width)
            term = jnp.dot(pieces[p][at(k), :], mat[source, :], preferred_element_type=F32)
            preact = term if preact is None else preact + term
        preact = preact + vec[...].astype(F32).reshape(1, width)
        grad_preact = jnp.where(preact > 0.0, cot[slot].astype(F32), 0.0)
        total[pl.ds(depth, 8), :] += jnp.sum(grad_preact.reshape(tile // 8, 8, width), axis=0)
        grad_preact = grad_preact.astype(BF16)
        grad[slot] = grad_preact
        store_grad(k).start()
        for p in range(n):
            target = pl.ds(pl.multiple_of(blocks[p] * width, width), width)
            total[target, :] += lax.dot_general(
                pieces[p][at(k), :], grad_preact, (((0,), (0,)), ((), ())), preferred_element_type=F32
            )
        activations[at(k), :] = jnp.maximum(preact, 0.0).astype(BF16)

    def step(k, carry):
        @pl.when(k < count)
        def _():
            for shift in range(1, outer):
                hop(2 * shift, k).wait_recv()
                hop(2 * shift + 1, k).start()

        @pl.when(k == 1)
        def _():
            for shift in range(1, outer):
                share(shift).wait_recv()
                for peer in others:
                    spread(shift, cluster, peer).start()

        @pl.when(k == 4)
        def _():
            for shift in range(1, outer):
                for peer in others:
                    spread(shift, peer, cluster).wait_recv()
                block(2 * shift).start()
                block(2 * shift + 1).start()

        @pl.when(k >= 1)
        def _():
            forward_tile(k - 1)

        return carry

    lax.fori_loop(0, count + 1, step, 0)
    sums = cluster_sum(total, summed_total, half_in, quarter_in, bias_in, sum_sems, clusters)
    sums.start()
    for k in (count - 2, count - 1):
        store_grad(k).wait()
        send_grad(k)
    for p in range(n):
        if p % 2:
            block(p).wait_recv()
        else:
            block(p).wait()
    copies = [
        pltpu.make_async_copy(blocks_out.at[p], mat.at[pl.ds(p * width, width)], block_send.at[p - p % 2])
        for p in range(0, n, 2)
    ] + [
        pltpu.make_async_copy(blocks_out.at[p], mat.at[pl.ds(p * width, width)], block_recv.at[p])
        for p in range(1, n, 2)
    ]
    for copy in copies:
        copy.start()
    for copy in copies:
        copy.wait()

    def backward_tile(k):
        slot = lax.rem(k, 2)
        for p in range(n):
            load_piece(p, k).wait()

        value = None
        for p in range(n):
            term = lax.dot_general(
                back[slot, p], mat[pl.ds(p * width, width), :], (((1,), (1,)), ((), ())), preferred_element_type=F32
            )
            value = term if value is None else value + term
        inverse = 1.0 / (jnp.sum(sten[at(k), :].astype(F32), axis=1, keepdims=True) - 1.0)
        scaled[at(k), :] = (value.astype(BF16).astype(F32) * inverse).astype(BF16)

    def moment(r):
        return max(r * 512 // tile, 0)

    def back_step(k, carry):
        @pl.when(k >= 1)
        def _():
            backward_tile(k - 1)

        @pl.when(k < count)
        def _():
            for shift in range(1, outer):
                grad_hop(2 * shift, k).wait_recv()
                grad_hop(2 * shift + 1, k).start()
            grad_hop(1, k).wait_recv()
            for shift in range(1, outer):
                grad_hop(2 * shift + 1, k).wait_recv()
            for p in range(n):
                load_piece(p, k).start()

        for r in range(sums.rounds):
            if moment(r) <= count:
                pl.when(k == moment(r))(functools.partial(sums.advance, r))
        if moment(sums.last) <= count:
            pl.when(k == moment(sums.last))(sums.finish)
        return carry

    lax.fori_loop(0, count + 1, back_step, 0)
    for r in range(sums.rounds):
        if moment(r) > count:
            sums.advance(r)
    if moment(sums.last) > count:
        sums.finish()

    def finish(k, carry):
        for p in range(1, n):
            hop(p, k).wait_send()
            grad_hop(p, k).wait_send()
        return carry

    lax.fori_loop(0, count, finish, 0)
    for p in range(1, n, 2):
        block(p).wait_send()
    for shift in range(1, outer):
        share(shift).wait_send()
        for peer in others:
            spread(shift, cluster, peer).wait_send()


def exchange(features, adjacency, cotangent, segments, weight, bias, n, clusters, tile):
    rows, width = features.shape
    depth = weight.shape[0]
    count, outer = rows // tile, n // 2
    parts, high = cluster_sum.PARTS, clusters // 2
    dma = pltpu.SemaphoreType.DMA
    array = jax.ShapeDtypeStruct
    return pl.pallas_call(
        functools.partial(exchange_kernel, n, clusters, tile),
        in_specs=[HBM] * 6,
        out_specs=[VMEM] * 4 + [HBM] * (n + 1),
        out_shape=[
            pltpu.VMEM((rows, width), BF16),
            pltpu.VMEM((rows, width), BF16),
            pltpu.VMEM((depth + 8, width), F32),
            pltpu.VMEM((rows, BLOCK), BF16),
            array((n, width, width), BF16),
        ]
        + [array((rows, width), BF16)] * n,
        scratch_shapes=[pltpu.VMEM((rows, width), BF16)] * (n - 2)
        + [
            pltpu.VMEM((2, tile, width), BF16),
            pltpu.VMEM((2, tile, BLOCK), jnp.int32),
            pltpu.VMEM((2, tile, width), BF16),
            pltpu.VMEM((2, tile, width), BF16),
            pltpu.VMEM(segments.shape, jnp.int32),
            pltpu.VMEM((depth, width), BF16),
            pltpu.VMEM((width,), BF16),
            pltpu.VMEM((depth + 8, width), F32),
            pltpu.VMEM((outer, 2 * width, width), BF16),
            pltpu.VMEM((2, n, tile, width), BF16),
            dma((2, 2)),
            dma((2,)),
            dma((2,)),
            dma((3,)),
            dma((n, count)),
            dma((n, count)),
            dma((n, count)),
            dma((n, count)),
            dma((2, n)),
            dma((outer,)),
            dma((outer,)),
            dma((outer, clusters)),
            dma((outer, clusters)),
            dma((n,)),
            dma((n,)),
            pltpu.VMEM((parts, depth // parts // 2, width), F32),
            pltpu.VMEM((parts, high, depth // parts // 2 // high, width), F32),
            pltpu.VMEM((clusters, 8, width), F32),
            [
                dma((parts,)), dma((parts,)), dma((parts, high)), dma((parts, high)), dma((parts, high)),
                dma((parts, high)), dma((parts,)), dma((parts,)), dma((clusters,)), dma((clusters,)),
            ],
        ],
        compiler_params=pltpu.CompilerParams(
            collective_id=0, has_side_effects=True, vmem_limit_bytes=40 << 20
        ),
    )(*[pltpu.with_memory_space_constraint(x, pltpu.HBM) for x in (features, adjacency, cotangent, segments, weight, bias)])


def finish_kernel(tile, activations, scaled, total, stencil, grad_features, out, grad_weight, grad_bias, slots, row, slot_sem, fixed_sem):
    rows, width = scaled.shape
    depth = total.shape[0] - 8
    count = rows // tile
    row[...] = jnp.sum(total[pl.ds(depth, 8), :], axis=0, keepdims=True)
    fixed = [
        pltpu.make_async_copy(activations, out, fixed_sem.at[0]),
        pltpu.make_async_copy(total.at[pl.ds(0, depth)], grad_weight, fixed_sem.at[1]),
        pltpu.make_async_copy(row, grad_bias, fixed_sem.at[2]),
    ]
    for copy in fixed:
        copy.start()

    def store(k):
        slot = lax.rem(k, SLOTS)
        target = pl.ds(pl.multiple_of(k * tile, tile), tile)
        return pltpu.make_async_copy(slots.at[slot], grad_features.at[target], slot_sem.at[slot])

    def step(k, carry):
        slot = lax.rem(k, SLOTS)

        @pl.when(k >= SLOTS)
        def _():
            store(k - SLOTS).wait()

        for b in range(tile // BLOCK):
            source = pl.ds(pl.multiple_of(k * tile + b * BLOCK, BLOCK), BLOCK)
            slots[slot, pl.ds(b * BLOCK, BLOCK), :] = jnp.dot(
                stencil[source, :], scaled[source, :], preferred_element_type=F32
            )
        store(k).start()
        return carry

    lax.fori_loop(0, count, step, 0)
    for k in range(max(count - SLOTS, 0), count):
        store(k).wait()
    for copy in fixed:
        copy.wait()


def finish(activations, scaled, total, stencil):
    rows, width = scaled.shape
    depth = total.shape[0] - 8
    tile = 512
    dma = pltpu.SemaphoreType.DMA
    return pl.pallas_call(
        functools.partial(finish_kernel, tile),
        in_specs=[VMEM] * 4,
        out_specs=[HBM] * 4,
        out_shape=[
            jax.ShapeDtypeStruct((rows, width), F32),
            jax.ShapeDtypeStruct((rows, width), BF16),
            jax.ShapeDtypeStruct((depth, width), F32),
            jax.ShapeDtypeStruct((1, width), F32),
        ],
        scratch_shapes=[
            pltpu.VMEM((SLOTS, tile, width), F32),
            pltpu.VMEM((1, width), F32),
            dma((SLOTS,)),
            dma((3,)),
        ],
        cost_estimate=pl.CostEstimate(
            flops=2 * rows * BLOCK * width, bytes_accessed=6 * rows * width + 4 * depth * width, transcendentals=0
        ),
        compiler_params=pltpu.CompilerParams(vmem_limit_bytes=12 << 20),
    )(activations, scaled, total, stencil)


def build(n, clusters):
    def local(features, weight, bias, adjacency, segments, cotangent):
        tile = 256 if n <= 4 else 512
        held = exchange(features, adjacency, cotangent, segments, weight, bias, n, clusters, tile)[:4]
        grad_features, out, grad_weight, grad_bias = finish(*held)
        return (out, grad_features, grad_weight, grad_bias.reshape(-1))

    return local


def solution(mesh):
    return jax.shard_map(
        build(mesh.shape["col"], mesh.shape["clu"]),
        mesh=mesh,
        in_specs=(
            P("clu", "col"),
            P(None, "col"),
            P("col"),
            P("clu", None),
            P("clu", None),
            P("clu", "col"),
        ),
        out_specs=(P("clu", "col"), P("clu", "col"), P(None, "col"), P("col")),
        check_vma=False,
    )
```

```python
import functools

import jax
import jax.numpy as jnp
from jax import lax
from jax.experimental import pallas as pl
from jax.experimental.pallas import tpu as pltpu
from jax.sharding import PartitionSpec as P

BLOCK = 128
SLOTS = 4
F32 = jnp.float32
BF16 = jnp.bfloat16
MESH = pl.DeviceIdType.MESH
HBM = pl.BlockSpec(memory_space=pltpu.HBM)
VMEM = pl.BlockSpec(memory_space=pltpu.VMEM)


def stencil_of(adjacency, segment):
    columns = jnp.broadcast_to(segment, (BLOCK, BLOCK))
    links = jnp.where(columns == columns.T, adjacency, 0).astype(F32)
    inverse = 1.0 / (jnp.sum(links, axis=1, keepdims=True) + 1.0)
    row = lax.broadcasted_iota(jnp.int32, (BLOCK, BLOCK), 0)
    column = lax.broadcasted_iota(jnp.int32, (BLOCK, BLOCK), 1)
    return (links + jnp.where(row == column, 2.0, 0.0)).astype(BF16), inverse


def back_through(piece, n, blocks, stencil):
    width = blocks.shape[1]
    value = None
    for p in range(n):
        term = lax.dot_general(
            piece(p), blocks[pl.ds(p * width, width), :], (((1,), (1,)), ((), ())), preferred_element_type=F32
        )
        value = term if value is None else value + term
    inverse = 1.0 / (jnp.sum(stencil.astype(F32), axis=1, keepdims=True) - 1.0)
    return (value.astype(BF16).astype(F32) * inverse).astype(BF16)


class cluster_sum:
    PARTS = 4
    BACK = (5, 7, 8, 9)
    rounds = 10
    last = 12

    def __init__(self, total, result, half_in, quarter_in, bias_in, sems, clusters):
        self.result = result
        self.total, self.half_in, self.quarter_in, self.bias_in, self.sems = total, half_in, quarter_in, bias_in, sems
        self.clusters, self.high = clusters, clusters // 2
        self.depth = total.shape[0] - 8
        self.half = self.depth // self.PARTS // 2
        self.quarter = self.half // self.high
        self.me = lax.axis_index("clu")
        self.z, self.x = self.me // 2, lax.rem(self.me, 2)
        self.others = [lax.rem(self.me + d, clusters) for d in range(1, clusters)]
        self.levels = [lax.rem(self.z + d, self.high) for d in range(1, self.high)]

    def rows_of_half(self, c, x):
        return pl.ds(pl.multiple_of(c * 2 * self.half + x * self.half, self.half), self.half)

    def rows_of_quarter(self, c, q):
        start = c * 2 * self.half + self.x * self.half + q * self.quarter
        return pl.ds(pl.multiple_of(start, self.quarter), self.quarter)

    def copy(self, source, target, kind, send, recv, device):
        return pltpu.make_async_remote_copy(
            src_ref=source, dst_ref=target, send_sem=self.sems[2 * kind].at[send],
            recv_sem=self.sems[2 * kind + 1].at[recv], device_id={"clu": device}, device_id_type=MESH,
        )

    def give_half(self, c):
        rows = self.rows_of_half(c, 1 - self.x)
        return self.copy(self.total.at[rows], self.half_in.at[c], 0, c, c, self.z * 2 + 1 - self.x)

    def give_quarter(self, c, source, target):
        rows = self.rows_of_quarter(c, target)
        return self.copy(
            self.total.at[rows], self.quarter_in.at[c, source], 1, (c, target), (c, source), target * 2 + self.x
        )

    def return_quarter(self, c, source, target):
        rows = self.rows_of_quarter(c, source)
        return self.copy(
            self.result.at[rows], self.result.at[rows], 2, (c, target), (c, source), target * 2 + self.x
        )

    def return_half(self, c, x):
        rows = self.rows_of_half(c, x)
        return self.copy(self.result.at[rows], self.result.at[rows], 3, c, c, self.z * 2 + 1 - self.x)

    def give_bias(self, source, target):
        return self.copy(
            self.total.at[pl.ds(self.depth, 8)], self.bias_in.at[source], 4, target, source, target
        )

    def start(self):
        for c in range(self.PARTS):
            self.give_half(c).start()
        for other in self.others:
            self.give_bias(self.me, other).start()

    def advance(self, k):
        total = self.total
        if k < self.PARTS:
            self.give_half(k).wait_recv()
            total[self.rows_of_half(k, self.x), :] += self.half_in[k]
            for level in self.levels:
                self.give_quarter(k, self.z, level).start()
        c = k - 2
        if 0 <= c < self.PARTS:
            rows = self.rows_of_quarter(c, self.z)
            for level in self.levels:
                self.give_quarter(c, level, self.z).wait_recv()
            value = total[rows, :]
            for level in self.levels:
                value = value + self.quarter_in[c, level]
            self.result[rows, :] = value
            for level in self.levels:
                self.return_quarter(c, self.z, level).start()
        if k in self.BACK:
            c = self.BACK.index(k)
            for level in self.levels:
                self.return_quarter(c, level, self.z).wait_recv()
            self.return_half(c, self.x).start()

    def finish(self):
        for c in range(self.PARTS):
            self.give_half(c).wait_send()
            for level in self.levels:
                self.give_quarter(c, self.z, level).wait_send()
                self.return_quarter(c, self.z, level).wait_send()
            self.return_half(c, self.x).wait_send()
            self.return_half(c, 1 - self.x).wait_recv()
        for other in self.others:
            self.give_bias(self.me, other).wait_send()
            self.give_bias(other, self.me).wait_recv()
        value = self.total[pl.ds(self.depth, 8), :]
        for other in self.others:
            value = value + self.bias_in[other]
        self.result[pl.ds(self.depth, 8), :] = value


def exchange_kernel(
    n, clusters, tile, features, adjacency, cotangent, segments, weight, bias,
    activations, scaled, summed_total, sten, mat, last, blocks_out, grads, *rest,
):
    landing = (None,) + rest[: n - 1]
    pieces = list(rest[n - 1 : 2 * n - 3])
    pieces = pieces[:1] + [activations] + pieces[1:] + [scaled]
    (feat, adj, cot, grad, seg, vec, total, shares, back, load_sem, cot_sem, grad_sem,
     fixed_sem, send_sem, recv_sem, grad_out, grad_in, back_sem, share_send, share_recv, spread_send, spread_recv,
     block_send, block_recv, half_in, quarter_in, bias_in, sum_sems) = rest[2 * n - 3 :]
    outer = n // 2
    rows, width = features.shape
    depth = mat.shape[0]
    count = rows // tile
    me, cluster = lax.axis_index("col"), lax.axis_index("clu")
    chip, core = me // 2, lax.rem(me, 2)
    sibling = chip * 2 + 1 - core
    part = 2 * width // clusters

    def chip_at(shift):
        return lax.rem(chip + shift + outer, outer) * 2 + core

    def at(k):
        return pl.ds(pl.multiple_of(k * tile, tile), tile)

    def loads(k):
        slot = lax.rem(k, 2)
        return (
            pltpu.make_async_copy(features.at[at(k)], feat.at[slot], load_sem.at[0, slot]),
            pltpu.make_async_copy(adjacency.at[at(k)], adj.at[slot], load_sem.at[1, slot]),
        )

    def load_cot(k):
        slot = lax.rem(k, 2)
        return pltpu.make_async_copy(cotangent.at[at(k)], cot.at[slot], cot_sem.at[slot])

    def store_grad(k):
        slot = lax.rem(k, 2)
        return pltpu.make_async_copy(grad.at[slot], grads.at[at(k)], grad_sem.at[slot])

    def remote(source, target, send, recv, device, axis="col"):
        return pltpu.make_async_remote_copy(
            src_ref=source, dst_ref=target, send_sem=send, recv_sem=recv,
            device_id={axis: device}, device_id_type=MESH,
        )

    def hop(p, k):
        source = 0 if p % 2 == 0 else p - 1
        device = chip_at(-(p // 2)) if p % 2 == 0 else sibling
        return remote(pieces[source].at[at(k)], pieces[p].at[at(k)], send_sem.at[p, k], recv_sem.at[p, k], device)

    def grad_hop(p, k):
        source = grads if p < 2 or p % 2 == 0 else landing[p - 1]
        device = chip_at(-(p // 2)) if p % 2 == 0 else sibling
        return remote(source.at[at(k)], landing[p].at[at(k)], grad_out.at[p, k], grad_in.at[p, k], device)

    def last_hop(p):
        device = chip_at(-(p // 2)) if p % 2 == 0 else sibling
        source = last.at[0 if p % 2 == 0 else p - 1]
        return remote(source, last.at[p], grad_out.at[p, count - 1], grad_in.at[p, count - 1], device)

    def send_grad(k):
        for shift in range(1, outer):
            grad_hop(2 * shift, k).start()
        grad_hop(1, k).start()

    def load_piece(p, k):
        slot = lax.rem(k, 2)
        source = landing[p] if p else grads
        return pltpu.make_async_copy(source.at[at(k)], back.at[slot, p], back_sem.at[slot, p])

    def share(shift):
        owner = lax.rem(chip - shift + outer, outer)
        rows = pl.ds(pl.multiple_of(owner * 2 * width + cluster * part, part), part)
        mine = pl.ds(pl.multiple_of(cluster * part, part), part)
        return remote(
            weight.at[rows], shares.at[shift, mine], share_send.at[shift], share_recv.at[shift], chip_at(-shift)
        )

    def spread(shift, source, peer):
        rows = pl.ds(pl.multiple_of(source * part, part), part)
        return remote(
            shares.at[shift, rows], shares.at[shift, rows],
            spread_send.at[shift, peer], spread_recv.at[shift, source], peer, "clu",
        )

    def block(p):
        half = core if p % 2 == 0 else 1 - core
        if p < 2:
            source = weight.at[pl.ds(pl.multiple_of((chip * 2 + half) * width, width), width)]
        else:
            source = shares.at[p // 2, pl.ds(pl.multiple_of(half * width, width), width)]
        if p % 2 == 0:
            return pltpu.make_async_copy(source, blocks_out.at[p], block_recv.at[p])
        return remote(source, blocks_out.at[p], block_send.at[p], block_recv.at[p], sibling)

    others = [lax.rem(cluster + d, clusters) for d in range(1, clusters)]
    for copy in loads(0):
        copy.start()
    fixed = [
        pltpu.make_async_copy(source, target, fixed_sem.at[i])
        for i, (source, target) in enumerate([(segments, seg), (weight, mat), (bias, vec)])
    ]
    for copy in fixed:
        copy.start()
    load_cot(0).start()

    barrier = pltpu.get_barrier_semaphore()
    peers = [("col", sibling)] + [("col", chip_at(shift)) for shift in range(1, outer)]
    peers += [("clu", peer) for peer in others]
    for axis, peer in peers:
        pl.semaphore_signal(barrier, inc=1, device_id={axis: peer}, device_id_type=MESH)
    pl.semaphore_wait(barrier, len(peers))
    for shift in range(1, outer):
        share(shift).start()
    block(0).start()
    block(1).start()
    fixed[0].wait()

    def aggregate_tile(k, carry):
        slot = lax.rem(k, 2)
        for copy in loads(k):
            copy.wait()

        @pl.when(k + 1 < count)
        def _():
            for copy in loads(k + 1):
                copy.start()

        for b in range(tile // BLOCK):
            part = pl.ds(b * BLOCK, BLOCK)
            stencil, inverse = stencil_of(adj[slot, part, :], seg[pl.ds(k * (tile // BLOCK) + b, 1), :])
            summed = jnp.dot(stencil, feat[slot, part, :], preferred_element_type=F32)
            target = pl.ds(pl.multiple_of(k * tile + b * BLOCK, BLOCK), BLOCK)
            sten[target, :] = stencil
            pieces[0][target, :] = (summed * inverse).astype(BF16)
        for shift in range(1, outer):
            hop(2 * shift, k).start()
        hop(1, k).start()
        return carry

    lax.fori_loop(0, count, aggregate_tile, 0)
    total[...] = jnp.zeros_like(total)
    fixed[1].wait()
    fixed[2].wait()
    blocks = [lax.rem(chip + p // 2, outer) * 2 + (core if p % 2 == 0 else 1 - core) for p in range(n)]

    def forward_tile(k):
        slot = lax.rem(k, 2)
        load_cot(k).wait()

        @pl.when(k + 1 < count)
        def _():
            load_cot(k + 1).start()

        hop(1, k).wait_recv()
        for shift in range(1, outer):
            hop(2 * shift + 1, k).wait_recv()

        @pl.when(k >= 2)
        def _():
            store_grad(k - 2).wait()
            send_grad(k - 2)

        preact = None
        for p in range(n):
            source = pl.ds(pl.multiple_of(blocks[p] * width, width), width)
            term = jnp.dot(pieces[p][at(k), :], mat[source, :], preferred_element_type=F32)
            preact = term if preact is None else preact + term
        preact = preact + vec[...].astype(F32).reshape(1, width)
        grad_preact = jnp.where(preact > 0.0, cot[slot].astype(F32), 0.0)
        total[pl.ds(depth, 8), :] += jnp.sum(grad_preact.reshape(tile // 8, 8, width), axis=0)
        grad_preact = grad_preact.astype(BF16)
        grad[slot] = grad_preact

        @pl.when(k < count - 1)
        def _():
            store_grad(k).start()

        @pl.when(k == count - 1)
        def _():
            last[0] = grad_preact

        for p in range(n):
            target = pl.ds(pl.multiple_of(blocks[p] * width, width), width)
            total[target, :] += lax.dot_general(
                pieces[p][at(k), :], grad_preact, (((0,), (0,)), ((), ())), preferred_element_type=F32
            )
        activations[at(k), :] = jnp.maximum(preact, 0.0).astype(BF16)

    def step(k, carry):
        @pl.when(k < count)
        def _():
            for shift in range(1, outer):
                hop(2 * shift, k).wait_recv()
                hop(2 * shift + 1, k).start()

        @pl.when(k == 1)
        def _():
            for shift in range(1, outer):
                share(shift).wait_recv()
                for peer in others:
                    spread(shift, cluster, peer).start()

        @pl.when(k == 4)
        def _():
            for shift in range(1, outer):
                for peer in others:
                    spread(shift, peer, cluster).wait_recv()
                block(2 * shift).start()
                block(2 * shift + 1).start()

        @pl.when(k >= 1)
        def _():
            forward_tile(k - 1)

        return carry

    lax.fori_loop(0, count + 1, step, 0)
    sums = cluster_sum(total, summed_total, half_in, quarter_in, bias_in, sum_sems, clusters)
    sums.start()
    store_grad(count - 2).wait()
    send_grad(count - 2)
    for p in range(1, n):
        if p == 1 or p % 2 == 0:
            last_hop(p).start()
    for p in range(1, n, 2):
        block(p).wait_send()
    for shift in range(1, outer):
        share(shift).wait_send()
        for peer in others:
            spread(shift, cluster, peer).wait_send()
    for p in range(n):
        if p % 2:
            block(p).wait_recv()
        else:
            block(p).wait()
    copies = [
        pltpu.make_async_copy(blocks_out.at[p], mat.at[pl.ds(p * width, width)], block_send.at[p - p % 2])
        for p in range(0, n, 2)
    ] + [
        pltpu.make_async_copy(blocks_out.at[p], mat.at[pl.ds(p * width, width)], block_recv.at[p])
        for p in range(1, n, 2)
    ]
    for copy in copies:
        copy.start()
    for copy in copies:
        copy.wait()

    def backward_tile(k):
        slot = lax.rem(k, 2)
        for p in range(n):
            load_piece(p, k).wait()
        scaled[at(k), :] = back_through(lambda p: back[slot, p], n, mat, sten[at(k), :])

    def moment(r):
        return max(r * 512 // tile, 0)

    def back_step(k, carry):
        @pl.when(k >= 1)
        def _():
            backward_tile(k - 1)
            for p in range(1, n):
                grad_hop(p, k - 1).wait_send()

        for p in range(1, n):
            hop(p, k).wait_send()

        @pl.when(k < count - 1)
        def _():
            for shift in range(1, outer):
                grad_hop(2 * shift, k).wait_recv()
                grad_hop(2 * shift + 1, k).start()
            grad_hop(1, k).wait_recv()
            for shift in range(1, outer):
                grad_hop(2 * shift + 1, k).wait_recv()
            for p in range(n):
                load_piece(p, k).start()

        for r in range(sums.rounds):
            if moment(r) < count:
                pl.when(k == moment(r))(functools.partial(sums.advance, r))
        if moment(sums.last) < count:
            pl.when(k == moment(sums.last))(sums.finish)
        return carry

    lax.fori_loop(0, count, back_step, 0)
    for r in range(sums.rounds):
        if moment(r) >= count:
            sums.advance(r)
    if moment(sums.last) >= count:
        sums.finish()
    for p in range(2, n, 2):
        last_hop(p).wait_recv()
        last_hop(p + 1).start()
    for p in range(1, n):
        if p % 2:
            last_hop(p).wait_recv()
        last_hop(p).wait_send()


def exchange(features, adjacency, cotangent, segments, weight, bias, n, clusters, tile):
    rows, width = features.shape
    depth = weight.shape[0]
    count, outer = rows // tile, n // 2
    parts, high = cluster_sum.PARTS, clusters // 2
    dma = pltpu.SemaphoreType.DMA
    array = jax.ShapeDtypeStruct
    return pl.pallas_call(
        functools.partial(exchange_kernel, n, clusters, tile),
        in_specs=[HBM] * 6,
        out_specs=[VMEM] * 6 + [HBM] * (n + 1),
        out_shape=[
            pltpu.VMEM((rows, width), BF16),
            pltpu.VMEM((rows, width), BF16),
            pltpu.VMEM((depth + 8, width), F32),
            pltpu.VMEM((rows, BLOCK), BF16),
            pltpu.VMEM((depth, width), BF16),
            pltpu.VMEM((n, tile, width), BF16),
            array((n, width, width), BF16),
        ]
        + [array((rows, width), BF16)] * n,
        scratch_shapes=[pltpu.VMEM((rows, width), BF16)] * (n - 2)
        + [
            pltpu.VMEM((2, tile, width), BF16),
            pltpu.VMEM((2, tile, BLOCK), jnp.int32),
            pltpu.VMEM((2, tile, width), BF16),
            pltpu.VMEM((2, tile, width), BF16),
            pltpu.VMEM(segments.shape, jnp.int32),
            pltpu.VMEM((width,), BF16),
            pltpu.VMEM((depth + 8, width), F32),
            pltpu.VMEM((outer, 2 * width, width), BF16),
            pltpu.VMEM((2, n, tile, width), BF16),
            dma((2, 2)),
            dma((2,)),
            dma((2,)),
            dma((3,)),
            dma((n, count)),
            dma((n, count)),
            dma((n, count)),
            dma((n, count)),
            dma((2, n)),
            dma((outer,)),
            dma((outer,)),
            dma((outer, clusters)),
            dma((outer, clusters)),
            dma((n,)),
            dma((n,)),
            pltpu.VMEM((parts, depth // parts // 2, width), F32),
            pltpu.VMEM((parts, high, depth // parts // 2 // high, width), F32),
            pltpu.VMEM((clusters, 8, width), F32),
            [
                dma((parts,)), dma((parts,)), dma((parts, high)), dma((parts, high)), dma((parts, high)),
                dma((parts, high)), dma((parts,)), dma((parts,)), dma((clusters,)), dma((clusters,)),
            ],
        ],
        compiler_params=pltpu.CompilerParams(
            collective_id=0, has_side_effects=True, vmem_limit_bytes=38 << 20
        ),
    )(*[pltpu.with_memory_space_constraint(x, pltpu.HBM) for x in (features, adjacency, cotangent, segments, weight, bias)])


def finish_kernel(
    activations, scaled, total, stencil, blocks, last,
    grad_features, out, grad_weight, grad_bias, slots, row, rest, slot_sem, fixed_sem,
):
    rows, width = scaled.shape
    n, tile, _ = last.shape
    depth = total.shape[0] - 8
    span = 2 * tile
    count = rows // span
    row[...] = jnp.sum(total[pl.ds(depth, 8), :], axis=0, keepdims=True)
    fixed = [
        pltpu.make_async_copy(activations, out, fixed_sem.at[0]),
        pltpu.make_async_copy(total.at[pl.ds(0, depth)], grad_weight, fixed_sem.at[1]),
        pltpu.make_async_copy(row, grad_bias, fixed_sem.at[2]),
    ]
    for copy in fixed:
        copy.start()
    rest[...] = back_through(lambda p: last[p], n, blocks, stencil[pl.ds(rows - tile, tile), :])

    def store(k):
        slot = lax.rem(k, SLOTS)
        target = pl.ds(pl.multiple_of(k * span, span), span)
        return pltpu.make_async_copy(slots.at[slot], grad_features.at[target], slot_sem.at[slot])

    def step(k, own):
        slot = lax.rem(k, SLOTS)
        for b in range(span // BLOCK):
            source = pl.ds(pl.multiple_of(k * span + b * BLOCK, BLOCK), BLOCK)
            if b * BLOCK < own:
                value = scaled[source, :]
            else:
                value = rest[pl.ds(b * BLOCK - own, BLOCK), :]
            slots[slot, pl.ds(b * BLOCK, BLOCK), :] = jnp.dot(
                stencil[source, :], value, preferred_element_type=F32
            )
        store(k).start()

    def full(k, carry):
        @pl.when(k >= SLOTS)
        def _():
            store(k - SLOTS).wait()

        step(k, span)
        return carry

    lax.fori_loop(0, count - 1, full, 0)
    if count > SLOTS:
        store(count - 1 - SLOTS).wait()
    step(count - 1, tile)
    for k in range(max(count - SLOTS, 0), count):
        store(k).wait()
    for copy in fixed:
        copy.wait()


def finish(activations, scaled, total, stencil, blocks, last):
    rows, width = scaled.shape
    tile = last.shape[1]
    depth = total.shape[0] - 8
    dma = pltpu.SemaphoreType.DMA
    return pl.pallas_call(
        finish_kernel,
        in_specs=[VMEM] * 6,
        out_specs=[HBM] * 4,
        out_shape=[
            jax.ShapeDtypeStruct((rows, width), F32),
            jax.ShapeDtypeStruct((rows, width), BF16),
            jax.ShapeDtypeStruct((depth, width), F32),
            jax.ShapeDtypeStruct((1, width), F32),
        ],
        scratch_shapes=[
            pltpu.VMEM((SLOTS, 2 * tile, width), F32),
            pltpu.VMEM((1, width), F32),
            pltpu.VMEM((tile, width), BF16),
            dma((SLOTS,)),
            dma((3,)),
        ],
        cost_estimate=pl.CostEstimate(
            flops=2 * rows * BLOCK * width, bytes_accessed=6 * rows * width + 4 * depth * width, transcendentals=0
        ),
        compiler_params=pltpu.CompilerParams(vmem_limit_bytes=12 << 20),
    )(activations, scaled, total, stencil, blocks, last)


def build(n, clusters):
    def local(features, weight, bias, adjacency, segments, cotangent):
        tile = 256 if n <= 4 else 512
        held = exchange(features, adjacency, cotangent, segments, weight, bias, n, clusters, tile)[:6]
        grad_features, out, grad_weight, grad_bias = finish(*held)
        return (out, grad_features, grad_weight, grad_bias.reshape(-1))

    return local


def solution(mesh):
    return jax.shard_map(
        build(mesh.shape["col"], mesh.shape["clu"]),
        mesh=mesh,
        in_specs=(
            P("clu", "col"),
            P(None, "col"),
            P("col"),
            P("clu", None),
            P("clu", None),
            P("clu", "col"),
        ),
        out_specs=(P("clu", "col"), P("clu", "col"), P(None, "col"), P("col")),
        check_vma=False,
    )
```

```python
import functools

import jax
import jax.numpy as jnp
from jax import lax
from jax.experimental import pallas as pl
from jax.experimental.pallas import tpu as pltpu
from jax.sharding import PartitionSpec as P

BLOCK = 128
SLOTS = 4
F32 = jnp.float32
BF16 = jnp.bfloat16
MESH = pl.DeviceIdType.MESH
HBM = pl.BlockSpec(memory_space=pltpu.HBM)
VMEM = pl.BlockSpec(memory_space=pltpu.VMEM)


def stencil_of(adjacency, segment):
    columns = jnp.broadcast_to(segment, (BLOCK, BLOCK))
    links = jnp.where(columns == columns.T, adjacency, 0).astype(F32)
    inverse = 1.0 / (jnp.sum(links, axis=1, keepdims=True) + 1.0)
    row = lax.broadcasted_iota(jnp.int32, (BLOCK, BLOCK), 0)
    column = lax.broadcasted_iota(jnp.int32, (BLOCK, BLOCK), 1)
    return (links + jnp.where(row == column, 2.0, 0.0)).astype(BF16), inverse


def back_through(piece, n, blocks, stencil):
    width = blocks.shape[1]
    value = None
    for p in range(n):
        term = lax.dot_general(
            piece(p), blocks[pl.ds(p * width, width), :], (((1,), (1,)), ((), ())), preferred_element_type=F32
        )
        value = term if value is None else value + term
    inverse = 1.0 / (jnp.sum(stencil.astype(F32), axis=1, keepdims=True) - 1.0)
    return (value.astype(BF16).astype(F32) * inverse).astype(BF16)


class cluster_sum:
    PARTS = 4
    BACK = (5, 7, 8, 9)
    rounds = 10
    last = 12

    def __init__(self, total, result, half_in, quarter_in, bias_in, sems, clusters):
        self.result = result
        self.total, self.half_in, self.quarter_in, self.bias_in, self.sems = total, half_in, quarter_in, bias_in, sems
        self.clusters, self.high = clusters, clusters // 2
        self.depth = total.shape[0] - 8
        self.half = self.depth // self.PARTS // 2
        self.quarter = self.half // self.high
        self.me = lax.axis_index("clu")
        self.z, self.x = self.me // 2, lax.rem(self.me, 2)
        self.others = [lax.rem(self.me + d, clusters) for d in range(1, clusters)]
        self.levels = [lax.rem(self.z + d, self.high) for d in range(1, self.high)]

    def rows_of_half(self, c, x):
        return pl.ds(pl.multiple_of(c * 2 * self.half + x * self.half, self.half), self.half)

    def rows_of_quarter(self, c, q):
        start = c * 2 * self.half + self.x * self.half + q * self.quarter
        return pl.ds(pl.multiple_of(start, self.quarter), self.quarter)

    def copy(self, source, target, kind, recv, device):
        return pltpu.make_async_remote_copy(
            src_ref=source, dst_ref=target, send_sem=self.sems[0].at[kind],
            recv_sem=self.sems[1 + kind].at[recv], device_id={"clu": device}, device_id_type=MESH,
        )

    def several(self, rows, kind, recv=0):
        return self.copy(self.total.at[pl.ds(0, rows)], self.result.at[pl.ds(0, rows)], kind, recv, self.others[0])

    def give_half(self, c):
        rows = self.rows_of_half(c, 1 - self.x)
        return self.copy(self.total.at[rows], self.half_in.at[c], 0, c, self.z * 2 + 1 - self.x)

    def give_quarter(self, c, source, target):
        rows = self.rows_of_quarter(c, target)
        return self.copy(
            self.total.at[rows], self.quarter_in.at[c, source], 1, c, target * 2 + self.x
        )

    def return_quarter(self, c, source, target):
        rows = self.rows_of_quarter(c, source)
        return self.copy(
            self.result.at[rows], self.result.at[rows], 2, c, target * 2 + self.x
        )

    def return_half(self, c, x):
        rows = self.rows_of_half(c, x)
        return self.copy(self.result.at[rows], self.result.at[rows], 3, 0, self.z * 2 + 1 - self.x)

    def give_bias(self, source, target):
        return self.copy(
            self.total.at[pl.ds(self.depth, 8)], self.bias_in.at[source], 4, 0, target
        )

    def start(self):
        for c in range(self.PARTS):
            self.give_half(c).start()
        for other in self.others:
            self.give_bias(self.me, other).start()

    def advance(self, k):
        total = self.total
        if k < self.PARTS:
            self.give_half(k).wait_recv()
            total[self.rows_of_half(k, self.x), :] += self.half_in[k]
            for level in self.levels:
                self.give_quarter(k, self.z, level).start()
        c = k - 2
        if 0 <= c < self.PARTS:
            rows = self.rows_of_quarter(c, self.z)
            self.several(len(self.levels) * self.quarter, 1, c).wait_recv()
            value = total[rows, :]
            for level in self.levels:
                value = value + self.quarter_in[c, level]
            self.result[rows, :] = value
            for level in self.levels:
                self.return_quarter(c, self.z, level).start()
        if k in self.BACK:
            c = self.BACK.index(k)
            self.several(len(self.levels) * self.quarter, 2, c).wait_recv()
            self.return_half(c, self.x).start()

    def finish(self):
        halves = self.PARTS * self.half
        quarters = self.PARTS * len(self.levels) * self.quarter
        for kind, rows in enumerate((halves, quarters, quarters, halves, 8 * len(self.others))):
            self.several(rows, kind).wait_send()
        self.several(halves, 3).wait_recv()
        self.several(8 * len(self.others), 4).wait_recv()
        value = self.total[pl.ds(self.depth, 8), :]
        for other in self.others:
            value = value + self.bias_in[other]
        self.result[pl.ds(self.depth, 8), :] = value


def exchange_kernel(
    n, clusters, tile, features, adjacency, cotangent, segments, weight, bias,
    activations, scaled, summed_total, sten, mat, last, blocks_out, grads, *rest,
):
    landing = (None,) + rest[: n - 1]
    pieces = list(rest[n - 1 : 2 * n - 3])
    pieces = pieces[:1] + [activations] + pieces[1:] + [scaled]
    (feat, adj, cot, grad, seg, vec, total, shares, back, load_sem, cot_sem, grad_sem,
     fixed_sem, send_sem, far_in, near_in, grad_out, grad_far, grad_near, last_out, back_sem, share_send, share_recv, spread_send, spread_recv,
     block_send, block_recv, half_in, quarter_in, bias_in, sum_sems) = rest[2 * n - 3 :]
    outer = n // 2
    rows, width = features.shape
    depth = mat.shape[0]
    count = rows // tile
    me, cluster = lax.axis_index("col"), lax.axis_index("clu")
    chip, core = me // 2, lax.rem(me, 2)
    sibling = chip * 2 + 1 - core
    part = 2 * width // clusters
    others = [lax.rem(cluster + d, clusters) for d in range(1, clusters)]

    def chip_at(shift):
        return lax.rem(chip + shift + outer, outer) * 2 + core

    def at(k):
        return pl.ds(pl.multiple_of(k * tile, tile), tile)

    def loads(k):
        slot = lax.rem(k, 2)
        return (
            pltpu.make_async_copy(features.at[at(k)], feat.at[slot], load_sem.at[0, slot]),
            pltpu.make_async_copy(adjacency.at[at(k)], adj.at[slot], load_sem.at[1, slot]),
        )

    def load_cot(k):
        slot = lax.rem(k, 2)
        return pltpu.make_async_copy(cotangent.at[at(k)], cot.at[slot], cot_sem.at[slot])

    def store_grad(k):
        slot = lax.rem(k, 2)
        return pltpu.make_async_copy(grad.at[slot], grads.at[at(k)], grad_sem.at[slot])

    def remote(source, target, send, recv, device, axis="col"):
        return pltpu.make_async_remote_copy(
            src_ref=source, dst_ref=target, send_sem=send, recv_sem=recv,
            device_id={axis: device}, device_id_type=MESH,
        )

    def hop(p, k):
        source = 0 if p % 2 == 0 else p - 1
        device = chip_at(-(p // 2)) if p % 2 == 0 else sibling
        arrival = far_in.at[p // 2 - 1, k] if p % 2 == 0 else near_in.at[k]
        return remote(pieces[source].at[at(k)], pieces[p].at[at(k)], send_sem.at[p], arrival, device)

    def grad_hop(p, k):
        source = grads if p < 2 or p % 2 == 0 else landing[p - 1]
        device = chip_at(-(p // 2)) if p % 2 == 0 else sibling
        arrival = grad_far.at[p // 2 - 1, k] if p % 2 == 0 else grad_near.at[k]
        return remote(source.at[at(k)], landing[p].at[at(k)], grad_out.at[p], arrival, device)

    def several(tiles, send, arrival):
        span = pl.ds(0, tiles * tile)
        return remote(grads.at[span], landing[1].at[span], send, arrival, sibling)

    def last_hop(p):
        device = chip_at(-(p // 2)) if p % 2 == 0 else sibling
        source = last.at[0 if p % 2 == 0 else p - 1]
        arrival = grad_far.at[p // 2 - 1, count - 1] if p % 2 == 0 else grad_near.at[count - 1]
        return remote(source, last.at[p], last_out.at[p], arrival, device)

    def send_grad(k):
        for shift in range(1, outer):
            grad_hop(2 * shift, k).start()
        grad_hop(1, k).start()

    def load_piece(p, k):
        slot = lax.rem(k, 2)
        source = landing[p] if p else grads
        return pltpu.make_async_copy(source.at[at(k)], back.at[slot, p], back_sem.at[slot, p])

    def share(shift):
        owner = lax.rem(chip - shift + outer, outer)
        rows = pl.ds(pl.multiple_of(owner * 2 * width + cluster * part, part), part)
        mine = pl.ds(pl.multiple_of(cluster * part, part), part)
        return remote(
            weight.at[rows], shares.at[shift, mine], share_send.at[shift], share_recv.at[shift], chip_at(-shift)
        )

    def spread(shift, source, peer):
        rows = pl.ds(pl.multiple_of(source * part, part), part)
        return remote(
            shares.at[shift, rows], shares.at[shift, rows],
            spread_send.at[shift], spread_recv.at[shift], peer, "clu",
        )

    def all_shares(shift):
        rows = pl.ds(0, len(others) * part)
        return remote(
            shares.at[shift, rows], shares.at[shift, rows], spread_send.at[shift], spread_recv.at[shift], others[0], "clu"
        )

    def block(p):
        half = core if p % 2 == 0 else 1 - core
        if p < 2:
            source = weight.at[pl.ds(pl.multiple_of((chip * 2 + half) * width, width), width)]
        else:
            source = shares.at[p // 2, pl.ds(pl.multiple_of(half * width, width), width)]
        if p % 2 == 0:
            return pltpu.make_async_copy(source, blocks_out.at[p], block_recv.at[p])
        return remote(source, blocks_out.at[p], block_send.at[p], block_recv.at[p], sibling)

    for copy in loads(0):
        copy.start()
    fixed = [
        pltpu.make_async_copy(source, target, fixed_sem.at[i])
        for i, (source, target) in enumerate([(segments, seg), (weight, mat), (bias, vec)])
    ]
    for copy in fixed:
        copy.start()
    load_cot(0).start()

    barrier = pltpu.get_barrier_semaphore()
    peers = [("col", sibling)] + [("col", chip_at(shift)) for shift in range(1, outer)]
    peers += [("clu", peer) for peer in others]
    for axis, peer in peers:
        pl.semaphore_signal(barrier, inc=1, device_id={axis: peer}, device_id_type=MESH)
    pl.semaphore_wait(barrier, len(peers))
    for shift in range(1, outer):
        share(shift).start()
    block(0).start()
    block(1).start()
    fixed[0].wait()

    def aggregate_tile(k, carry):
        slot = lax.rem(k, 2)
        for copy in loads(k):
            copy.wait()

        @pl.when(k + 1 < count)
        def _():
            for copy in loads(k + 1):
                copy.start()

        for b in range(tile // BLOCK):
            part = pl.ds(b * BLOCK, BLOCK)
            stencil, inverse = stencil_of(adj[slot, part, :], seg[pl.ds(k * (tile // BLOCK) + b, 1), :])
            summed = jnp.dot(stencil, feat[slot, part, :], preferred_element_type=F32)
            target = pl.ds(pl.multiple_of(k * tile + b * BLOCK, BLOCK), BLOCK)
            sten[target, :] = stencil
            pieces[0][target, :] = (summed * inverse).astype(BF16)
        for shift in range(1, outer):
            hop(2 * shift, k).start()
        hop(1, k).start()
        return carry

    lax.fori_loop(0, count, aggregate_tile, 0)
    total[...] = jnp.zeros_like(total)
    fixed[1].wait()
    fixed[2].wait()
    blocks = [lax.rem(chip + p // 2, outer) * 2 + (core if p % 2 == 0 else 1 - core) for p in range(n)]

    def forward_tile(k):
        slot = lax.rem(k, 2)
        load_cot(k).wait()

        @pl.when(k + 1 < count)
        def _():
            load_cot(k + 1).start()

        several(outer, send_sem.at[0], near_in.at[k]).wait_recv()

        @pl.when(k >= 2)
        def _():
            store_grad(k - 2).wait()
            send_grad(k - 2)

        preact = None
        for p in range(n):
            source = pl.ds(pl.multiple_of(blocks[p] * width, width), width)
            term = jnp.dot(pieces[p][at(k), :], mat[source, :], preferred_element_type=F32)
            preact = term if preact is None else preact + term
        preact = preact + vec[...].astype(F32).reshape(1, width)
        grad_preact = jnp.where(preact > 0.0, cot[slot].astype(F32), 0.0)
        total[pl.ds(depth, 8), :] += jnp.sum(grad_preact.reshape(tile // 8, 8, width), axis=0)
        grad_preact = grad_preact.astype(BF16)
        grad[slot] = grad_preact

        @pl.when(k < count - 1)
        def _():
            store_grad(k).start()

        @pl.when(k == count - 1)
        def _():
            last[0] = grad_preact

        for p in range(n):
            target = pl.ds(pl.multiple_of(blocks[p] * width, width), width)
            total[target, :] += lax.dot_general(
                pieces[p][at(k), :], grad_preact, (((0,), (0,)), ((), ())), preferred_element_type=F32
            )
        activations[at(k), :] = jnp.maximum(preact, 0.0).astype(BF16)

    def step(k, carry):
        @pl.when(k < count)
        def _():
            for shift in range(1, outer):
                hop(2 * shift, k).wait_recv()
                hop(2 * shift + 1, k).start()

        @pl.when(k == 1)
        def _():
            for shift in range(1, outer):
                share(shift).wait_recv()
                for peer in others:
                    spread(shift, cluster, peer).start()

        @pl.when(k == 4)
        def _():
            for shift in range(1, outer):
                all_shares(shift).wait_recv()
                block(2 * shift).start()
                block(2 * shift + 1).start()

        @pl.when(k >= 1)
        def _():
            forward_tile(k - 1)

        return carry

    lax.fori_loop(0, count + 1, step, 0)
    sums = cluster_sum(total, summed_total, half_in, quarter_in, bias_in, sum_sems, clusters)
    sums.start()
    store_grad(count - 2).wait()
    send_grad(count - 2)
    for p in range(1, n):
        if p == 1 or p % 2 == 0:
            last_hop(p).start()
    for p in range(1, n):
        several(count, send_sem.at[p], near_in.at[0]).wait_send()
    for p in range(1, n, 2):
        block(p).wait_send()
    for shift in range(1, outer):
        share(shift).wait_send()
        all_shares(shift).wait_send()
    for p in range(n):
        if p % 2:
            block(p).wait_recv()
        else:
            block(p).wait()
    copies = [
        pltpu.make_async_copy(blocks_out.at[p], mat.at[pl.ds(p * width, width)], block_send.at[p - p % 2])
        for p in range(0, n, 2)
    ] + [
        pltpu.make_async_copy(blocks_out.at[p], mat.at[pl.ds(p * width, width)], block_recv.at[p])
        for p in range(1, n, 2)
    ]
    for copy in copies:
        copy.start()
    for copy in copies:
        copy.wait()

    def backward_tile(k):
        slot = lax.rem(k, 2)
        for p in range(n):
            load_piece(p, k).wait()
        scaled[at(k), :] = back_through(lambda p: back[slot, p], n, mat, sten[at(k), :])

    def moment(r):
        return max(r * 512 // tile, 0)

    def back_step(k, carry):
        @pl.when(k >= 1)
        def _():
            backward_tile(k - 1)

        @pl.when(k < count - 1)
        def _():
            for shift in range(1, outer):
                grad_hop(2 * shift, k).wait_recv()
                grad_hop(2 * shift + 1, k).start()
            several(outer, grad_out.at[0], grad_near.at[k]).wait_recv()
            for p in range(n):
                load_piece(p, k).start()

        for r in range(sums.rounds):
            if moment(r) < count:
                pl.when(k == moment(r))(functools.partial(sums.advance, r))
        if moment(sums.last) < count:
            pl.when(k == moment(sums.last))(sums.finish)
        return carry

    lax.fori_loop(0, count, back_step, 0)
    for r in range(sums.rounds):
        if moment(r) >= count:
            sums.advance(r)
    if moment(sums.last) >= count:
        sums.finish()
    for p in range(2, n, 2):
        last_hop(p).wait_recv()
        last_hop(p + 1).start()
    for p in range(1, n):
        several(count - 1, grad_out.at[p], grad_near.at[0]).wait_send()
        last_hop(p).wait_send()
    several(outer, last_out.at[0], grad_near.at[count - 1]).wait_recv()


def exchange(features, adjacency, cotangent, segments, weight, bias, n, clusters, tile):
    rows, width = features.shape
    depth = weight.shape[0]
    count, outer = rows // tile, n // 2
    parts, high = cluster_sum.PARTS, clusters // 2
    dma = pltpu.SemaphoreType.DMA
    array = jax.ShapeDtypeStruct
    return pl.pallas_call(
        functools.partial(exchange_kernel, n, clusters, tile),
        in_specs=[HBM] * 6,
        out_specs=[VMEM] * 6 + [HBM] * (n + 1),
        out_shape=[
            pltpu.VMEM((rows, width), BF16),
            pltpu.VMEM((rows, width), BF16),
            pltpu.VMEM((depth + 8, width), F32),
            pltpu.VMEM((rows, BLOCK), BF16),
            pltpu.VMEM((depth, width), BF16),
            pltpu.VMEM((n, tile, width), BF16),
            array((n, width, width), BF16),
        ]
        + [array((rows, width), BF16)] * n,
        scratch_shapes=[pltpu.VMEM((rows, width), BF16)] * (n - 2)
        + [
            pltpu.VMEM((2, tile, width), BF16),
            pltpu.VMEM((2, tile, BLOCK), jnp.int32),
            pltpu.VMEM((2, tile, width), BF16),
            pltpu.VMEM((2, tile, width), BF16),
            pltpu.VMEM(segments.shape, jnp.int32),
            pltpu.VMEM((width,), BF16),
            pltpu.VMEM((depth + 8, width), F32),
            pltpu.VMEM((outer, 2 * width, width), BF16),
            pltpu.VMEM((2, n, tile, width), BF16),
            dma((2, 2)),
            dma((2,)),
            dma((2,)),
            dma((3,)),
            dma((n,)),
            dma((outer - 1, count)),
            dma((count,)),
            dma((n,)),
            dma((outer - 1, count)),
            dma((count,)),
            dma((n,)),
            dma((2, n)),
            dma((outer,)),
            dma((outer,)),
            dma((outer,)),
            dma((outer,)),
            dma((n,)),
            dma((n,)),
            pltpu.VMEM((parts, depth // parts // 2, width), F32),
            pltpu.VMEM((parts, high, depth // parts // 2 // high, width), F32),
            pltpu.VMEM((clusters, 8, width), F32),
            [dma((5,)), dma((parts,)), dma((parts,)), dma((parts,)), dma((1,)), dma((1,))],
        ],
        compiler_params=pltpu.CompilerParams(
            collective_id=0, has_side_effects=True, vmem_limit_bytes=38 << 20
        ),
    )(*[pltpu.with_memory_space_constraint(x, pltpu.HBM) for x in (features, adjacency, cotangent, segments, weight, bias)])


def finish_kernel(
    activations, scaled, total, stencil, blocks, last,
    grad_features, out, grad_weight, grad_bias, slots, row, rest, slot_sem, fixed_sem,
):
    rows, width = scaled.shape
    n, tile, _ = last.shape
    depth = total.shape[0] - 8
    span = 2 * tile
    count = rows // span
    row[...] = jnp.sum(total[pl.ds(depth, 8), :], axis=0, keepdims=True)
    fixed = [
        pltpu.make_async_copy(activations, out, fixed_sem.at[0]),
        pltpu.make_async_copy(total.at[pl.ds(0, depth)], grad_weight, fixed_sem.at[1]),
        pltpu.make_async_copy(row, grad_bias, fixed_sem.at[2]),
    ]
    for copy in fixed:
        copy.start()
    rest[...] = back_through(lambda p: last[p], n, blocks, stencil[pl.ds(rows - tile, tile), :])

    def store(k):
        slot = lax.rem(k, SLOTS)
        target = pl.ds(pl.multiple_of(k * span, span), span)
        return pltpu.make_async_copy(slots.at[slot], grad_features.at[target], slot_sem.at[slot])

    def step(k, own):
        slot = lax.rem(k, SLOTS)
        for b in range(span // BLOCK):
            source = pl.ds(pl.multiple_of(k * span + b * BLOCK, BLOCK), BLOCK)
            if b * BLOCK < own:
                value = scaled[source, :]
            else:
                value = rest[pl.ds(b * BLOCK - own, BLOCK), :]
            slots[slot, pl.ds(b * BLOCK, BLOCK), :] = jnp.dot(
                stencil[source, :], value, preferred_element_type=F32
            )
        store(k).start()

    def full(k, carry):
        @pl.when(k >= SLOTS)
        def _():
            store(k - SLOTS).wait()

        step(k, span)
        return carry

    lax.fori_loop(0, count - 1, full, 0)
    if count > SLOTS:
        store(count - 1 - SLOTS).wait()
    step(count - 1, tile)
    for k in range(max(count - SLOTS, 0), count):
        store(k).wait()
    for copy in fixed:
        copy.wait()


def finish(activations, scaled, total, stencil, blocks, last):
    rows, width = scaled.shape
    tile = last.shape[1]
    depth = total.shape[0] - 8
    dma = pltpu.SemaphoreType.DMA
    return pl.pallas_call(
        finish_kernel,
        in_specs=[VMEM] * 6,
        out_specs=[HBM] * 4,
        out_shape=[
            jax.ShapeDtypeStruct((rows, width), F32),
            jax.ShapeDtypeStruct((rows, width), BF16),
            jax.ShapeDtypeStruct((depth, width), F32),
            jax.ShapeDtypeStruct((1, width), F32),
        ],
        scratch_shapes=[
            pltpu.VMEM((SLOTS, 2 * tile, width), F32),
            pltpu.VMEM((1, width), F32),
            pltpu.VMEM((tile, width), BF16),
            dma((SLOTS,)),
            dma((3,)),
        ],
        cost_estimate=pl.CostEstimate(
            flops=2 * rows * BLOCK * width, bytes_accessed=6 * rows * width + 4 * depth * width, transcendentals=0
        ),
        compiler_params=pltpu.CompilerParams(vmem_limit_bytes=12 << 20),
    )(activations, scaled, total, stencil, blocks, last)


def build(n, clusters):
    def local(features, weight, bias, adjacency, segments, cotangent):
        tile = 256 if n <= 4 else 512
        held = exchange(features, adjacency, cotangent, segments, weight, bias, n, clusters, tile)[:6]
        grad_features, out, grad_weight, grad_bias = finish(*held)
        return (out, grad_features, grad_weight, grad_bias.reshape(-1))

    return local


def solution(mesh):
    return jax.shard_map(
        build(mesh.shape["col"], mesh.shape["clu"]),
        mesh=mesh,
        in_specs=(
            P("clu", "col"),
            P(None, "col"),
            P("col"),
            P("clu", None),
            P("clu", None),
            P("clu", "col"),
        ),
        out_specs=(P("clu", "col"), P("clu", "col"), P(None, "col"), P("col")),
        check_vma=False,
    )
```

```python
import functools

import jax
import jax.numpy as jnp
from jax import lax
from jax.experimental import pallas as pl
from jax.experimental.pallas import tpu as pltpu
from jax.sharding import PartitionSpec as P

BLOCK = 128
SLOTS = 4
F32 = jnp.float32
BF16 = jnp.bfloat16
MESH = pl.DeviceIdType.MESH
HBM = pl.BlockSpec(memory_space=pltpu.HBM)
VMEM = pl.BlockSpec(memory_space=pltpu.VMEM)


def stencil_of(adjacency, segment):
    columns = jnp.broadcast_to(segment, (BLOCK, BLOCK))
    links = jnp.where(columns == columns.T, adjacency, 0).astype(F32)
    inverse = 1.0 / (jnp.sum(links, axis=1, keepdims=True) + 1.0)
    row = lax.broadcasted_iota(jnp.int32, (BLOCK, BLOCK), 0)
    column = lax.broadcasted_iota(jnp.int32, (BLOCK, BLOCK), 1)
    return (links + jnp.where(row == column, 2.0, 0.0)).astype(BF16), inverse


def back_through(piece, n, blocks, stencil):
    width = blocks.shape[1]
    value = None
    for p in range(n):
        term = lax.dot_general(
            piece(p), blocks[pl.ds(p * width, width), :], (((1,), (1,)), ((), ())), preferred_element_type=F32
        )
        value = term if value is None else value + term
    inverse = 1.0 / (jnp.sum(stencil.astype(F32), axis=1, keepdims=True) - 1.0)
    return (value.astype(BF16).astype(F32) * inverse).astype(BF16)


class cluster_sum:
    PARTS = 4
    BACK = (5, 7, 8, 9)
    rounds = 10
    last = 12

    def __init__(self, total, result, half_in, quarter_in, bias_in, sems, clusters):
        self.result = result
        self.total, self.half_in, self.quarter_in, self.bias_in, self.sems = total, half_in, quarter_in, bias_in, sems
        self.clusters, self.high = clusters, clusters // 2
        self.depth = total.shape[0] - 8
        self.half = self.depth // self.PARTS // 2
        self.quarter = self.half // self.high
        self.me = lax.axis_index("clu")
        self.z, self.x = self.me // 2, lax.rem(self.me, 2)
        self.others = [lax.rem(self.me + d, clusters) for d in range(1, clusters)]
        self.levels = [lax.rem(self.z + d, self.high) for d in range(1, self.high)]

    def rows_of_half(self, c, x):
        return pl.ds(pl.multiple_of(c * 2 * self.half + x * self.half, self.half), self.half)

    def rows_of_quarter(self, c, q):
        start = c * 2 * self.half + self.x * self.half + q * self.quarter
        return pl.ds(pl.multiple_of(start, self.quarter), self.quarter)

    def copy(self, source, target, kind, recv, device):
        return pltpu.make_async_remote_copy(
            src_ref=source, dst_ref=target, send_sem=self.sems[0].at[kind],
            recv_sem=self.sems[1 + kind].at[recv], device_id={"clu": device}, device_id_type=MESH,
        )

    def several(self, rows, kind, recv=0):
        return self.copy(self.total.at[pl.ds(0, rows)], self.result.at[pl.ds(0, rows)], kind, recv, self.others[0])

    def give_half(self, c):
        rows = self.rows_of_half(c, 1 - self.x)
        return self.copy(self.total.at[rows], self.half_in.at[c], 0, c, self.z * 2 + 1 - self.x)

    def give_quarter(self, c, source, target):
        rows = self.rows_of_quarter(c, target)
        return self.copy(
            self.total.at[rows], self.quarter_in.at[c, source], 1, c, target * 2 + self.x
        )

    def return_quarter(self, c, source, target):
        rows = self.rows_of_quarter(c, source)
        return self.copy(
            self.result.at[rows], self.result.at[rows], 2, c, target * 2 + self.x
        )

    def return_half(self, c, x):
        rows = self.rows_of_half(c, x)
        return self.copy(self.result.at[rows], self.result.at[rows], 3, 0, self.z * 2 + 1 - self.x)

    def give_bias(self, source, target):
        return self.copy(
            self.total.at[pl.ds(self.depth, 8)], self.bias_in.at[source], 4, 0, target
        )

    def start(self):
        for c in range(self.PARTS):
            self.give_half(c).start()
        for other in self.others:
            self.give_bias(self.me, other).start()

    def advance(self, k):
        total = self.total
        if k < self.PARTS:
            self.give_half(k).wait_recv()
            total[self.rows_of_half(k, self.x), :] += self.half_in[k]
            for level in self.levels:
                self.give_quarter(k, self.z, level).start()
        c = k - 2
        if 0 <= c < self.PARTS:
            rows = self.rows_of_quarter(c, self.z)
            self.several(len(self.levels) * self.quarter, 1, c).wait_recv()
            value = total[rows, :]
            for level in self.levels:
                value = value + self.quarter_in[c, level]
            self.result[rows, :] = value
            for level in self.levels:
                self.return_quarter(c, self.z, level).start()
        if k in self.BACK:
            c = self.BACK.index(k)
            self.several(len(self.levels) * self.quarter, 2, c).wait_recv()
            self.return_half(c, self.x).start()

    def finish(self):
        halves = self.PARTS * self.half
        quarters = self.PARTS * len(self.levels) * self.quarter
        for kind, rows in enumerate((halves, quarters, quarters, halves, 8 * len(self.others))):
            self.several(rows, kind).wait_send()
        self.several(halves, 3).wait_recv()
        self.several(8 * len(self.others), 4).wait_recv()
        value = self.total[pl.ds(self.depth, 8), :]
        for other in self.others:
            value = value + self.bias_in[other]
        self.result[pl.ds(self.depth, 8), :] = value


def exchange_kernel(
    n, clusters, tile, features, adjacency, cotangent, segments, weight, bias,
    activations, scaled, summed_total, sten, mat, last, blocks_out, grads, *rest,
):
    landing = (None,) + rest[: n - 1]
    pieces = list(rest[n - 1 : 2 * n - 3])
    pieces = pieces[:1] + [activations] + pieces[1:] + [scaled]
    (feat, adj, cot, grad, seg, vec, total, shares, back, load_sem, cot_sem, grad_sem,
     fixed_sem, send_sem, far_in, near_in, grad_out, grad_far, grad_near, last_out, back_sem, share_send, share_recv, spread_send, spread_recv,
     block_send, block_recv, half_in, quarter_in, bias_in, sum_sems) = rest[2 * n - 3 :]
    outer = n // 2
    rows, width = features.shape
    depth = mat.shape[0]
    count = rows // tile
    me, cluster = lax.axis_index("col"), lax.axis_index("clu")
    chip, core = me // 2, lax.rem(me, 2)
    sibling = chip * 2 + 1 - core
    part = 2 * width // clusters
    others = [lax.rem(cluster + d, clusters) for d in range(1, clusters)]

    def chip_at(shift):
        return lax.rem(chip + shift + outer, outer) * 2 + core

    def at(k):
        return pl.ds(pl.multiple_of(k * tile, tile), tile)

    def loads(k):
        slot = lax.rem(k, 2)
        return (
            pltpu.make_async_copy(features.at[at(k)], feat.at[slot], load_sem.at[0, slot]),
            pltpu.make_async_copy(adjacency.at[at(k)], adj.at[slot], load_sem.at[1, slot]),
        )

    def load_cot(k):
        slot = lax.rem(k, 2)
        return pltpu.make_async_copy(cotangent.at[at(k)], cot.at[slot], cot_sem.at[slot])

    def store_grad(k):
        slot = lax.rem(k, 2)
        return pltpu.make_async_copy(grad.at[slot], grads.at[at(k)], grad_sem.at[slot])

    def remote(source, target, send, recv, device, axis="col"):
        return pltpu.make_async_remote_copy(
            src_ref=source, dst_ref=target, send_sem=send, recv_sem=recv,
            device_id={axis: device}, device_id_type=MESH,
        )

    def hop(p, k):
        source = 0 if p % 2 == 0 else p - 1
        device = chip_at(-(p // 2)) if p % 2 == 0 else sibling
        arrival = far_in.at[p // 2 - 1, k] if p % 2 == 0 else near_in.at[k]
        return remote(pieces[source].at[at(k)], pieces[p].at[at(k)], send_sem.at[p], arrival, device)

    def grad_hop(p, k):
        source = grads if p < 2 or p % 2 == 0 else landing[p - 1]
        device = chip_at(-(p // 2)) if p % 2 == 0 else sibling
        arrival = grad_far.at[p // 2 - 1, k] if p % 2 == 0 else grad_near.at[k]
        return remote(source.at[at(k)], landing[p].at[at(k)], grad_out.at[p], arrival, device)

    def several(tiles, send, arrival):
        span = pl.ds(0, tiles * tile)
        return remote(grads.at[span], landing[1].at[span], send, arrival, sibling)

    def last_hop(p):
        device = chip_at(-(p // 2)) if p % 2 == 0 else sibling
        source = last.at[0 if p % 2 == 0 else p - 1]
        arrival = grad_far.at[p // 2 - 1, count - 1] if p % 2 == 0 else grad_near.at[count - 1]
        return remote(source, last.at[p], last_out.at[p], arrival, device)

    def send_grad(k):
        for shift in range(1, outer):
            grad_hop(2 * shift, k).start()
        grad_hop(1, k).start()

    def load_piece(p, k):
        slot = lax.rem(k, 2)
        source = landing[p] if p else grads
        return pltpu.make_async_copy(source.at[at(k)], back.at[slot, p], back_sem.at[slot, p])

    def share(shift):
        owner = lax.rem(chip - shift + outer, outer)
        rows = pl.ds(pl.multiple_of(owner * 2 * width + cluster * part, part), part)
        mine = pl.ds(pl.multiple_of(cluster * part, part), part)
        return remote(
            weight.at[rows], shares.at[shift, mine], share_send.at[shift], share_recv.at[shift], chip_at(-shift)
        )

    def spread(shift, source, peer):
        rows = pl.ds(pl.multiple_of(source * part, part), part)
        return remote(
            shares.at[shift, rows], shares.at[shift, rows],
            spread_send.at[shift], spread_recv.at[shift], peer, "clu",
        )

    def all_shares(shift):
        rows = pl.ds(0, len(others) * part)
        return remote(
            shares.at[shift, rows], shares.at[shift, rows], spread_send.at[shift], spread_recv.at[shift], others[0], "clu"
        )

    def block(p):
        half = core if p % 2 == 0 else 1 - core
        if p < 2:
            source = weight.at[pl.ds(pl.multiple_of((chip * 2 + half) * width, width), width)]
        else:
            source = shares.at[p // 2, pl.ds(pl.multiple_of(half * width, width), width)]
        if p % 2 == 0:
            return pltpu.make_async_copy(source, blocks_out.at[p], block_recv.at[p])
        return remote(source, blocks_out.at[p], block_send.at[p], block_recv.at[p], sibling)

    for copy in loads(0):
        copy.start()
    fixed = [
        pltpu.make_async_copy(source, target, fixed_sem.at[i])
        for i, (source, target) in enumerate([(segments, seg), (weight, mat), (bias, vec)])
    ]
    for copy in fixed:
        copy.start()
    load_cot(0).start()

    barrier = pltpu.get_barrier_semaphore()
    centre = core * (clusters - 1)
    neighbours = [sibling] + [chip_at(shift) for shift in range(1, outer)]

    def greet(axis, peer):
        pl.semaphore_signal(barrier, inc=1, device_id={axis: peer}, device_id_type=MESH)

    for peer in neighbours:
        greet("col", peer)

    @pl.when(cluster == centre)
    def _():
        pl.semaphore_wait(barrier, len(neighbours) + len(others))
        for peer in others:
            greet("clu", peer)

    @pl.when(cluster != centre)
    def _():
        pl.semaphore_wait(barrier, len(neighbours))
        greet("clu", centre)

    for shift in range(1, outer):
        share(shift).start()
    block(0).start()
    block(1).start()
    fixed[0].wait()

    def aggregate_tile(k, carry):
        slot = lax.rem(k, 2)
        for copy in loads(k):
            copy.wait()

        @pl.when(k + 1 < count)
        def _():
            for copy in loads(k + 1):
                copy.start()

        for b in range(tile // BLOCK):
            part = pl.ds(b * BLOCK, BLOCK)
            stencil, inverse = stencil_of(adj[slot, part, :], seg[pl.ds(k * (tile // BLOCK) + b, 1), :])
            summed = jnp.dot(stencil, feat[slot, part, :], preferred_element_type=F32)
            target = pl.ds(pl.multiple_of(k * tile + b * BLOCK, BLOCK), BLOCK)
            sten[target, :] = stencil
            pieces[0][target, :] = (summed * inverse).astype(BF16)
        for shift in range(1, outer):
            hop(2 * shift, k).start()
        hop(1, k).start()
        return carry

    lax.fori_loop(0, count, aggregate_tile, 0)
    total[...] = jnp.zeros_like(total)
    fixed[1].wait()
    fixed[2].wait()
    blocks = [lax.rem(chip + p // 2, outer) * 2 + (core if p % 2 == 0 else 1 - core) for p in range(n)]

    def forward_tile(k):
        slot = lax.rem(k, 2)
        load_cot(k).wait()

        @pl.when(k + 1 < count)
        def _():
            load_cot(k + 1).start()

        several(outer, send_sem.at[0], near_in.at[k]).wait_recv()

        @pl.when(k >= 2)
        def _():
            store_grad(k - 2).wait()
            send_grad(k - 2)

        preact = None
        for p in range(n):
            source = pl.ds(pl.multiple_of(blocks[p] * width, width), width)
            term = jnp.dot(pieces[p][at(k), :], mat[source, :], preferred_element_type=F32)
            preact = term if preact is None else preact + term
        preact = preact + vec[...].astype(F32).reshape(1, width)
        grad_preact = jnp.where(preact > 0.0, cot[slot].astype(F32), 0.0)
        total[pl.ds(depth, 8), :] += jnp.sum(grad_preact.reshape(tile // 8, 8, width), axis=0)
        grad_preact = grad_preact.astype(BF16)
        grad[slot] = grad_preact

        @pl.when(k < count - 1)
        def _():
            store_grad(k).start()

        @pl.when(k == count - 1)
        def _():
            last[0] = grad_preact

        for p in range(n):
            target = pl.ds(pl.multiple_of(blocks[p] * width, width), width)
            total[target, :] += lax.dot_general(
                pieces[p][at(k), :], grad_preact, (((0,), (0,)), ((), ())), preferred_element_type=F32
            )
        activations[at(k), :] = jnp.maximum(preact, 0.0).astype(BF16)

    def step(k, carry):
        @pl.when(k < count)
        def _():
            for shift in range(1, outer):
                hop(2 * shift, k).wait_recv()
                hop(2 * shift + 1, k).start()

        @pl.when((k == 2) & (cluster != centre))
        def _():
            pl.semaphore_wait(barrier, 1)

        @pl.when(k == 2)
        def _():
            for shift in range(1, outer):
                share(shift).wait_recv()
                for peer in others:
                    spread(shift, cluster, peer).start()

        @pl.when(k == 6)
        def _():
            for shift in range(1, outer):
                all_shares(shift).wait_recv()
                block(2 * shift).start()
                block(2 * shift + 1).start()

        @pl.when(k >= 1)
        def _():
            forward_tile(k - 1)

        return carry

    lax.fori_loop(0, count + 1, step, 0)
    sums = cluster_sum(total, summed_total, half_in, quarter_in, bias_in, sum_sems, clusters)
    sums.start()
    store_grad(count - 2).wait()
    send_grad(count - 2)
    for p in range(1, n):
        if p == 1 or p % 2 == 0:
            last_hop(p).start()
    for p in range(1, n):
        several(count, send_sem.at[p], near_in.at[0]).wait_send()
    for p in range(1, n, 2):
        block(p).wait_send()
    for shift in range(1, outer):
        share(shift).wait_send()
        all_shares(shift).wait_send()
    for p in range(n):
        if p % 2:
            block(p).wait_recv()
        else:
            block(p).wait()
    copies = [
        pltpu.make_async_copy(blocks_out.at[p], mat.at[pl.ds(p * width, width)], block_send.at[p - p % 2])
        for p in range(0, n, 2)
    ] + [
        pltpu.make_async_copy(blocks_out.at[p], mat.at[pl.ds(p * width, width)], block_recv.at[p])
        for p in range(1, n, 2)
    ]
    for copy in copies:
        copy.start()
    for copy in copies:
        copy.wait()

    def backward_tile(k):
        slot = lax.rem(k, 2)
        for p in range(n):
            load_piece(p, k).wait()
        scaled[at(k), :] = back_through(lambda p: back[slot, p], n, mat, sten[at(k), :])

    def moment(r):
        return max(r * 512 // tile, 0)

    def back_step(k, carry):
        @pl.when(k >= 1)
        def _():
            backward_tile(k - 1)

        @pl.when(k < count - 1)
        def _():
            for shift in range(1, outer):
                grad_hop(2 * shift, k).wait_recv()
                grad_hop(2 * shift + 1, k).start()
            several(outer, grad_out.at[0], grad_near.at[k]).wait_recv()
            for p in range(n):
                load_piece(p, k).start()

        for r in range(sums.rounds):
            if moment(r) < count:
                pl.when(k == moment(r))(functools.partial(sums.advance, r))
        if moment(sums.last) < count:
            pl.when(k == moment(sums.last))(sums.finish)
        return carry

    lax.fori_loop(0, count, back_step, 0)
    for r in range(sums.rounds):
        if moment(r) >= count:
            sums.advance(r)
    if moment(sums.last) >= count:
        sums.finish()
    for p in range(2, n, 2):
        last_hop(p).wait_recv()
        last_hop(p + 1).start()
    for p in range(1, n):
        several(count - 1, grad_out.at[p], grad_near.at[0]).wait_send()
        last_hop(p).wait_send()
    several(outer, last_out.at[0], grad_near.at[count - 1]).wait_recv()


def exchange(features, adjacency, cotangent, segments, weight, bias, n, clusters, tile):
    rows, width = features.shape
    depth = weight.shape[0]
    count, outer = rows // tile, n // 2
    parts, high = cluster_sum.PARTS, clusters // 2
    dma = pltpu.SemaphoreType.DMA
    array = jax.ShapeDtypeStruct
    return pl.pallas_call(
        functools.partial(exchange_kernel, n, clusters, tile),
        in_specs=[HBM] * 6,
        out_specs=[VMEM] * 6 + [HBM] * (n + 1),
        out_shape=[
            pltpu.VMEM((rows, width), BF16),
            pltpu.VMEM((rows, width), BF16),
            pltpu.VMEM((depth + 8, width), F32),
            pltpu.VMEM((rows, BLOCK), BF16),
            pltpu.VMEM((depth, width), BF16),
            pltpu.VMEM((n, tile, width), BF16),
            array((n, width, width), BF16),
        ]
        + [array((rows, width), BF16)] * n,
        scratch_shapes=[pltpu.VMEM((rows, width), BF16)] * (n - 2)
        + [
            pltpu.VMEM((2, tile, width), BF16),
            pltpu.VMEM((2, tile, BLOCK), jnp.int32),
            pltpu.VMEM((2, tile, width), BF16),
            pltpu.VMEM((2, tile, width), BF16),
            pltpu.VMEM(segments.shape, jnp.int32),
            pltpu.VMEM((width,), BF16),
            pltpu.VMEM((depth + 8, width), F32),
            pltpu.VMEM((outer, 2 * width, width), BF16),
            pltpu.VMEM((2, n, tile, width), BF16),
            dma((2, 2)),
            dma((2,)),
            dma((2,)),
            dma((3,)),
            dma((n,)),
            dma((outer - 1, count)),
            dma((count,)),
            dma((n,)),
            dma((outer - 1, count)),
            dma((count,)),
            dma((n,)),
            dma((2, n)),
            dma((outer,)),
            dma((outer,)),
            dma((outer,)),
            dma((outer,)),
            dma((n,)),
            dma((n,)),
            pltpu.VMEM((parts, depth // parts // 2, width), F32),
            pltpu.VMEM((parts, high, depth // parts // 2 // high, width), F32),
            pltpu.VMEM((clusters, 8, width), F32),
            [dma((5,)), dma((parts,)), dma((parts,)), dma((parts,)), dma((1,)), dma((1,))],
        ],
        compiler_params=pltpu.CompilerParams(
            collective_id=0, has_side_effects=True, vmem_limit_bytes=38 << 20
        ),
    )(*[pltpu.with_memory_space_constraint(x, pltpu.HBM) for x in (features, adjacency, cotangent, segments, weight, bias)])


def finish_kernel(
    activations, scaled, total, stencil, blocks, last,
    grad_features, out, grad_weight, grad_bias, slots, row, rest, slot_sem, fixed_sem,
):
    rows, width = scaled.shape
    n, tile, _ = last.shape
    depth = total.shape[0] - 8
    span = 2 * tile
    count = rows // span
    row[...] = jnp.sum(total[pl.ds(depth, 8), :], axis=0, keepdims=True)
    fixed = [
        pltpu.make_async_copy(activations, out, fixed_sem.at[0]),
        pltpu.make_async_copy(total.at[pl.ds(0, depth)], grad_weight, fixed_sem.at[1]),
        pltpu.make_async_copy(row, grad_bias, fixed_sem.at[2]),
    ]
    for copy in fixed:
        copy.start()
    rest[...] = back_through(lambda p: last[p], n, blocks, stencil[pl.ds(rows - tile, tile), :])

    def store(k):
        slot = lax.rem(k, SLOTS)
        target = pl.ds(pl.multiple_of(k * span, span), span)
        return pltpu.make_async_copy(slots.at[slot], grad_features.at[target], slot_sem.at[slot])

    def step(k, own):
        slot = lax.rem(k, SLOTS)
        for b in range(span // BLOCK):
            source = pl.ds(pl.multiple_of(k * span + b * BLOCK, BLOCK), BLOCK)
            if b * BLOCK < own:
                value = scaled[source, :]
            else:
                value = rest[pl.ds(b * BLOCK - own, BLOCK), :]
            slots[slot, pl.ds(b * BLOCK, BLOCK), :] = jnp.dot(
                stencil[source, :], value, preferred_element_type=F32
            )
        store(k).start()

    def full(k, carry):
        @pl.when(k >= SLOTS)
        def _():
            store(k - SLOTS).wait()

        step(k, span)
        return carry

    lax.fori_loop(0, count - 1, full, 0)
    if count > SLOTS:
        store(count - 1 - SLOTS).wait()
    step(count - 1, tile)
    for k in range(max(count - SLOTS, 0), count):
        store(k).wait()
    for copy in fixed:
        copy.wait()


def finish(activations, scaled, total, stencil, blocks, last):
    rows, width = scaled.shape
    tile = last.shape[1]
    depth = total.shape[0] - 8
    dma = pltpu.SemaphoreType.DMA
    return pl.pallas_call(
        finish_kernel,
        in_specs=[VMEM] * 6,
        out_specs=[HBM] * 4,
        out_shape=[
            jax.ShapeDtypeStruct((rows, width), F32),
            jax.ShapeDtypeStruct((rows, width), BF16),
            jax.ShapeDtypeStruct((depth, width), F32),
            jax.ShapeDtypeStruct((1, width), F32),
        ],
        scratch_shapes=[
            pltpu.VMEM((SLOTS, 2 * tile, width), F32),
            pltpu.VMEM((1, width), F32),
            pltpu.VMEM((tile, width), BF16),
            dma((SLOTS,)),
            dma((3,)),
        ],
        cost_estimate=pl.CostEstimate(
            flops=2 * rows * BLOCK * width, bytes_accessed=6 * rows * width + 4 * depth * width, transcendentals=0
        ),
        compiler_params=pltpu.CompilerParams(vmem_limit_bytes=12 << 20),
    )(activations, scaled, total, stencil, blocks, last)


def build(n, clusters):
    def local(features, weight, bias, adjacency, segments, cotangent):
        tile = 256 if n <= 4 else 512
        held = exchange(features, adjacency, cotangent, segments, weight, bias, n, clusters, tile)[:6]
        grad_features, out, grad_weight, grad_bias = finish(*held)
        return (out, grad_features, grad_weight, grad_bias.reshape(-1))

    return local


def solution(mesh):
    return jax.shard_map(
        build(mesh.shape["col"], mesh.shape["clu"]),
        mesh=mesh,
        in_specs=(
            P("clu", "col"),
            P(None, "col"),
            P("col"),
            P("clu", None),
            P("clu", None),
            P("clu", "col"),
        ),
        out_specs=(P("clu", "col"), P("clu", "col"), P(None, "col"), P("col")),
        check_vma=False,
    )
```

```python
import functools

import jax
import jax.numpy as jnp
from jax import lax
from jax.experimental import pallas as pl
from jax.experimental.pallas import tpu as pltpu
from jax.sharding import PartitionSpec as P

BLOCK = 128
SLOTS = 4
F32 = jnp.float32
BF16 = jnp.bfloat16
MESH = pl.DeviceIdType.MESH
HBM = pl.BlockSpec(memory_space=pltpu.HBM)
VMEM = pl.BlockSpec(memory_space=pltpu.VMEM)


def stencil_of(adjacency, segment):
    columns = jnp.broadcast_to(segment, (BLOCK, BLOCK))
    links = jnp.where(columns == columns.T, adjacency, 0).astype(F32)
    inverse = 1.0 / (jnp.sum(links, axis=1, keepdims=True) + 1.0)
    row = lax.broadcasted_iota(jnp.int32, (BLOCK, BLOCK), 0)
    column = lax.broadcasted_iota(jnp.int32, (BLOCK, BLOCK), 1)
    return (links + jnp.where(row == column, 2.0, 0.0)).astype(BF16), inverse


def back_through(piece, n, blocks, stencil):
    width = blocks.shape[1]
    value = None
    for p in range(n):
        term = lax.dot_general(
            piece(p), blocks[pl.ds(p * width, width), :], (((1,), (1,)), ((), ())), preferred_element_type=F32
        )
        value = term if value is None else value + term
    inverse = 1.0 / (jnp.sum(stencil.astype(F32), axis=1, keepdims=True) - 1.0)
    return (value.astype(BF16).astype(F32) * inverse).astype(BF16)


class cluster_sum:
    PARTS = 4
    BACK = (5, 7, 8, 9)
    rounds = 10
    last = 12

    def __init__(self, total, result, half_in, quarter_in, bias_in, sems, clusters):
        self.result = result
        self.total, self.half_in, self.quarter_in, self.bias_in, self.sems = total, half_in, quarter_in, bias_in, sems
        self.clusters, self.high = clusters, clusters // 2
        self.depth = total.shape[0] - 8
        self.half = self.depth // self.PARTS // 2
        self.quarter = self.half // self.high
        self.me = lax.axis_index("clu")
        self.z, self.x = self.me // 2, lax.rem(self.me, 2)
        self.others = [lax.rem(self.me + d, clusters) for d in range(1, clusters)]
        self.levels = [lax.rem(self.z + d, self.high) for d in range(1, self.high)]

    def rows_of_half(self, c, x):
        return pl.ds(pl.multiple_of(c * 2 * self.half + x * self.half, self.half), self.half)

    def rows_of_quarter(self, c, q):
        start = c * 2 * self.half + self.x * self.half + q * self.quarter
        return pl.ds(pl.multiple_of(start, self.quarter), self.quarter)

    def copy(self, source, target, kind, recv, device):
        return pltpu.make_async_remote_copy(
            src_ref=source, dst_ref=target, send_sem=self.sems[0].at[kind],
            recv_sem=self.sems[1 + kind].at[recv], device_id={"clu": device}, device_id_type=MESH,
        )

    def several(self, rows, kind, recv=0):
        return self.copy(self.total.at[pl.ds(0, rows)], self.result.at[pl.ds(0, rows)], kind, recv, self.others[0])

    def give_half(self, c):
        rows = self.rows_of_half(c, 1 - self.x)
        return self.copy(self.total.at[rows], self.half_in.at[c], 0, c, self.z * 2 + 1 - self.x)

    def give_quarter(self, c, source, target):
        rows = self.rows_of_quarter(c, target)
        return self.copy(
            self.total.at[rows], self.quarter_in.at[c, source], 1, c, target * 2 + self.x
        )

    def return_quarter(self, c, source, target):
        rows = self.rows_of_quarter(c, source)
        return self.copy(
            self.result.at[rows], self.result.at[rows], 2, c, target * 2 + self.x
        )

    def return_half(self, c, x):
        rows = self.rows_of_half(c, x)
        return self.copy(self.result.at[rows], self.result.at[rows], 3, 0, self.z * 2 + 1 - self.x)

    def give_bias(self, source, target):
        return self.copy(
            self.total.at[pl.ds(self.depth, 8)], self.bias_in.at[source], 4, 0, target
        )

    def start(self):
        for c in range(self.PARTS):
            self.give_half(c).start()
        for other in self.others:
            self.give_bias(self.me, other).start()

    def advance(self, k):
        total = self.total
        if k < self.PARTS:
            self.give_half(k).wait_recv()
            total[self.rows_of_half(k, self.x), :] += self.half_in[k]
            for level in self.levels:
                self.give_quarter(k, self.z, level).start()
        c = k - 2
        if 0 <= c < self.PARTS:
            rows = self.rows_of_quarter(c, self.z)
            self.several(len(self.levels) * self.quarter, 1, c).wait_recv()
            value = total[rows, :]
            for level in self.levels:
                value = value + self.quarter_in[c, level]
            self.result[rows, :] = value
            for level in self.levels:
                self.return_quarter(c, self.z, level).start()
        if k in self.BACK:
            c = self.BACK.index(k)
            self.several(len(self.levels) * self.quarter, 2, c).wait_recv()
            self.return_half(c, self.x).start()

    def finish(self):
        halves = self.PARTS * self.half
        quarters = self.PARTS * len(self.levels) * self.quarter
        for kind, rows in enumerate((halves, quarters, quarters, halves, 8 * len(self.others))):
            self.several(rows, kind).wait_send()
        self.several(halves, 3).wait_recv()
        self.several(8 * len(self.others), 4).wait_recv()
        value = self.total[pl.ds(self.depth, 8), :]
        for other in self.others:
            value = value + self.bias_in[other]
        self.result[pl.ds(self.depth, 8), :] = value


def exchange_kernel(
    n, clusters, tile, features, adjacency, cotangent, segments, weight, bias,
    activations, scaled, summed_total, sten, mat, last, blocks_out, grads, *rest,
):
    landing = (None,) + rest[: n - 1]
    pieces = list(rest[n - 1 : 2 * n - 3])
    pieces = pieces[:1] + [activations] + pieces[1:] + [scaled]
    (feat, adj, cot, grad, seg, vec, total, shares, back, load_sem, cot_sem, grad_sem,
     fixed_sem, send_sem, far_in, near_in, grad_out, grad_far, grad_near, last_out, back_sem, share_send, share_recv, spread_send, spread_recv,
     block_send, block_recv, half_in, quarter_in, bias_in, sum_sems) = rest[2 * n - 3 :]
    outer = n // 2
    rows, width = features.shape
    depth = mat.shape[0]
    count = rows // tile
    me, cluster = lax.axis_index("col"), lax.axis_index("clu")
    chip, core = me // 2, lax.rem(me, 2)
    sibling = chip * 2 + 1 - core
    part = 2 * width // clusters
    others = [lax.rem(cluster + d, clusters) for d in range(1, clusters)]

    def chip_at(shift):
        return lax.rem(chip + shift + outer, outer) * 2 + core

    def at(k):
        return pl.ds(pl.multiple_of(k * tile, tile), tile)

    def pair(c):
        return pl.ds(pl.multiple_of(c * 2 * tile, 2 * tile), 2 * tile)

    def loads(k):
        slot = lax.rem(k, 2)
        return (
            pltpu.make_async_copy(features.at[at(k)], feat.at[slot], load_sem.at[0, slot]),
            pltpu.make_async_copy(adjacency.at[at(k)], adj.at[slot], load_sem.at[1, slot]),
        )

    def load_cot(k):
        slot = lax.rem(k, 2)
        return pltpu.make_async_copy(cotangent.at[at(k)], cot.at[slot], cot_sem.at[slot])

    def store_grad(k):
        slot = lax.rem(k, 2)
        return pltpu.make_async_copy(grad.at[slot], grads.at[at(k)], grad_sem.at[slot])

    def remote(source, target, send, recv, device, axis="col"):
        return pltpu.make_async_remote_copy(
            src_ref=source, dst_ref=target, send_sem=send, recv_sem=recv,
            device_id={axis: device}, device_id_type=MESH,
        )

    def hop(p, c):
        source = 0 if p % 2 == 0 else p - 1
        device = chip_at(-(p // 2)) if p % 2 == 0 else sibling
        arrival = far_in.at[p // 2 - 1, c] if p % 2 == 0 else near_in.at[c]
        return remote(pieces[source].at[pair(c)], pieces[p].at[pair(c)], send_sem.at[p], arrival, device)

    def grad_hop(p, c, rows):
        source = grads if p < 2 or p % 2 == 0 else landing[p - 1]
        device = chip_at(-(p // 2)) if p % 2 == 0 else sibling
        arrival = grad_far.at[p // 2 - 1, c] if p % 2 == 0 else grad_near.at[c]
        return remote(source.at[rows], landing[p].at[rows], grad_out.at[p], arrival, device)

    def several(tiles, send, arrival):
        span = pl.ds(0, tiles * tile)
        return remote(grads.at[span], landing[1].at[span], send, arrival, sibling)

    def last_hop(p):
        device = chip_at(-(p // 2)) if p % 2 == 0 else sibling
        source = last.at[0 if p % 2 == 0 else p - 1]
        arrival = grad_far.at[p // 2 - 1, count // 2] if p % 2 == 0 else grad_near.at[count // 2]
        return remote(source, last.at[p], last_out.at[p], arrival, device)

    def send_grad(c, rows):
        for shift in range(1, outer):
            grad_hop(2 * shift, c, rows).start()
        grad_hop(1, c, rows).start()

    def pass_grad(c, rows, tiles):
        for shift in range(1, outer):
            grad_hop(2 * shift, c, rows).wait_recv()
            grad_hop(2 * shift + 1, c, rows).start()
        several(tiles * outer, grad_out.at[0], grad_near.at[c]).wait_recv()

    def load_piece(p, k):
        slot = lax.rem(k, 2)
        source = landing[p] if p else grads
        return pltpu.make_async_copy(source.at[at(k)], back.at[slot, p], back_sem.at[slot, p])

    def share(shift):
        owner = lax.rem(chip - shift + outer, outer)
        rows = pl.ds(pl.multiple_of(owner * 2 * width + cluster * part, part), part)
        mine = pl.ds(pl.multiple_of(cluster * part, part), part)
        return remote(
            weight.at[rows], shares.at[shift, mine], share_send.at[shift], share_recv.at[shift], chip_at(-shift)
        )

    def spread(shift, source, peer):
        rows = pl.ds(pl.multiple_of(source * part, part), part)
        return remote(
            shares.at[shift, rows], shares.at[shift, rows],
            spread_send.at[shift], spread_recv.at[shift], peer, "clu",
        )

    def all_shares(shift):
        rows = pl.ds(0, len(others) * part)
        return remote(
            shares.at[shift, rows], shares.at[shift, rows], spread_send.at[shift], spread_recv.at[shift], others[0], "clu"
        )

    def block(p):
        half = core if p % 2 == 0 else 1 - core
        if p < 2:
            source = weight.at[pl.ds(pl.multiple_of((chip * 2 + half) * width, width), width)]
        else:
            source = shares.at[p // 2, pl.ds(pl.multiple_of(half * width, width), width)]
        if p % 2 == 0:
            return pltpu.make_async_copy(source, blocks_out.at[p], block_recv.at[p])
        return remote(source, blocks_out.at[p], block_send.at[p], block_recv.at[p], sibling)

    for copy in loads(0):
        copy.start()
    fixed = [
        pltpu.make_async_copy(source, target, fixed_sem.at[i])
        for i, (source, target) in enumerate([(segments, seg), (weight, mat), (bias, vec)])
    ]
    for copy in fixed:
        copy.start()
    load_cot(0).start()

    barrier = pltpu.get_barrier_semaphore()
    centre = clusters - 2 + core
    neighbours = [sibling] + [chip_at(shift) for shift in range(1, outer)]

    def greet(axis, peer):
        pl.semaphore_signal(barrier, inc=1, device_id={axis: peer}, device_id_type=MESH)

    for peer in neighbours:
        greet("col", peer)

    @pl.when(cluster == centre)
    def _():
        pl.semaphore_wait(barrier, len(neighbours) + len(others))
        for peer in others:
            greet("clu", peer)

    @pl.when(cluster != centre)
    def _():
        pl.semaphore_wait(barrier, len(neighbours))
        greet("clu", centre)

    for shift in range(1, outer):
        share(shift).start()
    block(0).start()
    block(1).start()
    fixed[0].wait()

    def aggregate_tile(k, carry):
        slot = lax.rem(k, 2)
        for copy in loads(k):
            copy.wait()

        @pl.when(k + 1 < count)
        def _():
            for copy in loads(k + 1):
                copy.start()

        for b in range(tile // BLOCK):
            part = pl.ds(b * BLOCK, BLOCK)
            stencil, inverse = stencil_of(adj[slot, part, :], seg[pl.ds(k * (tile // BLOCK) + b, 1), :])
            summed = jnp.dot(stencil, feat[slot, part, :], preferred_element_type=F32)
            target = pl.ds(pl.multiple_of(k * tile + b * BLOCK, BLOCK), BLOCK)
            sten[target, :] = stencil
            pieces[0][target, :] = (summed * inverse).astype(BF16)

        @pl.when(lax.rem(k, 2) == 1)
        def _():
            for shift in range(1, outer):
                hop(2 * shift, k // 2).start()
            hop(1, k // 2).start()

        return carry

    lax.fori_loop(0, count, aggregate_tile, 0)
    total[...] = jnp.zeros_like(total)
    fixed[1].wait()
    fixed[2].wait()
    blocks = [lax.rem(chip + p // 2, outer) * 2 + (core if p % 2 == 0 else 1 - core) for p in range(n)]

    def forward_tile(k):
        slot = lax.rem(k, 2)
        load_cot(k).wait()

        @pl.when(k + 1 < count)
        def _():
            load_cot(k + 1).start()

        @pl.when(lax.rem(k, 2) == 0)
        def _():
            several(2 * outer, send_sem.at[0], near_in.at[k // 2]).wait_recv()


        @pl.when(k >= 2)
        def _():
            store_grad(k - 2).wait()

        @pl.when((k >= 3) & (lax.rem(k, 2) == 1))
        def _():
            send_grad((k - 3) // 2, pair((k - 3) // 2))

        preact = None
        for p in range(n):
            source = pl.ds(pl.multiple_of(blocks[p] * width, width), width)
            term = jnp.dot(pieces[p][at(k), :], mat[source, :], preferred_element_type=F32)
            preact = term if preact is None else preact + term
        preact = preact + vec[...].astype(F32).reshape(1, width)
        grad_preact = jnp.where(preact > 0.0, cot[slot].astype(F32), 0.0)
        total[pl.ds(depth, 8), :] += jnp.sum(grad_preact.reshape(tile // 8, 8, width), axis=0)
        grad_preact = grad_preact.astype(BF16)
        grad[slot] = grad_preact

        @pl.when(k < count - 1)
        def _():
            store_grad(k).start()

        @pl.when(k == count - 1)
        def _():
            last[0] = grad_preact

        for p in range(n):
            target = pl.ds(pl.multiple_of(blocks[p] * width, width), width)
            total[target, :] += lax.dot_general(
                pieces[p][at(k), :], grad_preact, (((0,), (0,)), ((), ())), preferred_element_type=F32
            )
        activations[at(k), :] = jnp.maximum(preact, 0.0).astype(BF16)

    def step(k, carry):
        @pl.when((k < count) & (lax.rem(k, 2) == 0))
        def _():
            for shift in range(1, outer):
                hop(2 * shift, k // 2).wait_recv()
                hop(2 * shift + 1, k // 2).start()

        @pl.when((k == 2) & (cluster != centre))
        def _():
            pl.semaphore_wait(barrier, 1)

        @pl.when(k == 2)
        def _():
            for shift in range(1, outer):
                share(shift).wait_recv()
                for peer in others:
                    spread(shift, cluster, peer).start()

        @pl.when(k == 6)
        def _():
            for shift in range(1, outer):
                all_shares(shift).wait_recv()
                block(2 * shift).start()
                block(2 * shift + 1).start()

        @pl.when(k >= 1)
        def _():
            forward_tile(k - 1)

        return carry

    lax.fori_loop(0, count + 1, step, 0)
    sums = cluster_sum(total, summed_total, half_in, quarter_in, bias_in, sum_sems, clusters)
    sums.start()
    store_grad(count - 2).wait()
    send_grad(count // 2 - 1, at(count - 2))
    for p in range(1, n):
        if p == 1 or p % 2 == 0:
            last_hop(p).start()
    for p in range(1, n):
        several(count, send_sem.at[p], near_in.at[0]).wait_send()
    for p in range(1, n, 2):
        block(p).wait_send()
    for shift in range(1, outer):
        share(shift).wait_send()
        all_shares(shift).wait_send()
    for p in range(n):
        if p % 2:
            block(p).wait_recv()
        else:
            block(p).wait()
    copies = [
        pltpu.make_async_copy(blocks_out.at[p], mat.at[pl.ds(p * width, width)], block_send.at[p - p % 2])
        for p in range(0, n, 2)
    ] + [
        pltpu.make_async_copy(blocks_out.at[p], mat.at[pl.ds(p * width, width)], block_recv.at[p])
        for p in range(1, n, 2)
    ]
    for copy in copies:
        copy.start()
    for copy in copies:
        copy.wait()

    def backward_tile(k):
        slot = lax.rem(k, 2)
        for p in range(n):
            load_piece(p, k).wait()
        scaled[at(k), :] = back_through(lambda p: back[slot, p], n, mat, sten[at(k), :])

    def moment(r):
        return max(r * 512 // tile, 0)

    def back_step(k, carry):
        @pl.when(k >= 1)
        def _():
            backward_tile(k - 1)

        @pl.when((k < count - 2) & (lax.rem(k, 2) == 0))
        def _():
            pass_grad(k // 2, pair(k // 2), 2)
            for p in range(n):
                load_piece(p, k).start()
                load_piece(p, k + 1).start()

        @pl.when(k == count - 2)
        def _():
            pass_grad(count // 2 - 1, at(count - 2), 1)
            for p in range(n):
                load_piece(p, count - 2).start()

        for r in range(sums.rounds):
            if moment(r) < count:
                pl.when(k == moment(r))(functools.partial(sums.advance, r))
        if moment(sums.last) < count:
            pl.when(k == moment(sums.last))(sums.finish)
        return carry

    lax.fori_loop(0, count, back_step, 0)
    for r in range(sums.rounds):
        if moment(r) >= count:
            sums.advance(r)
    if moment(sums.last) >= count:
        sums.finish()
    for p in range(2, n, 2):
        last_hop(p).wait_recv()
        last_hop(p + 1).start()
    for p in range(1, n):
        several(count - 1, grad_out.at[p], grad_near.at[0]).wait_send()
        last_hop(p).wait_send()
    several(outer, last_out.at[0], grad_near.at[count // 2]).wait_recv()


def exchange(features, adjacency, cotangent, segments, weight, bias, n, clusters, tile):
    rows, width = features.shape
    depth = weight.shape[0]
    count, outer = rows // tile, n // 2
    parts, high = cluster_sum.PARTS, clusters // 2
    dma = pltpu.SemaphoreType.DMA
    array = jax.ShapeDtypeStruct
    return pl.pallas_call(
        functools.partial(exchange_kernel, n, clusters, tile),
        in_specs=[HBM] * 6,
        out_specs=[VMEM] * 6 + [HBM] * (n + 1),
        out_shape=[
            pltpu.VMEM((rows, width), BF16),
            pltpu.VMEM((rows, width), BF16),
            pltpu.VMEM((depth + 8, width), F32),
            pltpu.VMEM((rows, BLOCK), BF16),
            pltpu.VMEM((depth, width), BF16),
            pltpu.VMEM((n, tile, width), BF16),
            array((n, width, width), BF16),
        ]
        + [array((rows, width), BF16)] * n,
        scratch_shapes=[pltpu.VMEM((rows, width), BF16)] * (n - 2)
        + [
            pltpu.VMEM((2, tile, width), BF16),
            pltpu.VMEM((2, tile, BLOCK), jnp.int32),
            pltpu.VMEM((2, tile, width), BF16),
            pltpu.VMEM((2, tile, width), BF16),
            pltpu.VMEM(segments.shape, jnp.int32),
            pltpu.VMEM((width,), BF16),
            pltpu.VMEM((depth + 8, width), F32),
            pltpu.VMEM((outer, 2 * width, width), BF16),
            pltpu.VMEM((2, n, tile, width), BF16),
            dma((2, 2)),
            dma((2,)),
            dma((2,)),
            dma((3,)),
            dma((n,)),
            dma((outer - 1, count // 2)),
            dma((count // 2,)),
            dma((n,)),
            dma((outer - 1, count // 2 + 1)),
            dma((count // 2 + 1,)),
            dma((n,)),
            dma((2, n)),
            dma((outer,)),
            dma((outer,)),
            dma((outer,)),
            dma((outer,)),
            dma((n,)),
            dma((n,)),
            pltpu.VMEM((parts, depth // parts // 2, width), F32),
            pltpu.VMEM((parts, high, depth // parts // 2 // high, width), F32),
            pltpu.VMEM((clusters, 8, width), F32),
            [dma((5,)), dma((parts,)), dma((parts,)), dma((parts,)), dma((1,)), dma((1,))],
        ],
        compiler_params=pltpu.CompilerParams(
            collective_id=0, has_side_effects=True, vmem_limit_bytes=38 << 20
        ),
    )(*[pltpu.with_memory_space_constraint(x, pltpu.HBM) for x in (features, adjacency, cotangent, segments, weight, bias)])


def finish_kernel(
    activations, scaled, total, stencil, blocks, last,
    grad_features, out, grad_weight, grad_bias, slots, row, rest, slot_sem, fixed_sem,
):
    rows, width = scaled.shape
    n, tile, _ = last.shape
    depth = total.shape[0] - 8
    span = 2 * tile
    count = rows // span
    row[...] = jnp.sum(total[pl.ds(depth, 8), :], axis=0, keepdims=True)
    fixed = [
        pltpu.make_async_copy(activations, out, fixed_sem.at[0]),
        pltpu.make_async_copy(total.at[pl.ds(0, depth)], grad_weight, fixed_sem.at[1]),
        pltpu.make_async_copy(row, grad_bias, fixed_sem.at[2]),
    ]
    for copy in fixed:
        copy.start()
    rest[...] = back_through(lambda p: last[p], n, blocks, stencil[pl.ds(rows - tile, tile), :])

    def store(k):
        slot = lax.rem(k, SLOTS)
        target = pl.ds(pl.multiple_of(k * span, span), span)
        return pltpu.make_async_copy(slots.at[slot], grad_features.at[target], slot_sem.at[slot])

    def step(k, own):
        slot = lax.rem(k, SLOTS)
        for b in range(span // BLOCK):
            source = pl.ds(pl.multiple_of(k * span + b * BLOCK, BLOCK), BLOCK)
            if b * BLOCK < own:
                value = scaled[source, :]
            else:
                value = rest[pl.ds(b * BLOCK - own, BLOCK), :]
            slots[slot, pl.ds(b * BLOCK, BLOCK), :] = jnp.dot(
                stencil[source, :], value, preferred_element_type=F32
            )
        store(k).start()

    def full(k, carry):
        @pl.when(k >= SLOTS)
        def _():
            store(k - SLOTS).wait()

        step(k, span)
        return carry

    lax.fori_loop(0, count - 1, full, 0)
    if count > SLOTS:
        store(count - 1 - SLOTS).wait()
    step(count - 1, tile)
    for k in range(max(count - SLOTS, 0), count):
        store(k).wait()
    for copy in fixed:
        copy.wait()


def finish(activations, scaled, total, stencil, blocks, last):
    rows, width = scaled.shape
    tile = last.shape[1]
    depth = total.shape[0] - 8
    dma = pltpu.SemaphoreType.DMA
    return pl.pallas_call(
        finish_kernel,
        in_specs=[VMEM] * 6,
        out_specs=[HBM] * 4,
        out_shape=[
            jax.ShapeDtypeStruct((rows, width), F32),
            jax.ShapeDtypeStruct((rows, width), BF16),
            jax.ShapeDtypeStruct((depth, width), F32),
            jax.ShapeDtypeStruct((1, width), F32),
        ],
        scratch_shapes=[
            pltpu.VMEM((SLOTS, 2 * tile, width), F32),
            pltpu.VMEM((1, width), F32),
            pltpu.VMEM((tile, width), BF16),
            dma((SLOTS,)),
            dma((3,)),
        ],
        cost_estimate=pl.CostEstimate(
            flops=2 * rows * BLOCK * width, bytes_accessed=6 * rows * width + 4 * depth * width, transcendentals=0
        ),
        compiler_params=pltpu.CompilerParams(vmem_limit_bytes=12 << 20),
    )(activations, scaled, total, stencil, blocks, last)


def build(n, clusters):
    def local(features, weight, bias, adjacency, segments, cotangent):
        tile = 256 if n <= 4 else 512
        held = exchange(features, adjacency, cotangent, segments, weight, bias, n, clusters, tile)[:6]
        grad_features, out, grad_weight, grad_bias = finish(*held)
        return (out, grad_features, grad_weight, grad_bias.reshape(-1))

    return local


def solution(mesh):
    return jax.shard_map(
        build(mesh.shape["col"], mesh.shape["clu"]),
        mesh=mesh,
        in_specs=(
            P("clu", "col"),
            P(None, "col"),
            P("col"),
            P("clu", None),
            P("clu", None),
            P("clu", "col"),
        ),
        out_specs=(P("clu", "col"), P("clu", "col"), P(None, "col"), P("col")),
        check_vma=False,
    )
```

```python
import functools

import jax
import jax.numpy as jnp
from jax import lax
from jax.experimental import pallas as pl
from jax.experimental.pallas import tpu as pltpu
from jax.sharding import PartitionSpec as P

BLOCK = 128
SLOTS = 4
TAIL = 6
F32 = jnp.float32
BF16 = jnp.bfloat16
MESH = pl.DeviceIdType.MESH
HBM = pl.BlockSpec(memory_space=pltpu.HBM)
VMEM = pl.BlockSpec(memory_space=pltpu.VMEM)


def stencil_of(adjacency, segment):
    columns = jnp.broadcast_to(segment, (BLOCK, BLOCK))
    links = jnp.where(columns == columns.T, adjacency, 0).astype(F32)
    inverse = 1.0 / (jnp.sum(links, axis=1, keepdims=True) + 1.0)
    row = lax.broadcasted_iota(jnp.int32, (BLOCK, BLOCK), 0)
    column = lax.broadcasted_iota(jnp.int32, (BLOCK, BLOCK), 1)
    return (links + jnp.where(row == column, 2.0, 0.0)).astype(BF16), inverse


def back_through(piece, n, blocks, stencil):
    width = blocks.shape[1]
    value = None
    for p in range(n):
        term = lax.dot_general(
            piece(p), blocks[pl.ds(p * width, width), :], (((1,), (1,)), ((), ())), preferred_element_type=F32
        )
        value = term if value is None else value + term
    inverse = 1.0 / (jnp.sum(stencil.astype(F32), axis=1, keepdims=True) - 1.0)
    return (value.astype(BF16).astype(F32) * inverse).astype(BF16)


class cluster_sum:
    PARTS = 4
    BACK = (5, 7, 8, 9)
    rounds = 10
    last = 12

    def __init__(self, total, result, half_in, quarter_in, bias_in, sems, clusters):
        self.result = result
        self.total, self.half_in, self.quarter_in, self.bias_in, self.sems = total, half_in, quarter_in, bias_in, sems
        self.clusters, self.high = clusters, clusters // 2
        self.depth = total.shape[0] - 8
        self.half = self.depth // self.PARTS // 2
        self.quarter = self.half // self.high
        self.me = lax.axis_index("clu")
        self.z, self.x = self.me // 2, lax.rem(self.me, 2)
        self.others = [lax.rem(self.me + d, clusters) for d in range(1, clusters)]
        self.levels = [lax.rem(self.z + d, self.high) for d in range(1, self.high)]

    def rows_of_half(self, c, x):
        return pl.ds(pl.multiple_of(c * 2 * self.half + x * self.half, self.half), self.half)

    def rows_of_quarter(self, c, q):
        start = c * 2 * self.half + self.x * self.half + q * self.quarter
        return pl.ds(pl.multiple_of(start, self.quarter), self.quarter)

    def copy(self, source, target, kind, recv, device):
        return pltpu.make_async_remote_copy(
            src_ref=source, dst_ref=target, send_sem=self.sems[0].at[kind],
            recv_sem=self.sems[1 + kind].at[recv], device_id={"clu": device}, device_id_type=MESH,
        )

    def several(self, rows, kind, recv=0):
        return self.copy(self.total.at[pl.ds(0, rows)], self.result.at[pl.ds(0, rows)], kind, recv, self.others[0])

    def give_half(self, c):
        rows = self.rows_of_half(c, 1 - self.x)
        return self.copy(self.total.at[rows], self.half_in.at[c], 0, c, self.z * 2 + 1 - self.x)

    def give_quarter(self, c, source, target):
        rows = self.rows_of_quarter(c, target)
        return self.copy(
            self.total.at[rows], self.quarter_in.at[c, source], 1, c, target * 2 + self.x
        )

    def return_quarter(self, c, source, target):
        rows = self.rows_of_quarter(c, source)
        return self.copy(
            self.result.at[rows], self.result.at[rows], 2, c, target * 2 + self.x
        )

    def return_half(self, c, x):
        rows = self.rows_of_half(c, x)
        return self.copy(self.result.at[rows], self.result.at[rows], 3, 0, self.z * 2 + 1 - self.x)

    def give_bias(self, source, target):
        return self.copy(
            self.total.at[pl.ds(self.depth, 8)], self.bias_in.at[source], 4, 0, target
        )

    def start(self):
        for c in range(self.PARTS):
            self.give_half(c).start()
        for other in self.others:
            self.give_bias(self.me, other).start()

    def advance(self, k):
        total = self.total
        if k < self.PARTS:
            self.give_half(k).wait_recv()
            total[self.rows_of_half(k, self.x), :] += self.half_in[k]
            for level in self.levels:
                self.give_quarter(k, self.z, level).start()
        c = k - 2
        if 0 <= c < self.PARTS:
            rows = self.rows_of_quarter(c, self.z)
            self.several(len(self.levels) * self.quarter, 1, c).wait_recv()
            value = total[rows, :]
            for level in self.levels:
                value = value + self.quarter_in[c, level]
            self.result[rows, :] = value
            for level in self.levels:
                self.return_quarter(c, self.z, level).start()
        if k in self.BACK:
            c = self.BACK.index(k)
            self.several(len(self.levels) * self.quarter, 2, c).wait_recv()
            self.return_half(c, self.x).start()

    def finish(self):
        halves = self.PARTS * self.half
        quarters = self.PARTS * len(self.levels) * self.quarter
        for kind, rows in enumerate((halves, quarters, quarters, halves, 8 * len(self.others))):
            self.several(rows, kind).wait_send()
        self.several(halves, 3).wait_recv()
        self.several(8 * len(self.others), 4).wait_recv()
        value = self.total[pl.ds(self.depth, 8), :]
        for other in self.others:
            value = value + self.bias_in[other]
        self.result[pl.ds(self.depth, 8), :] = value


def exchange_kernel(
    n, clusters, early, tile, features, adjacency, cotangent, segments, weight, bias,
    activations, scaled, summed_total, sten, mat, blocks_out, grads, *rest,
):
    landing = (None,) + rest[: n - 1]
    pieces = list(rest[n - 1 : 2 * n - 3])
    pieces = pieces[:1] + [activations] + pieces[1:] + [scaled]
    (feat, adj, cot, grad, seg, vec, total, shares, back, load_sem, cot_sem, grad_sem,
     fixed_sem, send_sem, far_in, near_in, grad_out, grad_far, grad_near, back_sem, share_send, share_recv, spread_send, spread_recv,
     block_send, block_recv, half_in, quarter_in, bias_in, sum_sems) = rest[2 * n - 3 :]
    outer = n // 2
    rows, width = features.shape
    depth = mat.shape[0]
    count = rows // tile
    me, cluster = lax.axis_index("col"), lax.axis_index("clu")
    chip, core = me // 2, lax.rem(me, 2)
    sibling = chip * 2 + 1 - core
    part = 2 * width // clusters
    others = [lax.rem(cluster + d, clusters) for d in range(1, clusters)]

    def chip_at(shift):
        return lax.rem(chip + shift + outer, outer) * 2 + core

    def at(k):
        return pl.ds(pl.multiple_of(k * tile, tile), tile)

    def pair(c):
        return pl.ds(pl.multiple_of(c * 2 * tile, 2 * tile), 2 * tile)

    def loads(k):
        slot = lax.rem(k, 2)
        return (
            pltpu.make_async_copy(features.at[at(k)], feat.at[slot], load_sem.at[0, slot]),
            pltpu.make_async_copy(adjacency.at[at(k)], adj.at[slot], load_sem.at[1, slot]),
        )

    def load_cot(k):
        slot = lax.rem(k, 2)
        return pltpu.make_async_copy(cotangent.at[at(k)], cot.at[slot], cot_sem.at[slot])

    def store_grad(k):
        slot = lax.rem(k, 2)
        return pltpu.make_async_copy(grad.at[slot], grads.at[at(k)], grad_sem.at[slot])

    def remote(source, target, send, recv, device, axis="col"):
        return pltpu.make_async_remote_copy(
            src_ref=source, dst_ref=target, send_sem=send, recv_sem=recv,
            device_id={axis: device}, device_id_type=MESH,
        )

    def hop(p, c):
        source = 0 if p % 2 == 0 else p - 1
        device = chip_at(-(p // 2)) if p % 2 == 0 else sibling
        arrival = far_in.at[p // 2 - 1, c] if p % 2 == 0 else near_in.at[c]
        return remote(pieces[source].at[pair(c)], pieces[p].at[pair(c)], send_sem.at[p], arrival, device)

    def grad_hop(p, c):
        rows = pair(c)
        source = grads if p < 2 or p % 2 == 0 else landing[p - 1]
        device = chip_at(-(p // 2)) if p % 2 == 0 else sibling
        arrival = grad_far.at[p // 2 - 1, c] if p % 2 == 0 else grad_near.at[c]
        return remote(source.at[rows], landing[p].at[rows], grad_out.at[p], arrival, device)

    def several(tiles, send, arrival):
        span = pl.ds(0, tiles * tile)
        return remote(grads.at[span], landing[1].at[span], send, arrival, sibling)

    def send_grad(c):
        @pl.when((c < early // 2) | (core == 1))
        def _():
            for shift in range(1, outer):
                grad_hop(2 * shift, c).start()

        grad_hop(1, c).start()

    def load_piece(p, k):
        slot = lax.rem(k, 2)
        source = landing[p] if p else grads
        return pltpu.make_async_copy(source.at[at(k)], back.at[slot, p], back_sem.at[slot, p])

    def share(shift):
        owner = lax.rem(chip - shift + outer, outer)
        rows = pl.ds(pl.multiple_of(owner * 2 * width + cluster * part, part), part)
        mine = pl.ds(pl.multiple_of(cluster * part, part), part)
        return remote(
            weight.at[rows], shares.at[shift, mine], share_send.at[shift], share_recv.at[shift], chip_at(-shift)
        )

    def spread(shift, source, peer):
        rows = pl.ds(pl.multiple_of(source * part, part), part)
        return remote(
            shares.at[shift, rows], shares.at[shift, rows],
            spread_send.at[shift], spread_recv.at[shift], peer, "clu",
        )

    def all_shares(shift):
        rows = pl.ds(0, len(others) * part)
        return remote(
            shares.at[shift, rows], shares.at[shift, rows], spread_send.at[shift], spread_recv.at[shift], others[0], "clu"
        )

    def block(p):
        half = core if p % 2 == 0 else 1 - core
        if p < 2:
            source = weight.at[pl.ds(pl.multiple_of((chip * 2 + half) * width, width), width)]
        else:
            source = shares.at[p // 2, pl.ds(pl.multiple_of(half * width, width), width)]
        if p % 2 == 0:
            return pltpu.make_async_copy(source, blocks_out.at[p], block_recv.at[p])
        return remote(source, blocks_out.at[p], block_send.at[p], block_recv.at[p], sibling)

    for copy in loads(0):
        copy.start()
    fixed = [
        pltpu.make_async_copy(source, target, fixed_sem.at[i])
        for i, (source, target) in enumerate([(segments, seg), (weight, mat), (bias, vec)])
    ]
    for copy in fixed:
        copy.start()
    load_cot(0).start()

    barrier = pltpu.get_barrier_semaphore()
    centre = clusters - 2 + core
    neighbours = [sibling] + [chip_at(shift) for shift in range(1, outer)]

    def greet(axis, peer):
        pl.semaphore_signal(barrier, inc=1, device_id={axis: peer}, device_id_type=MESH)

    for peer in neighbours:
        greet("col", peer)

    @pl.when(cluster == centre)
    def _():
        pl.semaphore_wait(barrier, len(neighbours) + len(others))
        for peer in others:
            greet("clu", peer)

    @pl.when(cluster != centre)
    def _():
        pl.semaphore_wait(barrier, len(neighbours))
        greet("clu", centre)

    for shift in range(1, outer):
        share(shift).start()
    block(0).start()
    block(1).start()
    fixed[0].wait()

    def aggregate_tile(k, carry):
        slot = lax.rem(k, 2)
        for copy in loads(k):
            copy.wait()

        @pl.when(k + 1 < count)
        def _():
            for copy in loads(k + 1):
                copy.start()

        for b in range(tile // BLOCK):
            part = pl.ds(b * BLOCK, BLOCK)
            stencil, inverse = stencil_of(adj[slot, part, :], seg[pl.ds(k * (tile // BLOCK) + b, 1), :])
            summed = jnp.dot(stencil, feat[slot, part, :], preferred_element_type=F32)
            target = pl.ds(pl.multiple_of(k * tile + b * BLOCK, BLOCK), BLOCK)
            sten[target, :] = stencil
            pieces[0][target, :] = (summed * inverse).astype(BF16)

        @pl.when(lax.rem(k, 2) == 1)
        def _():
            for shift in range(1, outer):
                hop(2 * shift, k // 2).start()
            hop(1, k // 2).start()

        return carry

    lax.fori_loop(0, count, aggregate_tile, 0)
    total[...] = jnp.zeros_like(total)
    fixed[1].wait()
    fixed[2].wait()
    blocks = [lax.rem(chip + p // 2, outer) * 2 + (core if p % 2 == 0 else 1 - core) for p in range(n)]

    def forward_tile(k):
        slot = lax.rem(k, 2)
        load_cot(k).wait()

        @pl.when(k + 1 < count)
        def _():
            load_cot(k + 1).start()

        @pl.when(lax.rem(k, 2) == 0)
        def _():
            several(2 * outer, send_sem.at[0], near_in.at[k // 2]).wait_recv()


        @pl.when(k >= 2)
        def _():
            store_grad(k - 2).wait()

        @pl.when((k >= 3) & (lax.rem(k, 2) == 1))
        def _():
            send_grad((k - 3) // 2)

        preact = None
        for p in range(n):
            source = pl.ds(pl.multiple_of(blocks[p] * width, width), width)
            term = jnp.dot(pieces[p][at(k), :], mat[source, :], preferred_element_type=F32)
            preact = term if preact is None else preact + term
        preact = preact + vec[...].astype(F32).reshape(1, width)
        grad_preact = jnp.where(preact > 0.0, cot[slot].astype(F32), 0.0)
        total[pl.ds(depth, 8), :] += jnp.sum(grad_preact.reshape(tile // 8, 8, width), axis=0)
        grad_preact = grad_preact.astype(BF16)
        grad[slot] = grad_preact

        store_grad(k).start()
        for p in range(n):
            target = pl.ds(pl.multiple_of(blocks[p] * width, width), width)
            total[target, :] += lax.dot_general(
                pieces[p][at(k), :], grad_preact, (((0,), (0,)), ((), ())), preferred_element_type=F32
            )
        activations[at(k), :] = jnp.maximum(preact, 0.0).astype(BF16)

    def step(k, carry):
        @pl.when((k < count) & (lax.rem(k, 2) == 0))
        def _():
            for shift in range(1, outer):
                hop(2 * shift, k // 2).wait_recv()
                hop(2 * shift + 1, k // 2).start()

        @pl.when((k == 2) & (cluster != centre))
        def _():
            pl.semaphore_wait(barrier, 1)

        @pl.when(k == 2)
        def _():
            for shift in range(1, outer):
                share(shift).wait_recv()
                for peer in others:
                    spread(shift, cluster, peer).start()

        @pl.when(k == 6)
        def _():
            for shift in range(1, outer):
                all_shares(shift).wait_recv()
                block(2 * shift).start()
                block(2 * shift + 1).start()

        @pl.when(k >= 1)
        def _():
            forward_tile(k - 1)

        return carry

    lax.fori_loop(0, count + 1, step, 0)
    sums = cluster_sum(total, summed_total, half_in, quarter_in, bias_in, sum_sems, clusters)
    sums.start()
    for k in (count - 2, count - 1):
        store_grad(k).wait()
    send_grad(count // 2 - 1)
    for p in range(1, n):
        several(count, send_sem.at[p], near_in.at[0]).wait_send()
    for p in range(1, n, 2):
        block(p).wait_send()
    for shift in range(1, outer):
        share(shift).wait_send()
        all_shares(shift).wait_send()
    for p in range(n):
        if p % 2:
            block(p).wait_recv()
        else:
            block(p).wait()
    copies = [
        pltpu.make_async_copy(blocks_out.at[p], mat.at[pl.ds(p * width, width)], block_send.at[p - p % 2])
        for p in range(0, n, 2)
    ] + [
        pltpu.make_async_copy(blocks_out.at[p], mat.at[pl.ds(p * width, width)], block_recv.at[p])
        for p in range(1, n, 2)
    ]
    for copy in copies:
        copy.start()
    for copy in copies:
        copy.wait()

    def backward_tile(k):
        slot = lax.rem(k, 2)
        for p in range(n):
            load_piece(p, k).wait()
        scaled[at(k), :] = back_through(lambda p: back[slot, p], n, mat, sten[at(k), :])

    def moment(r):
        return max(r * 512 // tile, 0)

    def back_step(k, carry):
        @pl.when(k >= 1)
        def _():
            backward_tile(k - 1)

        @pl.when((k < early) & (lax.rem(k, 2) == 0))
        def _():
            for shift in range(1, outer):
                grad_hop(2 * shift, k // 2).wait_recv()
                grad_hop(2 * shift + 1, k // 2).start()
            several(2 * outer, grad_out.at[0], grad_near.at[k // 2]).wait_recv()
            for p in range(n):
                load_piece(p, k).start()
                load_piece(p, k + 1).start()

        for r in range(sums.rounds):
            if moment(r) <= early:
                pl.when(k == moment(r))(functools.partial(sums.advance, r))
        if moment(sums.last) <= early:
            pl.when(k == moment(sums.last))(sums.finish)
        return carry

    lax.fori_loop(0, early + 1, back_step, 0)
    for r in range(sums.rounds):
        if moment(r) > early:
            sums.advance(r)
    if moment(sums.last) > early:
        sums.finish()
    def late_step(c, carry):
        several(2, grad_out.at[0], grad_near.at[c]).wait_recv()

        @pl.when(core == 1)
        def _():
            for shift in range(1, outer):
                grad_hop(2 * shift, c).wait_recv()

        return carry

    for p in range(3, n, 2):
        several(early, grad_out.at[p], grad_near.at[0]).wait_send()
    several(count, grad_out.at[1], grad_near.at[0]).wait_send()
    lax.fori_loop(early // 2, count // 2, late_step, 0)

    @pl.when(core == 0)
    def _():
        for p in range(2, n, 2):
            several(early, grad_out.at[p], grad_near.at[0]).wait_send()

    @pl.when(core == 1)
    def _():
        for p in range(2, n, 2):
            several(count, grad_out.at[p], grad_near.at[0]).wait_send()


def exchange(features, adjacency, cotangent, segments, weight, bias, n, clusters, early, tile):
    rows, width = features.shape
    depth = weight.shape[0]
    count, outer = rows // tile, n // 2
    parts, high = cluster_sum.PARTS, clusters // 2
    dma = pltpu.SemaphoreType.DMA
    array = jax.ShapeDtypeStruct
    return pl.pallas_call(
        functools.partial(exchange_kernel, n, clusters, early, tile),
        in_specs=[HBM] * 6,
        out_specs=[VMEM] * 5 + [HBM] * (n + 1),
        out_shape=[
            pltpu.VMEM((rows, width), BF16),
            pltpu.VMEM((rows, width), BF16),
            pltpu.VMEM((depth + 8, width), F32),
            pltpu.VMEM((rows, BLOCK), BF16),
            pltpu.VMEM((depth, width), BF16),
            array((n, width, width), BF16),
        ]
        + [array((rows, width), BF16)] * n,
        scratch_shapes=[pltpu.VMEM((rows, width), BF16)] * (n - 2)
        + [
            pltpu.VMEM((2, tile, width), BF16),
            pltpu.VMEM((2, tile, BLOCK), jnp.int32),
            pltpu.VMEM((2, tile, width), BF16),
            pltpu.VMEM((2, tile, width), BF16),
            pltpu.VMEM(segments.shape, jnp.int32),
            pltpu.VMEM((width,), BF16),
            pltpu.VMEM((depth + 8, width), F32),
            pltpu.VMEM((outer, 2 * width, width), BF16),
            pltpu.VMEM((2, n, tile, width), BF16),
            dma((2, 2)),
            dma((2,)),
            dma((2,)),
            dma((3,)),
            dma((n,)),
            dma((outer - 1, count // 2)),
            dma((count // 2,)),
            dma((n,)),
            dma((outer - 1, count // 2)),
            dma((count // 2,)),
            dma((2, n)),
            dma((outer,)),
            dma((outer,)),
            dma((outer,)),
            dma((outer,)),
            dma((n,)),
            dma((n,)),
            pltpu.VMEM((parts, depth // parts // 2, width), F32),
            pltpu.VMEM((parts, high, depth // parts // 2 // high, width), F32),
            pltpu.VMEM((clusters, 8, width), F32),
            [dma((5,)), dma((parts,)), dma((parts,)), dma((parts,)), dma((1,)), dma((1,))],
        ],
        compiler_params=pltpu.CompilerParams(
            collective_id=0, has_side_effects=True, vmem_limit_bytes=38 << 20
        ),
    )(*[pltpu.with_memory_space_constraint(x, pltpu.HBM) for x in (features, adjacency, cotangent, segments, weight, bias)])


def stencil_rows(stencil, scaled, slots, slot, first, start, span):
    for b in range(span // BLOCK):
        source = pl.multiple_of(start + b * BLOCK, BLOCK)
        slots[slot, pl.ds(b * BLOCK, BLOCK), :] = jnp.dot(
            stencil[pl.ds(first + source, BLOCK), :], scaled[pl.ds(source, BLOCK), :], preferred_element_type=F32
        )


def finish_kernel(
    early, span, activations, scaled, total, stencil,
    grad_features, out, grad_weight, grad_bias, slots, row, slot_sem, fixed_sem,
):
    depth = total.shape[0] - 8
    count = early // span
    row[...] = jnp.sum(total[pl.ds(depth, 8), :], axis=0, keepdims=True)
    fixed = [
        pltpu.make_async_copy(activations, out, fixed_sem.at[0]),
        pltpu.make_async_copy(total.at[pl.ds(0, depth)], grad_weight, fixed_sem.at[1]),
        pltpu.make_async_copy(row, grad_bias, fixed_sem.at[2]),
    ]
    for copy in fixed:
        copy.start()

    def store(k):
        slot = lax.rem(k, SLOTS)
        target = pl.ds(pl.multiple_of(k * span, span), span)
        return pltpu.make_async_copy(slots.at[slot], grad_features.at[target], slot_sem.at[slot])

    def step(k, carry):
        @pl.when(k >= SLOTS)
        def _():
            store(k - SLOTS).wait()

        stencil_rows(stencil, scaled, slots, lax.rem(k, SLOTS), 0, k * span, span)
        store(k).start()
        return carry

    lax.fori_loop(0, count, step, 0)
    for k in range(max(count - SLOTS, 0), count):
        store(k).wait()
    for copy in fixed:
        copy.wait()


def finish(activations, scaled, total, stencil, early, tile):
    rows, width = scaled.shape
    depth = total.shape[0] - 8
    dma = pltpu.SemaphoreType.DMA
    return pl.pallas_call(
        functools.partial(finish_kernel, early * tile, 2 * tile),
        in_specs=[VMEM] * 4,
        out_specs=[HBM] * 4,
        out_shape=[
            jax.ShapeDtypeStruct((rows, width), F32),
            jax.ShapeDtypeStruct((rows, width), BF16),
            jax.ShapeDtypeStruct((depth, width), F32),
            jax.ShapeDtypeStruct((1, width), F32),
        ],
        scratch_shapes=[
            pltpu.VMEM((SLOTS, 2 * tile, width), F32),
            pltpu.VMEM((1, width), F32),
            dma((SLOTS,)),
            dma((3,)),
        ],
        cost_estimate=pl.CostEstimate(
            flops=2 * rows * BLOCK * width, bytes_accessed=6 * rows * width + 4 * depth * width, transcendentals=0
        ),
        compiler_params=pltpu.CompilerParams(vmem_limit_bytes=12 << 20),
    )(activations, scaled, total, stencil)


def late_kernel(n, early, tile, *refs):
    grads, landing = refs[0], (None,) + refs[1:n]
    sten, mat, scaled, pieces, load_sem, far_out, far_in, near_out, near_in = refs[n + 1 :]
    outer = n // 2
    rows, width = grads.shape
    late = rows // tile - early
    kept = pl.ds(early * tile, late * tile)
    me = lax.axis_index("col")
    chip, core = me // 2, lax.rem(me, 2)
    sibling = chip * 2 + 1 - core

    def chip_at(shift):
        return lax.rem(chip + shift + outer, outer) * 2 + core

    def at(j):
        return pl.ds(pl.multiple_of(j * tile, tile), tile)

    def remote(source, target, send, recv, device):
        return pltpu.make_async_remote_copy(
            src_ref=source, dst_ref=target, send_sem=send, recv_sem=recv,
            device_id={"col": device}, device_id_type=MESH,
        )

    def load(p):
        source = landing[p] if p else grads
        return pltpu.make_async_copy(source.at[kept], pieces.at[p], load_sem.at[p])

    def far(p, j):
        source = grads.at[pl.ds(pl.multiple_of((early + j) * tile, tile), tile)]
        return remote(source, pieces.at[p, at(j)], far_out.at[p], far_in.at[p // 2 - 1, j], chip_at(-(p // 2)))

    def near(p, j):
        return remote(pieces.at[p - 1, at(j)], pieces.at[p, at(j)], near_out.at[p], near_in.at[p // 2 - 1, j], sibling)

    barrier = pltpu.get_barrier_semaphore()
    load(0).start()
    load(1).start()

    @pl.when(core == 0)
    def _():
        for shift in range(1, outer):
            pl.semaphore_signal(barrier, inc=1, device_id={"col": chip_at(shift)}, device_id_type=MESH)
        pl.semaphore_wait(barrier, outer - 1)
        for j in range(late):
            for p in range(2, n, 2):
                far(p, j).start()
        pl.semaphore_signal(barrier, inc=1, device_id={"col": sibling}, device_id_type=MESH)
        pl.semaphore_wait(barrier, 1)

    @pl.when(core == 1)
    def _():
        for p in range(2, n, 2):
            load(p).start()
        pl.semaphore_wait(barrier, 1)
        pl.semaphore_signal(barrier, inc=1, device_id={"col": sibling}, device_id_type=MESH)
        for p in range(2, n, 2):
            load(p).wait()
        for j in range(late):
            for p in range(3, n, 2):
                near(p, j).start()

    load(0).wait()
    load(1).wait()

    def step(j, carry):
        @pl.when(core == 0)
        def _():
            for p in range(2, n, 2):
                far(p, j).wait_recv()
                near(p + 1, j).start()

        for p in range(3, n, 2):
            near(p, j).wait_recv()
        stencil = sten[pl.ds(pl.multiple_of((early + j) * tile, tile), tile), :]
        scaled[at(j), :] = back_through(lambda p: pieces[p, at(j), :], n, mat, stencil)
        return carry

    lax.fori_loop(0, late, step, 0)

    @pl.when(core == 0)
    def _():
        for p in range(2, n, 2):
            remote(grads.at[kept], pieces.at[p], far_out.at[p], far_in.at[p // 2 - 1, 0], chip_at(-(p // 2))).wait_send()

    for p in range(3, n, 2):
        remote(pieces.at[p - 1], pieces.at[p], near_out.at[p], near_in.at[p // 2 - 1, 0], sibling).wait_send()


def exchange_late(grads, landing, earlier, stencil, blocks, n, early, tile):
    rows, width = grads.shape
    late, outer = rows // tile - early, n // 2
    dma = pltpu.SemaphoreType.DMA
    far = [pltpu.with_memory_space_constraint(x, pltpu.HBM) for x in (grads, *landing, earlier)]
    return pl.pallas_call(
        functools.partial(late_kernel, n, early, tile),
        in_specs=[HBM] * (n + 1) + [VMEM] * 2,
        out_specs=VMEM,
        out_shape=pltpu.VMEM((late * tile, width), BF16),
        scratch_shapes=[
            pltpu.VMEM((n, late * tile, width), BF16),
            dma((n,)),
            dma((n,)),
            dma((outer - 1, late)),
            dma((n,)),
            dma((outer - 1, late)),
        ],
        compiler_params=pltpu.CompilerParams(
            collective_id=1, has_side_effects=True, vmem_limit_bytes=12 << 20
        ),
    )(*far, stencil, blocks)


def finish_late_kernel(first, span, scaled, stencil, _, grad_features, slots, sem):
    count = scaled.shape[0] // span

    def store(k):
        return pltpu.make_async_copy(slots.at[k], grad_features.at[pl.ds(first + k * span, span)], sem.at[k])

    for k in range(count):
        stencil_rows(stencil, scaled, slots, k, first, k * span, span)
        store(k).start()
    for k in range(count):
        store(k).wait()


def finish_late(scaled, stencil, grad_features, early, tile):
    late, width = scaled.shape
    span = tile
    return pl.pallas_call(
        functools.partial(finish_late_kernel, early * tile, span),
        in_specs=[VMEM] * 2 + [HBM],
        out_specs=HBM,
        out_shape=jax.ShapeDtypeStruct(grad_features.shape, F32),
        input_output_aliases={2: 0},
        scratch_shapes=[pltpu.VMEM((late // span, span, width), F32), pltpu.SemaphoreType.DMA((late // span,))],
        cost_estimate=pl.CostEstimate(
            flops=2 * late * BLOCK * width, bytes_accessed=4 * late * width, transcendentals=0
        ),
        compiler_params=pltpu.CompilerParams(vmem_limit_bytes=12 << 20),
    )(scaled, stencil, grad_features)


def build(n, clusters):
    def local(features, weight, bias, adjacency, segments, cotangent):
        tile = 256 if n <= 4 else 512
        early = features.shape[0] // tile - TAIL
        activations, scaled, total, stencil, blocks, _, grads, *landing = exchange(
            features, adjacency, cotangent, segments, weight, bias, n, clusters, early, tile
        )
        grad_features, out, grad_weight, grad_bias = finish(activations, scaled, total, stencil, early, tile)
        scaled = exchange_late(grads, landing, grad_bias, stencil, blocks, n, early, tile)
        grad_features = finish_late(scaled, stencil, grad_features, early, tile)
        return (out, grad_features, grad_weight, grad_bias.reshape(-1))

    return local


def solution(mesh):
    return jax.shard_map(
        build(mesh.shape["col"], mesh.shape["clu"]),
        mesh=mesh,
        in_specs=(
            P("clu", "col"),
            P(None, "col"),
            P("col"),
            P("clu", None),
            P("clu", None),
            P("clu", "col"),
        ),
        out_specs=(P("clu", "col"), P("clu", "col"), P(None, "col"), P("col")),
        check_vma=False,
    )
```

```python
import functools

import jax
import jax.numpy as jnp
from jax import lax
from jax.experimental import pallas as pl
from jax.experimental.pallas import tpu as pltpu
from jax.sharding import PartitionSpec as P

BLOCK = 128
SLOTS = 4
TAIL = 8
GROUP = 2
F32 = jnp.float32
BF16 = jnp.bfloat16
MESH = pl.DeviceIdType.MESH
HBM = pl.BlockSpec(memory_space=pltpu.HBM)
VMEM = pl.BlockSpec(memory_space=pltpu.VMEM)


def stencil_of(adjacency, segment):
    columns = jnp.broadcast_to(segment, (BLOCK, BLOCK))
    links = jnp.where(columns == columns.T, adjacency, 0).astype(F32)
    inverse = 1.0 / (jnp.sum(links, axis=1, keepdims=True) + 1.0)
    row = lax.broadcasted_iota(jnp.int32, (BLOCK, BLOCK), 0)
    column = lax.broadcasted_iota(jnp.int32, (BLOCK, BLOCK), 1)
    return (links + jnp.where(row == column, 2.0, 0.0)).astype(BF16), inverse


def back_through(piece, numbers, blocks):
    width = blocks.shape[1]
    value = None
    for p in numbers:
        block = blocks[pl.ds(pl.multiple_of(p * width, width), width), :]
        term = lax.dot_general(piece(p), block, (((1,), (1,)), ((), ())), preferred_element_type=F32)
        value = term if value is None else value + term
    return value


def scale(value, stencil):
    inverse = 1.0 / (jnp.sum(stencil.astype(F32), axis=1, keepdims=True) - 1.0)
    return (value.astype(BF16).astype(F32) * inverse).astype(BF16)


class cluster_sum:
    PARTS = 4
    BACK = (5, 7, 8, 9)
    rounds = 10
    last = 12

    def __init__(self, total, result, half_in, quarter_in, bias_in, sems, clusters):
        self.result = result
        self.total, self.half_in, self.quarter_in, self.bias_in, self.sems = total, half_in, quarter_in, bias_in, sems
        self.clusters, self.high = clusters, clusters // 2
        self.depth = total.shape[0] - 8
        self.half = self.depth // self.PARTS // 2
        self.quarter = self.half // self.high
        self.me = lax.axis_index("clu")
        self.z, self.x = self.me // 2, lax.rem(self.me, 2)
        self.others = [lax.rem(self.me + d, clusters) for d in range(1, clusters)]
        self.levels = [lax.rem(self.z + d, self.high) for d in range(1, self.high)]

    def rows_of_half(self, c, x):
        return pl.ds(pl.multiple_of(c * 2 * self.half + x * self.half, self.half), self.half)

    def rows_of_quarter(self, c, q):
        start = c * 2 * self.half + self.x * self.half + q * self.quarter
        return pl.ds(pl.multiple_of(start, self.quarter), self.quarter)

    def copy(self, source, target, kind, recv, device):
        return pltpu.make_async_remote_copy(
            src_ref=source, dst_ref=target, send_sem=self.sems[0].at[kind],
            recv_sem=self.sems[1 + kind].at[recv], device_id={"clu": device}, device_id_type=MESH,
        )

    def several(self, rows, kind, recv=0):
        return self.copy(self.total.at[pl.ds(0, rows)], self.result.at[pl.ds(0, rows)], kind, recv, self.others[0])

    def give_half(self, c):
        rows = self.rows_of_half(c, 1 - self.x)
        return self.copy(self.total.at[rows], self.half_in.at[c], 0, c, self.z * 2 + 1 - self.x)

    def give_quarter(self, c, source, target):
        rows = self.rows_of_quarter(c, target)
        return self.copy(
            self.total.at[rows], self.quarter_in.at[c, source], 1, c, target * 2 + self.x
        )

    def return_quarter(self, c, source, target):
        rows = self.rows_of_quarter(c, source)
        return self.copy(
            self.result.at[rows], self.result.at[rows], 2, c, target * 2 + self.x
        )

    def return_half(self, c, x):
        rows = self.rows_of_half(c, x)
        return self.copy(self.result.at[rows], self.result.at[rows], 3, 0, self.z * 2 + 1 - self.x)

    def give_bias(self, source, target):
        return self.copy(
            self.total.at[pl.ds(self.depth, 8)], self.bias_in.at[source], 4, 0, target
        )

    def start(self):
        for c in range(self.PARTS):
            self.give_half(c).start()
        for other in self.others:
            self.give_bias(self.me, other).start()

    def advance(self, k):
        total = self.total
        if k < self.PARTS:
            self.give_half(k).wait_recv()
            total[self.rows_of_half(k, self.x), :] += self.half_in[k]
            for level in self.levels:
                self.give_quarter(k, self.z, level).start()
        c = k - 2
        if 0 <= c < self.PARTS:
            rows = self.rows_of_quarter(c, self.z)
            self.several(len(self.levels) * self.quarter, 1, c).wait_recv()
            value = total[rows, :]
            for level in self.levels:
                value = value + self.quarter_in[c, level]
            self.result[rows, :] = value
            for level in self.levels:
                self.return_quarter(c, self.z, level).start()
        if k in self.BACK:
            c = self.BACK.index(k)
            self.several(len(self.levels) * self.quarter, 2, c).wait_recv()
            self.return_half(c, self.x).start()

    def finish(self):
        halves = self.PARTS * self.half
        quarters = self.PARTS * len(self.levels) * self.quarter
        for kind, rows in enumerate((halves, quarters, quarters, halves, 8 * len(self.others))):
            self.several(rows, kind).wait_send()
        self.several(halves, 3).wait_recv()
        self.several(8 * len(self.others), 4).wait_recv()
        value = self.total[pl.ds(self.depth, 8), :]
        for other in self.others:
            value = value + self.bias_in[other]
        self.result[pl.ds(self.depth, 8), :] = value


def exchange_kernel(
    n, clusters, early, tile, features, adjacency, cotangent, segments, weight, bias,
    activations, scaled, summed_total, sten, mat, blocks_out, grads, *rest,
):
    landing = (None,) + rest[: n - 1]
    pieces = list(rest[n - 1 : 2 * n - 3])
    pieces = pieces[:1] + [activations] + pieces[1:] + [scaled]
    (feat, adj, cot, grad, seg, vec, total, shares, back, load_sem, cot_sem, grad_sem,
     fixed_sem, send_sem, far_in, near_in, grad_out, grad_far, grad_near, back_sem, share_send, share_recv, spread_send, spread_recv,
     block_send, block_recv, half_in, quarter_in, bias_in, sum_sems) = rest[2 * n - 3 :]
    outer = n // 2
    rows, width = features.shape
    depth = mat.shape[0]
    count = rows // tile
    me, cluster = lax.axis_index("col"), lax.axis_index("clu")
    chip, core = me // 2, lax.rem(me, 2)
    sibling = chip * 2 + 1 - core
    part = 2 * width // clusters
    others = [lax.rem(cluster + d, clusters) for d in range(1, clusters)]

    def chip_at(shift):
        return lax.rem(chip + shift + outer, outer) * 2 + core

    def at(k):
        return pl.ds(pl.multiple_of(k * tile, tile), tile)

    def pair(c):
        return pl.ds(pl.multiple_of(c * 2 * tile, 2 * tile), 2 * tile)

    def loads(k):
        slot = lax.rem(k, 2)
        return (
            pltpu.make_async_copy(features.at[at(k)], feat.at[slot], load_sem.at[0, slot]),
            pltpu.make_async_copy(adjacency.at[at(k)], adj.at[slot], load_sem.at[1, slot]),
        )

    def load_cot(k):
        slot = lax.rem(k, 2)
        return pltpu.make_async_copy(cotangent.at[at(k)], cot.at[slot], cot_sem.at[slot])

    def store_grad(k):
        slot = lax.rem(k, 2)
        return pltpu.make_async_copy(grad.at[slot], grads.at[at(k)], grad_sem.at[slot])

    def remote(source, target, send, recv, device, axis="col"):
        return pltpu.make_async_remote_copy(
            src_ref=source, dst_ref=target, send_sem=send, recv_sem=recv,
            device_id={axis: device}, device_id_type=MESH,
        )

    def hop(p, c):
        source = 0 if p % 2 == 0 else p - 1
        device = chip_at(-(p // 2)) if p % 2 == 0 else sibling
        arrival = far_in.at[p // 2 - 1, c] if p % 2 == 0 else near_in.at[c]
        return remote(pieces[source].at[pair(c)], pieces[p].at[pair(c)], send_sem.at[p], arrival, device)

    def grad_hop(p, c):
        rows = pair(c)
        source = grads if p < 2 or p % 2 == 0 else landing[p - 1]
        device = chip_at(-(p // 2)) if p % 2 == 0 else sibling
        arrival = grad_far.at[p // 2 - 1, c] if p % 2 == 0 else grad_near.at[c]
        return remote(source.at[rows], landing[p].at[rows], grad_out.at[p], arrival, device)

    def several(tiles, send, arrival):
        span = pl.ds(0, tiles * tile)
        return remote(grads.at[span], landing[1].at[span], send, arrival, sibling)

    def send_grad(c):
        @pl.when((c < early // 2) | (core == 1))
        def _():
            for shift in range(1, outer):
                grad_hop(2 * shift, c).start()

        grad_hop(1, c).start()

    def load_piece(p, k):
        slot = lax.rem(k, 2)
        source = landing[p] if p else grads
        return pltpu.make_async_copy(source.at[at(k)], back.at[slot, p], back_sem.at[slot, p])

    def share(shift):
        owner = lax.rem(chip - shift + outer, outer)
        rows = pl.ds(pl.multiple_of(owner * 2 * width + cluster * part, part), part)
        mine = pl.ds(pl.multiple_of(cluster * part, part), part)
        return remote(
            weight.at[rows], shares.at[shift, mine], share_send.at[shift], share_recv.at[shift], chip_at(-shift)
        )

    def spread(shift, source, peer):
        rows = pl.ds(pl.multiple_of(source * part, part), part)
        return remote(
            shares.at[shift, rows], shares.at[shift, rows],
            spread_send.at[shift], spread_recv.at[shift], peer, "clu",
        )

    def all_shares(shift):
        rows = pl.ds(0, len(others) * part)
        return remote(
            shares.at[shift, rows], shares.at[shift, rows], spread_send.at[shift], spread_recv.at[shift], others[0], "clu"
        )

    def block(p):
        half = core if p % 2 == 0 else 1 - core
        if p < 2:
            source = weight.at[pl.ds(pl.multiple_of((chip * 2 + half) * width, width), width)]
        else:
            source = shares.at[p // 2, pl.ds(pl.multiple_of(half * width, width), width)]
        if p % 2 == 0:
            return pltpu.make_async_copy(source, blocks_out.at[p], block_recv.at[p])
        return remote(source, blocks_out.at[p], block_send.at[p], block_recv.at[p], sibling)

    for copy in loads(0):
        copy.start()
    fixed = [
        pltpu.make_async_copy(source, target, fixed_sem.at[i])
        for i, (source, target) in enumerate([(segments, seg), (weight, mat), (bias, vec)])
    ]
    for copy in fixed:
        copy.start()
    load_cot(0).start()

    barrier = pltpu.get_barrier_semaphore()
    centre = clusters - 2 + core
    neighbours = [sibling] + [chip_at(shift) for shift in range(1, outer)]

    def greet(axis, peer):
        pl.semaphore_signal(barrier, inc=1, device_id={axis: peer}, device_id_type=MESH)

    for peer in neighbours:
        greet("col", peer)

    @pl.when(cluster == centre)
    def _():
        pl.semaphore_wait(barrier, len(neighbours) + len(others))
        for peer in others:
            greet("clu", peer)

    @pl.when(cluster != centre)
    def _():
        pl.semaphore_wait(barrier, len(neighbours))
        greet("clu", centre)

    for shift in range(1, outer):
        share(shift).start()
    block(0).start()
    block(1).start()
    fixed[0].wait()

    def aggregate_tile(k, carry):
        slot = lax.rem(k, 2)
        for copy in loads(k):
            copy.wait()

        @pl.when(k + 1 < count)
        def _():
            for copy in loads(k + 1):
                copy.start()

        for b in range(tile // BLOCK):
            part = pl.ds(b * BLOCK, BLOCK)
            stencil, inverse = stencil_of(adj[slot, part, :], seg[pl.ds(k * (tile // BLOCK) + b, 1), :])
            summed = jnp.dot(stencil, feat[slot, part, :], preferred_element_type=F32)
            target = pl.ds(pl.multiple_of(k * tile + b * BLOCK, BLOCK), BLOCK)
            sten[target, :] = stencil
            pieces[0][target, :] = (summed * inverse).astype(BF16)

        @pl.when(lax.rem(k, 2) == 1)
        def _():
            for shift in range(1, outer):
                hop(2 * shift, k // 2).start()
            hop(1, k // 2).start()

        return carry

    lax.fori_loop(0, count, aggregate_tile, 0)
    total[...] = jnp.zeros_like(total)
    fixed[1].wait()
    fixed[2].wait()
    blocks = [lax.rem(chip + p // 2, outer) * 2 + (core if p % 2 == 0 else 1 - core) for p in range(n)]

    def forward_tile(k):
        slot = lax.rem(k, 2)
        load_cot(k).wait()

        @pl.when(k + 1 < count)
        def _():
            load_cot(k + 1).start()

        @pl.when(lax.rem(k, 2) == 0)
        def _():
            several(2 * outer, send_sem.at[0], near_in.at[k // 2]).wait_recv()


        @pl.when(k >= 2)
        def _():
            store_grad(k - 2).wait()

        @pl.when((k >= 3) & (lax.rem(k, 2) == 1))
        def _():
            send_grad((k - 3) // 2)

        preact = None
        for p in range(n):
            source = pl.ds(pl.multiple_of(blocks[p] * width, width), width)
            term = jnp.dot(pieces[p][at(k), :], mat[source, :], preferred_element_type=F32)
            preact = term if preact is None else preact + term
        preact = preact + vec[...].astype(F32).reshape(1, width)
        grad_preact = jnp.where(preact > 0.0, cot[slot].astype(F32), 0.0)
        total[pl.ds(depth, 8), :] += jnp.sum(grad_preact.reshape(tile // 8, 8, width), axis=0)
        grad_preact = grad_preact.astype(BF16)
        grad[slot] = grad_preact

        store_grad(k).start()
        for p in range(n):
            target = pl.ds(pl.multiple_of(blocks[p] * width, width), width)
            total[target, :] += lax.dot_general(
                pieces[p][at(k), :], grad_preact, (((0,), (0,)), ((), ())), preferred_element_type=F32
            )
        activations[at(k), :] = jnp.maximum(preact, 0.0).astype(BF16)

    def step(k, carry):
        @pl.when((k < count) & (lax.rem(k, 2) == 0))
        def _():
            for shift in range(1, outer):
                hop(2 * shift, k // 2).wait_recv()
                hop(2 * shift + 1, k // 2).start()

        @pl.when((k == 2) & (cluster != centre))
        def _():
            pl.semaphore_wait(barrier, 1)

        @pl.when(k == 2)
        def _():
            for shift in range(1, outer):
                share(shift).wait_recv()
                for peer in others:
                    spread(shift, cluster, peer).start()

        @pl.when(k == 6)
        def _():
            for shift in range(1, outer):
                all_shares(shift).wait_recv()
                block(2 * shift).start()
                block(2 * shift + 1).start()

        @pl.when(k >= 1)
        def _():
            forward_tile(k - 1)

        return carry

    lax.fori_loop(0, count + 1, step, 0)
    sums = cluster_sum(total, summed_total, half_in, quarter_in, bias_in, sum_sems, clusters)
    sums.start()
    for k in (count - 2, count - 1):
        store_grad(k).wait()
    send_grad(count // 2 - 1)
    for p in range(1, n):
        several(count, send_sem.at[p], near_in.at[0]).wait_send()
    for p in range(1, n, 2):
        block(p).wait_send()
    for shift in range(1, outer):
        share(shift).wait_send()
        all_shares(shift).wait_send()
    for p in range(n):
        if p % 2:
            block(p).wait_recv()
        else:
            block(p).wait()
    copies = [
        pltpu.make_async_copy(blocks_out.at[p], mat.at[pl.ds(p * width, width)], block_send.at[p - p % 2])
        for p in range(0, n, 2)
    ] + [
        pltpu.make_async_copy(blocks_out.at[p], mat.at[pl.ds(p * width, width)], block_recv.at[p])
        for p in range(1, n, 2)
    ]
    for copy in copies:
        copy.start()
    for copy in copies:
        copy.wait()

    def backward_tile(k):
        slot = lax.rem(k, 2)
        for p in range(n):
            load_piece(p, k).wait()
        scaled[at(k), :] = scale(back_through(lambda p: back[slot, p], range(n), mat), sten[at(k), :])

    def moment(r):
        return max(r * 512 // tile, 0)

    def back_step(k, carry):
        @pl.when(k >= 1)
        def _():
            backward_tile(k - 1)

        @pl.when((k < early) & (lax.rem(k, 2) == 0))
        def _():
            for shift in range(1, outer):
                grad_hop(2 * shift, k // 2).wait_recv()
                grad_hop(2 * shift + 1, k // 2).start()
            several(2 * outer, grad_out.at[0], grad_near.at[k // 2]).wait_recv()
            for p in range(n):
                load_piece(p, k).start()
                load_piece(p, k + 1).start()

        for r in range(sums.rounds):
            if moment(r) <= early:
                pl.when(k == moment(r))(functools.partial(sums.advance, r))
        if moment(sums.last) <= early:
            pl.when(k == moment(sums.last))(sums.finish)
        return carry

    lax.fori_loop(0, early + 1, back_step, 0)
    for r in range(sums.rounds):
        if moment(r) > early:
            sums.advance(r)
    if moment(sums.last) > early:
        sums.finish()
    def late_step(c, carry):
        several(2, grad_out.at[0], grad_near.at[c]).wait_recv()

        @pl.when(core == 1)
        def _():
            for shift in range(1, outer):
                grad_hop(2 * shift, c).wait_recv()

        return carry

    for p in range(3, n, 2):
        several(early, grad_out.at[p], grad_near.at[0]).wait_send()
    several(count, grad_out.at[1], grad_near.at[0]).wait_send()
    lax.fori_loop(early // 2, count // 2, late_step, 0)

    @pl.when(core == 0)
    def _():
        for p in range(2, n, 2):
            several(early, grad_out.at[p], grad_near.at[0]).wait_send()

    @pl.when(core == 1)
    def _():
        for p in range(2, n, 2):
            several(count, grad_out.at[p], grad_near.at[0]).wait_send()


def exchange(features, adjacency, cotangent, segments, weight, bias, n, clusters, early, tile):
    rows, width = features.shape
    depth = weight.shape[0]
    count, outer = rows // tile, n // 2
    parts, high = cluster_sum.PARTS, clusters // 2
    dma = pltpu.SemaphoreType.DMA
    array = jax.ShapeDtypeStruct
    return pl.pallas_call(
        functools.partial(exchange_kernel, n, clusters, early, tile),
        in_specs=[HBM] * 6,
        out_specs=[VMEM] * 5 + [HBM] * (n + 1),
        out_shape=[
            pltpu.VMEM((rows, width), BF16),
            pltpu.VMEM((rows, width), BF16),
            pltpu.VMEM((depth + 8, width), F32),
            pltpu.VMEM((rows, BLOCK), BF16),
            pltpu.VMEM((depth, width), BF16),
            array((n, width, width), BF16),
        ]
        + [array((rows, width), BF16)] * n,
        scratch_shapes=[pltpu.VMEM((rows, width), BF16)] * (n - 2)
        + [
            pltpu.VMEM((2, tile, width), BF16),
            pltpu.VMEM((2, tile, BLOCK), jnp.int32),
            pltpu.VMEM((2, tile, width), BF16),
            pltpu.VMEM((2, tile, width), BF16),
            pltpu.VMEM(segments.shape, jnp.int32),
            pltpu.VMEM((width,), BF16),
            pltpu.VMEM((depth + 8, width), F32),
            pltpu.VMEM((outer, 2 * width, width), BF16),
            pltpu.VMEM((2, n, tile, width), BF16),
            dma((2, 2)),
            dma((2,)),
            dma((2,)),
            dma((3,)),
            dma((n,)),
            dma((outer - 1, count // 2)),
            dma((count // 2,)),
            dma((n,)),
            dma((outer - 1, count // 2)),
            dma((count // 2,)),
            dma((2, n)),
            dma((outer,)),
            dma((outer,)),
            dma((outer,)),
            dma((outer,)),
            dma((n,)),
            dma((n,)),
            pltpu.VMEM((parts, depth // parts // 2, width), F32),
            pltpu.VMEM((parts, high, depth // parts // 2 // high, width), F32),
            pltpu.VMEM((clusters, 8, width), F32),
            [dma((5,)), dma((parts,)), dma((parts,)), dma((parts,)), dma((1,)), dma((1,))],
        ],
        compiler_params=pltpu.CompilerParams(
            collective_id=0, has_side_effects=True, vmem_limit_bytes=38 << 20
        ),
    )(*[pltpu.with_memory_space_constraint(x, pltpu.HBM) for x in (features, adjacency, cotangent, segments, weight, bias)])


def stencil_rows(stencil, scaled, slots, slot, first, start, span):
    for b in range(span // BLOCK):
        source = pl.multiple_of(start + b * BLOCK, BLOCK)
        slots[slot, pl.ds(b * BLOCK, BLOCK), :] = jnp.dot(
            stencil[pl.ds(first + source, BLOCK), :], scaled[pl.ds(source, BLOCK), :], preferred_element_type=F32
        )


def finish_kernel(
    early, span, activations, scaled, total, stencil,
    grad_features, out, grad_weight, grad_bias, slots, row, slot_sem, fixed_sem,
):
    depth = total.shape[0] - 8
    count = early // span
    row[...] = jnp.sum(total[pl.ds(depth, 8), :], axis=0, keepdims=True)
    fixed = [
        pltpu.make_async_copy(activations, out, fixed_sem.at[0]),
        pltpu.make_async_copy(total.at[pl.ds(0, depth)], grad_weight, fixed_sem.at[1]),
        pltpu.make_async_copy(row, grad_bias, fixed_sem.at[2]),
    ]
    for copy in fixed:
        copy.start()

    def store(k):
        slot = lax.rem(k, SLOTS)
        target = pl.ds(pl.multiple_of(k * span, span), span)
        return pltpu.make_async_copy(slots.at[slot], grad_features.at[target], slot_sem.at[slot])

    def step(k, carry):
        @pl.when(k >= SLOTS)
        def _():
            store(k - SLOTS).wait()

        stencil_rows(stencil, scaled, slots, lax.rem(k, SLOTS), 0, k * span, span)
        store(k).start()
        return carry

    lax.fori_loop(0, count, step, 0)
    for k in range(max(count - SLOTS, 0), count):
        store(k).wait()
    for copy in fixed:
        copy.wait()


def finish(activations, scaled, total, stencil, early, tile):
    rows, width = scaled.shape
    depth = total.shape[0] - 8
    dma = pltpu.SemaphoreType.DMA
    return pl.pallas_call(
        functools.partial(finish_kernel, early * tile, 2 * tile),
        in_specs=[VMEM] * 4,
        out_specs=[HBM] * 4,
        out_shape=[
            jax.ShapeDtypeStruct((rows, width), F32),
            jax.ShapeDtypeStruct((rows, width), BF16),
            jax.ShapeDtypeStruct((depth, width), F32),
            jax.ShapeDtypeStruct((1, width), F32),
        ],
        scratch_shapes=[
            pltpu.VMEM((SLOTS, 2 * tile, width), F32),
            pltpu.VMEM((1, width), F32),
            dma((SLOTS,)),
            dma((3,)),
        ],
        cost_estimate=pl.CostEstimate(
            flops=2 * rows * BLOCK * width, bytes_accessed=6 * rows * width + 4 * depth * width, transcendentals=0
        ),
        compiler_params=pltpu.CompilerParams(vmem_limit_bytes=12 << 20),
    )(activations, scaled, total, stencil)


def late_kernel(n, early, tile, *refs):
    grads, landing = refs[0], (None,) + refs[1:n]
    sten, mat, scaled, pieces, load_sem, far_out, far_in, near_out, near_in = refs[n + 1 :]
    outer = n // 2
    rows, width = grads.shape
    late = rows // tile - early
    kept = pl.ds(early * tile, late * tile)
    me = lax.axis_index("col")
    chip, core = me // 2, lax.rem(me, 2)
    sibling = chip * 2 + 1 - core

    def chip_at(shift):
        return lax.rem(chip + shift + outer, outer) * 2 + core

    def at(j):
        return pl.ds(pl.multiple_of(j * tile, tile), tile)

    def remote(source, target, send, recv, device):
        return pltpu.make_async_remote_copy(
            src_ref=source, dst_ref=target, send_sem=send, recv_sem=recv,
            device_id={"col": device}, device_id_type=MESH,
        )

    def load(p, part):
        source = landing[p] if p else grads
        first, size = ((0, 2 * tile), (2 * tile, (late - 2) * tile))[part]
        here = source.at[pl.ds(early * tile + first, size)]
        return pltpu.make_async_copy(here, pieces.at[p, pl.ds(first, size)], load_sem.at[part, p])

    def far(p, j):
        source = grads.at[pl.ds(pl.multiple_of((early + j) * tile, tile), tile)]
        return remote(source, pieces.at[p, at(j)], far_out.at[p], far_in.at[p // 2 - 1, j], chip_at(-(p // 2)))

    def near(p, j):
        return remote(pieces.at[p - 1, at(j)], pieces.at[p, at(j)], near_out.at[p], near_in.at[p // 2 - 1, j], sibling)

    barrier = pltpu.get_barrier_semaphore()
    for part in range(2):
        for p in range(2):
            load(p, part).start()

    @pl.when(core == 0)
    def _():
        for shift in range(1, outer):
            pl.semaphore_signal(barrier, inc=1, device_id={"col": chip_at(shift)}, device_id_type=MESH)
        pl.semaphore_wait(barrier, outer - 1)
        for j in range(late):
            for p in range(2, n, 2):
                far(p, j).start()
        pl.semaphore_signal(barrier, inc=1, device_id={"col": sibling}, device_id_type=MESH)
        pl.semaphore_wait(barrier, 1)

    @pl.when(core == 1)
    def _():
        for part in range(2):
            for p in range(2, n, 2):
                load(p, part).start()
        pl.semaphore_wait(barrier, 1)
        pl.semaphore_signal(barrier, inc=1, device_id={"col": sibling}, device_id_type=MESH)
        for part in range(2):
            for p in range(2, n, 2):
                load(p, part).wait()
            for j in ((0, 1), range(2, late))[part]:
                for p in range(3, n, 2):
                    near(p, j).start()

    def loaded(part):
        for p in range(2):
            load(p, part).wait()

    def take(j):
        @pl.when(core == 0)
        def _():
            for p in range(2, n, 2):
                far(p, j).wait_recv()
                near(p + 1, j).start()

    def wait_near(j):
        for p in range(3, n, 2):
            near(p, j).wait_recv()

    def products(j, size, numbers):
        rows = pl.ds(pl.multiple_of(j * tile, tile), size * tile)
        return back_through(lambda p: pieces[p, rows, :], numbers, mat)

    def store(j, size, value):
        rows = pl.ds(pl.multiple_of((early + j) * tile, tile), size * tile)
        scaled[pl.ds(pl.multiple_of(j * tile, tile), size * tile), :] = scale(value, sten[rows, :])

    def step(g, carry):
        for j in range(GROUP):
            take(GROUP * g + j)
        for j in range(GROUP):
            wait_near(GROUP * g + j)
        store(GROUP * g, GROUP, products(GROUP * g, GROUP, range(n)))
        return carry

    loaded(0)
    lax.fori_loop(0, 2 // GROUP, step, 0)
    loaded(1)
    lax.fori_loop(2 // GROUP, (late - 2) // GROUP, step, 0)
    last = late - 1
    take(last - 1)
    wait_near(last - 1)
    store(last - 1, 1, products(last - 1, 1, range(n)))
    first = [0, 1] + [2 * shift + 1 - core for shift in range(1, outer)]

    @pl.when(core == 0)
    def _():
        wait_near(last)

    value = products(last, 1, first)
    take(last)

    @pl.when(core == 1)
    def _():
        wait_near(last)

    store(last, 1, value + products(last, 1, [2 * shift + core for shift in range(1, outer)]))

    @pl.when(core == 0)
    def _():
        for p in range(2, n, 2):
            remote(grads.at[kept], pieces.at[p], far_out.at[p], far_in.at[p // 2 - 1, 0], chip_at(-(p // 2))).wait_send()

    for p in range(3, n, 2):
        remote(pieces.at[p - 1], pieces.at[p], near_out.at[p], near_in.at[p // 2 - 1, 0], sibling).wait_send()


def exchange_late(grads, landing, earlier, stencil, blocks, n, early, tile):
    rows, width = grads.shape
    late, outer = rows // tile - early, n // 2
    dma = pltpu.SemaphoreType.DMA
    far = [pltpu.with_memory_space_constraint(x, pltpu.HBM) for x in (grads, *landing, earlier)]
    return pl.pallas_call(
        functools.partial(late_kernel, n, early, tile),
        in_specs=[HBM] * (n + 1) + [VMEM] * 2,
        out_specs=VMEM,
        out_shape=pltpu.VMEM((late * tile, width), BF16),
        scratch_shapes=[
            pltpu.VMEM((n, late * tile, width), BF16),
            dma((2, n)),
            dma((n,)),
            dma((outer - 1, late)),
            dma((n,)),
            dma((outer - 1, late)),
        ],
        compiler_params=pltpu.CompilerParams(
            collective_id=1, has_side_effects=True, vmem_limit_bytes=20 << 20
        ),
    )(*far, stencil, blocks)


def finish_late_kernel(first, span, scaled, stencil, _, grad_features, slots, sem):
    count = scaled.shape[0] // span

    def store(k):
        return pltpu.make_async_copy(slots.at[k], grad_features.at[pl.ds(first + k * span, span)], sem.at[k])

    for k in range(count):
        stencil_rows(stencil, scaled, slots, k, first, k * span, span)
        store(k).start()
    for k in range(count):
        store(k).wait()


def finish_late(scaled, stencil, grad_features, early, tile):
    late, width = scaled.shape
    span = tile
    return pl.pallas_call(
        functools.partial(finish_late_kernel, early * tile, span),
        in_specs=[VMEM] * 2 + [HBM],
        out_specs=HBM,
        out_shape=jax.ShapeDtypeStruct(grad_features.shape, F32),
        input_output_aliases={2: 0},
        scratch_shapes=[pltpu.VMEM((late // span, span, width), F32), pltpu.SemaphoreType.DMA((late // span,))],
        cost_estimate=pl.CostEstimate(
            flops=2 * late * BLOCK * width, bytes_accessed=4 * late * width, transcendentals=0
        ),
        compiler_params=pltpu.CompilerParams(vmem_limit_bytes=12 << 20),
    )(scaled, stencil, grad_features)


def build(n, clusters):
    def local(features, weight, bias, adjacency, segments, cotangent):
        tile = 256 if n <= 4 else 512
        early = features.shape[0] // tile - TAIL
        activations, scaled, total, stencil, blocks, _, grads, *landing = exchange(
            features, adjacency, cotangent, segments, weight, bias, n, clusters, early, tile
        )
        grad_features, out, grad_weight, grad_bias = finish(activations, scaled, total, stencil, early, tile)
        scaled = exchange_late(grads, landing, grad_bias, stencil, blocks, n, early, tile)
        grad_features = finish_late(scaled, stencil, grad_features, early, tile)
        return (out, grad_features, grad_weight, grad_bias.reshape(-1))

    return local


def solution(mesh):
    return jax.shard_map(
        build(mesh.shape["col"], mesh.shape["clu"]),
        mesh=mesh,
        in_specs=(
            P("clu", "col"),
            P(None, "col"),
            P("col"),
            P("clu", None),
            P("clu", None),
            P("clu", "col"),
        ),
        out_specs=(P("clu", "col"), P("clu", "col"), P(None, "col"), P("col")),
        check_vma=False,
    )
```

```python
import functools

import jax
import jax.numpy as jnp
from jax import lax
from jax.experimental import pallas as pl
from jax.experimental.pallas import tpu as pltpu
from jax.sharding import PartitionSpec as P

BLOCK = 128
SLOTS = 4
TAIL = 6
GROUP = 2
F32 = jnp.float32
BF16 = jnp.bfloat16
MESH = pl.DeviceIdType.MESH
HBM = pl.BlockSpec(memory_space=pltpu.HBM)
VMEM = pl.BlockSpec(memory_space=pltpu.VMEM)


def stencil_of(adjacency, segment):
    columns = jnp.broadcast_to(segment, (BLOCK, BLOCK))
    links = jnp.where(columns == columns.T, adjacency, 0).astype(F32)
    inverse = 1.0 / (jnp.sum(links, axis=1, keepdims=True) + 1.0)
    row = lax.broadcasted_iota(jnp.int32, (BLOCK, BLOCK), 0)
    column = lax.broadcasted_iota(jnp.int32, (BLOCK, BLOCK), 1)
    return (links + jnp.where(row == column, 2.0, 0.0)).astype(BF16), inverse


def back_through(piece, numbers, blocks):
    width = blocks.shape[1]
    value = None
    for p in numbers:
        block = blocks[pl.ds(pl.multiple_of(p * width, width), width), :]
        term = lax.dot_general(piece(p), block, (((1,), (1,)), ((), ())), preferred_element_type=F32)
        value = term if value is None else value + term
    return value


def scale(value, stencil):
    inverse = 1.0 / (jnp.sum(stencil.astype(F32), axis=1, keepdims=True) - 1.0)
    return (value.astype(BF16).astype(F32) * inverse).astype(BF16)


class cluster_sum:
    PARTS = 4
    BACK = (5, 7, 8, 9)
    rounds = 10
    last = 12

    def __init__(self, total, result, half_in, quarter_in, bias_in, sems, clusters):
        self.result = result
        self.total, self.half_in, self.quarter_in, self.bias_in, self.sems = total, half_in, quarter_in, bias_in, sems
        self.clusters, self.high = clusters, clusters // 2
        self.depth = total.shape[0] - 8
        self.half = self.depth // self.PARTS // 2
        self.quarter = self.half // self.high
        self.me = lax.axis_index("clu")
        self.z, self.x = self.me // 2, lax.rem(self.me, 2)
        self.others = [lax.rem(self.me + d, clusters) for d in range(1, clusters)]
        self.levels = [lax.rem(self.z + d, self.high) for d in range(1, self.high)]

    def rows_of_half(self, c, x):
        return pl.ds(pl.multiple_of(c * 2 * self.half + x * self.half, self.half), self.half)

    def rows_of_quarter(self, c, q):
        start = c * 2 * self.half + self.x * self.half + q * self.quarter
        return pl.ds(pl.multiple_of(start, self.quarter), self.quarter)

    def copy(self, source, target, kind, recv, device):
        return pltpu.make_async_remote_copy(
            src_ref=source, dst_ref=target, send_sem=self.sems[0].at[kind],
            recv_sem=self.sems[1 + kind].at[recv], device_id={"clu": device}, device_id_type=MESH,
        )

    def several(self, rows, kind, recv=0):
        return self.copy(self.total.at[pl.ds(0, rows)], self.result.at[pl.ds(0, rows)], kind, recv, self.others[0])

    def give_half(self, c):
        rows = self.rows_of_half(c, 1 - self.x)
        return self.copy(self.total.at[rows], self.half_in.at[c], 0, c, self.z * 2 + 1 - self.x)

    def give_quarter(self, c, source, target):
        rows = self.rows_of_quarter(c, target)
        return self.copy(
            self.total.at[rows], self.quarter_in.at[c, source], 1, c, target * 2 + self.x
        )

    def return_quarter(self, c, source, target):
        rows = self.rows_of_quarter(c, source)
        return self.copy(
            self.result.at[rows], self.result.at[rows], 2, c, target * 2 + self.x
        )

    def return_half(self, c, x):
        rows = self.rows_of_half(c, x)
        return self.copy(self.result.at[rows], self.result.at[rows], 3, 0, self.z * 2 + 1 - self.x)

    def give_bias(self, source, target):
        return self.copy(
            self.total.at[pl.ds(self.depth, 8)], self.bias_in.at[source], 4, 0, target
        )

    def start(self):
        for c in range(self.PARTS):
            self.give_half(c).start()
        for other in self.others:
            self.give_bias(self.me, other).start()

    def advance(self, k):
        total = self.total
        if k < self.PARTS:
            self.give_half(k).wait_recv()
            total[self.rows_of_half(k, self.x), :] += self.half_in[k]
            for level in self.levels:
                self.give_quarter(k, self.z, level).start()
        c = k - 2
        if 0 <= c < self.PARTS:
            rows = self.rows_of_quarter(c, self.z)
            self.several(len(self.levels) * self.quarter, 1, c).wait_recv()
            value = total[rows, :]
            for level in self.levels:
                value = value + self.quarter_in[c, level]
            self.result[rows, :] = value
            for level in self.levels:
                self.return_quarter(c, self.z, level).start()
        if k in self.BACK:
            c = self.BACK.index(k)
            self.several(len(self.levels) * self.quarter, 2, c).wait_recv()
            self.return_half(c, self.x).start()

    def finish(self):
        halves = self.PARTS * self.half
        quarters = self.PARTS * len(self.levels) * self.quarter
        for kind, rows in enumerate((halves, quarters, quarters, halves, 8 * len(self.others))):
            self.several(rows, kind).wait_send()
        self.several(halves, 3).wait_recv()
        self.several(8 * len(self.others), 4).wait_recv()
        value = self.total[pl.ds(self.depth, 8), :]
        for other in self.others:
            value = value + self.bias_in[other]
        self.result[pl.ds(self.depth, 8), :] = value


def exchange_kernel(
    n, clusters, early, tile, features, adjacency, cotangent, segments, weight, bias,
    activations, scaled, summed_total, sten, mat, blocks_out, grads, *rest,
):
    landing = (None,) + rest[: n - 1]
    pieces = list(rest[n - 1 : 2 * n - 3])
    pieces = pieces[:1] + [activations] + pieces[1:] + [scaled]
    (feat, adj, cot, grad, seg, vec, total, shares, back, load_sem, cot_sem, grad_sem,
     fixed_sem, send_sem, far_in, near_in, grad_out, grad_far, grad_near, back_sem, share_send, share_recv, spread_send, spread_recv,
     block_send, block_recv, half_in, quarter_in, bias_in, sum_sems) = rest[2 * n - 3 :]
    outer = n // 2
    rows, width = features.shape
    depth = mat.shape[0]
    count = rows // tile
    me, cluster = lax.axis_index("col"), lax.axis_index("clu")
    chip, core = me // 2, lax.rem(me, 2)
    sibling = chip * 2 + 1 - core
    part = 2 * width // clusters
    others = [lax.rem(cluster + d, clusters) for d in range(1, clusters)]

    def chip_at(shift):
        return lax.rem(chip + shift + outer, outer) * 2 + core

    def at(k):
        return pl.ds(pl.multiple_of(k * tile, tile), tile)

    def pair(c):
        return pl.ds(pl.multiple_of(c * 2 * tile, 2 * tile), 2 * tile)

    def loads(k):
        slot = lax.rem(k, 2)
        return (
            pltpu.make_async_copy(features.at[at(k)], feat.at[slot], load_sem.at[0, slot]),
            pltpu.make_async_copy(adjacency.at[at(k)], adj.at[slot], load_sem.at[1, slot]),
        )

    def load_cot(k):
        slot = lax.rem(k, 2)
        return pltpu.make_async_copy(cotangent.at[at(k)], cot.at[slot], cot_sem.at[slot])

    def store_grad(k):
        slot = lax.rem(k, 2)
        return pltpu.make_async_copy(grad.at[slot], grads.at[at(k)], grad_sem.at[slot])

    def remote(source, target, send, recv, device, axis="col"):
        return pltpu.make_async_remote_copy(
            src_ref=source, dst_ref=target, send_sem=send, recv_sem=recv,
            device_id={axis: device}, device_id_type=MESH,
        )

    def hop(p, c):
        source = 0 if p % 2 == 0 else p - 1
        device = chip_at(-(p // 2)) if p % 2 == 0 else sibling
        arrival = far_in.at[p // 2 - 1, c] if p % 2 == 0 else near_in.at[c]
        return remote(pieces[source].at[pair(c)], pieces[p].at[pair(c)], send_sem.at[p], arrival, device)

    def grad_hop(p, c):
        rows = pair(c)
        source = grads if p < 2 or p % 2 == 0 else landing[p - 1]
        device = chip_at(-(p // 2)) if p % 2 == 0 else sibling
        arrival = grad_far.at[p // 2 - 1, c] if p % 2 == 0 else grad_near.at[c]
        return remote(source.at[rows], landing[p].at[rows], grad_out.at[p], arrival, device)

    def several(tiles, send, arrival):
        span = pl.ds(0, tiles * tile)
        return remote(grads.at[span], landing[1].at[span], send, arrival, sibling)

    border = early // 2 - 1

    def border_hop(p, i):
        rows, c = at(early - 2 + i), (border, count // 2)[i]
        source = landing[p - 1] if p % 2 else grads
        device = sibling if p % 2 else chip_at(-(p // 2))
        arrival = grad_near.at[c] if p % 2 else grad_far.at[p // 2 - 1, c]
        return remote(source.at[rows], landing[p].at[rows], grad_out.at[p], arrival, device)

    def pass_border(i):
        for p in range(2, n, 2):
            border_hop(p, i).wait_recv()
            border_hop(p + 1, i).start()
        several(outer - 1 + 2 * (1 - i), grad_out.at[0], grad_near.at[(border, count // 2)[i]]).wait_recv()
        for p in range(n):
            load_piece(p, early - 2 + i).start()

    def send_grad(c):
        @pl.when(c == border)
        def _():
            for i in range(2):
                for p in range(2, n, 2):
                    border_hop(p, i).start()

        @pl.when((c < border) | ((core == 1) & (c > border)))
        def _():
            for shift in range(1, outer):
                grad_hop(2 * shift, c).start()

        grad_hop(1, c).start()

    def load_piece(p, k):
        slot = lax.rem(k, 2)
        source = landing[p] if p else grads
        return pltpu.make_async_copy(source.at[at(k)], back.at[slot, p], back_sem.at[slot, p])

    def share(shift):
        owner = lax.rem(chip - shift + outer, outer)
        rows = pl.ds(pl.multiple_of(owner * 2 * width + cluster * part, part), part)
        mine = pl.ds(pl.multiple_of(cluster * part, part), part)
        return remote(
            weight.at[rows], shares.at[shift, mine], share_send.at[shift], share_recv.at[shift], chip_at(-shift)
        )

    def spread(shift, source, peer):
        rows = pl.ds(pl.multiple_of(source * part, part), part)
        return remote(
            shares.at[shift, rows], shares.at[shift, rows],
            spread_send.at[shift], spread_recv.at[shift], peer, "clu",
        )

    def all_shares(shift):
        rows = pl.ds(0, len(others) * part)
        return remote(
            shares.at[shift, rows], shares.at[shift, rows], spread_send.at[shift], spread_recv.at[shift], others[0], "clu"
        )

    def block(p):
        half = core if p % 2 == 0 else 1 - core
        if p < 2:
            source = weight.at[pl.ds(pl.multiple_of((chip * 2 + half) * width, width), width)]
        else:
            source = shares.at[p // 2, pl.ds(pl.multiple_of(half * width, width), width)]
        if p % 2 == 0:
            return pltpu.make_async_copy(source, blocks_out.at[p], block_recv.at[p])
        return remote(source, blocks_out.at[p], block_send.at[p], block_recv.at[p], sibling)

    barrier = pltpu.get_barrier_semaphore()
    centre = clusters - 2 + core
    neighbours = [sibling] + [chip_at(shift) for shift in range(1, outer)]

    def greet(axis, peer):
        pl.semaphore_signal(barrier, inc=1, device_id={axis: peer}, device_id_type=MESH)

    for peer in neighbours:
        greet("col", peer)

    for copy in loads(0):
        copy.start()
    fixed = [
        pltpu.make_async_copy(source, target, fixed_sem.at[i])
        for i, (source, target) in enumerate([(segments, seg), (weight, mat), (bias, vec)])
    ]
    for copy in fixed:
        copy.start()
    load_cot(0).start()

    @pl.when(cluster == centre)
    def _():
        pl.semaphore_wait(barrier, len(neighbours) + len(others))
        for peer in others:
            greet("clu", peer)

    @pl.when(cluster != centre)
    def _():
        pl.semaphore_wait(barrier, len(neighbours))

    for shift in range(1, outer):
        share(shift).start()
    pl.when(cluster != centre)(functools.partial(greet, "clu", centre))
    block(0).start()
    block(1).start()
    fixed[0].wait()

    def aggregate_tile(k, carry):
        slot = lax.rem(k, 2)
        for copy in loads(k):
            copy.wait()

        @pl.when(k + 1 < count)
        def _():
            for copy in loads(k + 1):
                copy.start()

        for b in range(tile // BLOCK):
            part = pl.ds(b * BLOCK, BLOCK)
            stencil, inverse = stencil_of(adj[slot, part, :], seg[pl.ds(k * (tile // BLOCK) + b, 1), :])
            summed = jnp.dot(stencil, feat[slot, part, :], preferred_element_type=F32)
            target = pl.ds(pl.multiple_of(k * tile + b * BLOCK, BLOCK), BLOCK)
            sten[target, :] = stencil
            pieces[0][target, :] = (summed * inverse).astype(BF16)

        @pl.when(lax.rem(k, 2) == 1)
        def _():
            for shift in range(1, outer):
                hop(2 * shift, k // 2).start()
            hop(1, k // 2).start()

        return carry

    lax.fori_loop(0, count, aggregate_tile, 0)
    total[...] = jnp.zeros_like(total)
    fixed[1].wait()
    fixed[2].wait()
    blocks = [lax.rem(chip + p // 2, outer) * 2 + (core if p % 2 == 0 else 1 - core) for p in range(n)]

    def forward_tile(k):
        slot = lax.rem(k, 2)
        load_cot(k).wait()

        @pl.when(k + 1 < count)
        def _():
            load_cot(k + 1).start()

        @pl.when(lax.rem(k, 2) == 0)
        def _():
            several(2 * outer, send_sem.at[0], near_in.at[k // 2]).wait_recv()


        @pl.when(k >= 2)
        def _():
            store_grad(k - 2).wait()

        @pl.when((k >= 3) & (lax.rem(k, 2) == 1))
        def _():
            send_grad((k - 3) // 2)

        preact = None
        for p in range(n):
            source = pl.ds(pl.multiple_of(blocks[p] * width, width), width)
            term = jnp.dot(pieces[p][at(k), :], mat[source, :], preferred_element_type=F32)
            preact = term if preact is None else preact + term
        preact = preact + vec[...].astype(F32).reshape(1, width)
        grad_preact = jnp.where(preact > 0.0, cot[slot].astype(F32), 0.0)
        total[pl.ds(depth, 8), :] += jnp.sum(grad_preact.reshape(tile // 8, 8, width), axis=0)
        grad_preact = grad_preact.astype(BF16)
        grad[slot] = grad_preact

        store_grad(k).start()
        for p in range(n):
            target = pl.ds(pl.multiple_of(blocks[p] * width, width), width)
            total[target, :] += lax.dot_general(
                pieces[p][at(k), :], grad_preact, (((0,), (0,)), ((), ())), preferred_element_type=F32
            )
        activations[at(k), :] = jnp.maximum(preact, 0.0).astype(BF16)

    def step(k, carry):
        @pl.when((k < count) & (lax.rem(k, 2) == 0))
        def _():
            for shift in range(1, outer):
                hop(2 * shift, k // 2).wait_recv()
                hop(2 * shift + 1, k // 2).start()

        @pl.when((k == 2) & (cluster != centre))
        def _():
            pl.semaphore_wait(barrier, 1)

        @pl.when(k == 2)
        def _():
            for shift in range(1, outer):
                share(shift).wait_recv()
                for peer in others:
                    spread(shift, cluster, peer).start()

        @pl.when(k == 6)
        def _():
            for shift in range(1, outer):
                all_shares(shift).wait_recv()
                block(2 * shift).start()
                block(2 * shift + 1).start()

        @pl.when(k >= 1)
        def _():
            forward_tile(k - 1)

        return carry

    lax.fori_loop(0, count + 1, step, 0)
    sums = cluster_sum(total, summed_total, half_in, quarter_in, bias_in, sum_sems, clusters)
    sums.start()
    for k in (count - 2, count - 1):
        store_grad(k).wait()
    send_grad(count // 2 - 1)
    for p in range(1, n):
        several(count, send_sem.at[p], near_in.at[0]).wait_send()
    for p in range(1, n, 2):
        block(p).wait_send()
    for shift in range(1, outer):
        share(shift).wait_send()
        all_shares(shift).wait_send()
    for p in range(n):
        if p % 2:
            block(p).wait_recv()
        else:
            block(p).wait()
    copies = [
        pltpu.make_async_copy(blocks_out.at[p], mat.at[pl.ds(p * width, width)], block_send.at[p - p % 2])
        for p in range(0, n, 2)
    ] + [
        pltpu.make_async_copy(blocks_out.at[p], mat.at[pl.ds(p * width, width)], block_recv.at[p])
        for p in range(1, n, 2)
    ]
    for copy in copies:
        copy.start()
    for copy in copies:
        copy.wait()

    def backward_tile(k):
        slot = lax.rem(k, 2)
        for p in range(n):
            load_piece(p, k).wait()
        scaled[at(k), :] = scale(back_through(lambda p: back[slot, p], range(n), mat), sten[at(k), :])

    def moment(r):
        return max(r * 512 // tile, 0)

    def back_step(k, carry):
        @pl.when(k >= 1)
        def _():
            backward_tile(k - 1)

        for i in range(2):
            pl.when(k == early - 2 + i)(functools.partial(pass_border, i))

        @pl.when((k < early - 2) & (lax.rem(k, 2) == 0))
        def _():
            for shift in range(1, outer):
                grad_hop(2 * shift, k // 2).wait_recv()
                grad_hop(2 * shift + 1, k // 2).start()
            several(2 * outer, grad_out.at[0], grad_near.at[k // 2]).wait_recv()
            for p in range(n):
                load_piece(p, k).start()
                load_piece(p, k + 1).start()

        for r in range(sums.rounds):
            if moment(r) <= early:
                pl.when(k == moment(r))(functools.partial(sums.advance, r))
        if moment(sums.last) <= early:
            pl.when(k == moment(sums.last))(sums.finish)
        return carry

    lax.fori_loop(0, early + 1, back_step, 0)
    for r in range(sums.rounds):
        if moment(r) > early:
            sums.advance(r)
    if moment(sums.last) > early:
        sums.finish()
    def late_step(c, carry):
        several(2, grad_out.at[0], grad_near.at[c]).wait_recv()

        @pl.when(core == 1)
        def _():
            for shift in range(1, outer):
                grad_hop(2 * shift, c).wait_recv()

        return carry

    for p in range(3, n, 2):
        several(early, grad_out.at[p], grad_near.at[0]).wait_send()
    several(count, grad_out.at[1], grad_near.at[0]).wait_send()
    lax.fori_loop(early // 2, count // 2, late_step, 0)

    @pl.when(core == 0)
    def _():
        for p in range(2, n, 2):
            several(early, grad_out.at[p], grad_near.at[0]).wait_send()

    @pl.when(core == 1)
    def _():
        for p in range(2, n, 2):
            several(count, grad_out.at[p], grad_near.at[0]).wait_send()


def exchange(features, adjacency, cotangent, segments, weight, bias, n, clusters, early, tile):
    rows, width = features.shape
    depth = weight.shape[0]
    count, outer = rows // tile, n // 2
    parts, high = cluster_sum.PARTS, clusters // 2
    dma = pltpu.SemaphoreType.DMA
    array = jax.ShapeDtypeStruct
    return pl.pallas_call(
        functools.partial(exchange_kernel, n, clusters, early, tile),
        in_specs=[HBM] * 6,
        out_specs=[VMEM] * 5 + [HBM] * (n + 1),
        out_shape=[
            pltpu.VMEM((rows, width), BF16),
            pltpu.VMEM((rows, width), BF16),
            pltpu.VMEM((depth + 8, width), F32),
            pltpu.VMEM((rows, BLOCK), BF16),
            pltpu.VMEM((depth, width), BF16),
            array((n, width, width), BF16),
        ]
        + [array((rows, width), BF16)] * n,
        scratch_shapes=[pltpu.VMEM((rows, width), BF16)] * (n - 2)
        + [
            pltpu.VMEM((2, tile, width), BF16),
            pltpu.VMEM((2, tile, BLOCK), jnp.int32),
            pltpu.VMEM((2, tile, width), BF16),
            pltpu.VMEM((2, tile, width), BF16),
            pltpu.VMEM(segments.shape, jnp.int32),
            pltpu.VMEM((width,), BF16),
            pltpu.VMEM((depth + 8, width), F32),
            pltpu.VMEM((outer, 2 * width, width), BF16),
            pltpu.VMEM((2, n, tile, width), BF16),
            dma((2, 2)),
            dma((2,)),
            dma((2,)),
            dma((3,)),
            dma((n,)),
            dma((outer - 1, count // 2)),
            dma((count // 2,)),
            dma((n,)),
            dma((outer - 1, count // 2 + 1)),
            dma((count // 2 + 1,)),
            dma((2, n)),
            dma((outer,)),
            dma((outer,)),
            dma((outer,)),
            dma((outer,)),
            dma((n,)),
            dma((n,)),
            pltpu.VMEM((parts, depth // parts // 2, width), F32),
            pltpu.VMEM((parts, high, depth // parts // 2 // high, width), F32),
            pltpu.VMEM((clusters, 8, width), F32),
            [dma((5,)), dma((parts,)), dma((parts,)), dma((parts,)), dma((1,)), dma((1,))],
        ],
        compiler_params=pltpu.CompilerParams(
            collective_id=0, has_side_effects=True, vmem_limit_bytes=38 << 20
        ),
    )(*[pltpu.with_memory_space_constraint(x, pltpu.HBM) for x in (features, adjacency, cotangent, segments, weight, bias)])


def stencil_rows(stencil, scaled, slots, slot, first, start, span):
    for b in range(span // BLOCK):
        source = pl.multiple_of(start + b * BLOCK, BLOCK)
        slots[slot, pl.ds(b * BLOCK, BLOCK), :] = jnp.dot(
            stencil[pl.ds(first + source, BLOCK), :], scaled[pl.ds(source, BLOCK), :], preferred_element_type=F32
        )


def finish_kernel(
    early, span, activations, scaled, total, stencil,
    grad_features, out, grad_weight, grad_bias, slots, row, slot_sem, fixed_sem,
):
    depth = total.shape[0] - 8
    count = early // span
    row[...] = jnp.sum(total[pl.ds(depth, 8), :], axis=0, keepdims=True)
    fixed = [
        pltpu.make_async_copy(activations, out, fixed_sem.at[0]),
        pltpu.make_async_copy(total.at[pl.ds(0, depth)], grad_weight, fixed_sem.at[1]),
        pltpu.make_async_copy(row, grad_bias, fixed_sem.at[2]),
    ]
    for copy in fixed:
        copy.start()

    def store(k):
        slot = lax.rem(k, SLOTS)
        target = pl.ds(pl.multiple_of(k * span, span), span)
        return pltpu.make_async_copy(slots.at[slot], grad_features.at[target], slot_sem.at[slot])

    def step(k, carry):
        @pl.when(k >= SLOTS)
        def _():
            store(k - SLOTS).wait()

        stencil_rows(stencil, scaled, slots, lax.rem(k, SLOTS), 0, k * span, span)
        store(k).start()
        return carry

    lax.fori_loop(0, count, step, 0)
    for k in range(max(count - SLOTS, 0), count):
        store(k).wait()
    for copy in fixed:
        copy.wait()


def finish(activations, scaled, total, stencil, early, tile):
    rows, width = scaled.shape
    depth = total.shape[0] - 8
    dma = pltpu.SemaphoreType.DMA
    return pl.pallas_call(
        functools.partial(finish_kernel, early * tile, 2 * tile),
        in_specs=[VMEM] * 4,
        out_specs=[HBM] * 4,
        out_shape=[
            jax.ShapeDtypeStruct((rows, width), F32),
            jax.ShapeDtypeStruct((rows, width), BF16),
            jax.ShapeDtypeStruct((depth, width), F32),
            jax.ShapeDtypeStruct((1, width), F32),
        ],
        scratch_shapes=[
            pltpu.VMEM((SLOTS, 2 * tile, width), F32),
            pltpu.VMEM((1, width), F32),
            dma((SLOTS,)),
            dma((3,)),
        ],
        cost_estimate=pl.CostEstimate(
            flops=2 * rows * BLOCK * width, bytes_accessed=6 * rows * width + 4 * depth * width, transcendentals=0
        ),
        compiler_params=pltpu.CompilerParams(vmem_limit_bytes=12 << 20),
    )(activations, scaled, total, stencil)


def late_kernel(n, early, tile, *refs):
    grads, landing = refs[0], (None,) + refs[1:n]
    sten, mat, scaled, pieces, load_sem, far_out, far_in, near_out, near_in = refs[n + 1 :]
    outer = n // 2
    rows, width = grads.shape
    late = rows // tile - early
    kept = pl.ds(early * tile, late * tile)
    me = lax.axis_index("col")
    chip, core = me // 2, lax.rem(me, 2)
    sibling = chip * 2 + 1 - core

    def chip_at(shift):
        return lax.rem(chip + shift + outer, outer) * 2 + core

    def at(j):
        return pl.ds(pl.multiple_of(j * tile, tile), tile)

    def remote(source, target, send, recv, device):
        return pltpu.make_async_remote_copy(
            src_ref=source, dst_ref=target, send_sem=send, recv_sem=recv,
            device_id={"col": device}, device_id_type=MESH,
        )

    def load(p, part):
        source = landing[p] if p else grads
        first, size = ((0, 2 * tile), (2 * tile, (late - 2) * tile))[part]
        here = source.at[pl.ds(early * tile + first, size)]
        return pltpu.make_async_copy(here, pieces.at[p, pl.ds(first, size)], load_sem.at[part, p])

    def far(p, j):
        source = grads.at[pl.ds(pl.multiple_of((early + j) * tile, tile), tile)]
        return remote(source, pieces.at[p, at(j)], far_out.at[p], far_in.at[p // 2 - 1, j], chip_at(-(p // 2)))

    def near(p, j):
        return remote(pieces.at[p - 1, at(j)], pieces.at[p, at(j)], near_out.at[p], near_in.at[p // 2 - 1, j], sibling)

    barrier = pltpu.get_barrier_semaphore()

    @pl.when(core == 0)
    def _():
        for shift in range(1, outer):
            pl.semaphore_signal(barrier, inc=1, device_id={"col": chip_at(shift)}, device_id_type=MESH)
        pl.semaphore_wait(barrier, outer - 1)
        for j in range(late):
            for p in range(2, n, 2):
                far(p, j).start()
        pl.semaphore_signal(barrier, inc=1, device_id={"col": sibling}, device_id_type=MESH)
        for part in range(2):
            for p in range(2):
                load(p, part).start()
        pl.semaphore_wait(barrier, 1)

    @pl.when(core == 1)
    def _():
        for part in range(2):
            for p in range(n):
                if p < 2 or p % 2 == 0:
                    load(p, part).start()
        pl.semaphore_wait(barrier, 1)
        pl.semaphore_signal(barrier, inc=1, device_id={"col": sibling}, device_id_type=MESH)
        for part in range(2):
            for p in range(2, n, 2):
                load(p, part).wait()
            for j in ((0, 1), range(2, late))[part]:
                for p in range(3, n, 2):
                    near(p, j).start()

    def loaded(part):
        for p in range(2):
            load(p, part).wait()

    def take(j):
        @pl.when(core == 0)
        def _():
            for p in range(2, n, 2):
                far(p, j).wait_recv()
                near(p + 1, j).start()

    def wait_near(j):
        for p in range(3, n, 2):
            near(p, j).wait_recv()

    def products(j, size, numbers):
        rows = pl.ds(pl.multiple_of(j * tile, tile), size * tile)
        return back_through(lambda p: pieces[p, rows, :], numbers, mat)

    def store(j, size, value):
        rows = pl.ds(pl.multiple_of((early + j) * tile, tile), size * tile)
        scaled[pl.ds(pl.multiple_of(j * tile, tile), size * tile), :] = scale(value, sten[rows, :])

    def step(g, carry):
        for j in range(GROUP):
            take(GROUP * g + j)
        for j in range(GROUP):
            wait_near(GROUP * g + j)
        store(GROUP * g, GROUP, products(GROUP * g, GROUP, range(n)))
        return carry

    loaded(0)
    lax.fori_loop(0, 2 // GROUP, step, 0)
    loaded(1)
    lax.fori_loop(2 // GROUP, (late - 2) // GROUP, step, 0)
    last = late - 1
    take(last - 1)
    wait_near(last - 1)
    store(last - 1, 1, products(last - 1, 1, range(n)))
    first = [0, 1] + [2 * shift + 1 - core for shift in range(1, outer)]

    @pl.when(core == 0)
    def _():
        wait_near(last)

    value = products(last, 1, first)
    take(last)

    @pl.when(core == 1)
    def _():
        wait_near(last)

    store(last, 1, value + products(last, 1, [2 * shift + core for shift in range(1, outer)]))

    @pl.when(core == 0)
    def _():
        for p in range(2, n, 2):
            remote(grads.at[kept], pieces.at[p], far_out.at[p], far_in.at[p // 2 - 1, 0], chip_at(-(p // 2))).wait_send()

    for p in range(3, n, 2):
        remote(pieces.at[p - 1], pieces.at[p], near_out.at[p], near_in.at[p // 2 - 1, 0], sibling).wait_send()


def exchange_late(grads, landing, earlier, stencil, blocks, n, early, tile):
    rows, width = grads.shape
    late, outer = rows // tile - early, n // 2
    dma = pltpu.SemaphoreType.DMA
    far = [pltpu.with_memory_space_constraint(x, pltpu.HBM) for x in (grads, *landing, earlier)]
    return pl.pallas_call(
        functools.partial(late_kernel, n, early, tile),
        in_specs=[HBM] * (n + 1) + [VMEM] * 2,
        out_specs=VMEM,
        out_shape=pltpu.VMEM((late * tile, width), BF16),
        scratch_shapes=[
            pltpu.VMEM((n, late * tile, width), BF16),
            dma((2, n)),
            dma((n,)),
            dma((outer - 1, late)),
            dma((n,)),
            dma((outer - 1, late)),
        ],
        compiler_params=pltpu.CompilerParams(
            collective_id=1, has_side_effects=True, vmem_limit_bytes=20 << 20
        ),
    )(*far, stencil, blocks)


def finish_late_kernel(first, span, scaled, stencil, _, grad_features, slots, sem):
    count = scaled.shape[0] // span

    def store(k):
        return pltpu.make_async_copy(slots.at[k], grad_features.at[pl.ds(first + k * span, span)], sem.at[k])

    for k in range(count):
        stencil_rows(stencil, scaled, slots, k, first, k * span, span)
        store(k).start()
    for k in range(count):
        store(k).wait()


def finish_late(scaled, stencil, grad_features, early, tile):
    late, width = scaled.shape
    span = tile
    return pl.pallas_call(
        functools.partial(finish_late_kernel, early * tile, span),
        in_specs=[VMEM] * 2 + [HBM],
        out_specs=HBM,
        out_shape=jax.ShapeDtypeStruct(grad_features.shape, F32),
        input_output_aliases={2: 0},
        scratch_shapes=[pltpu.VMEM((late // span, span, width), F32), pltpu.SemaphoreType.DMA((late // span,))],
        cost_estimate=pl.CostEstimate(
            flops=2 * late * BLOCK * width, bytes_accessed=4 * late * width, transcendentals=0
        ),
        compiler_params=pltpu.CompilerParams(vmem_limit_bytes=12 << 20),
    )(scaled, stencil, grad_features)


def build(n, clusters):
    def local(features, weight, bias, adjacency, segments, cotangent):
        tile = 256 if n <= 4 else 512
        early = features.shape[0] // tile - TAIL
        activations, scaled, total, stencil, blocks, _, grads, *landing = exchange(
            features, adjacency, cotangent, segments, weight, bias, n, clusters, early, tile
        )
        grad_features, out, grad_weight, grad_bias = finish(activations, scaled, total, stencil, early, tile)
        scaled = exchange_late(grads, landing, grad_bias, stencil, blocks, n, early, tile)
        grad_features = finish_late(scaled, stencil, grad_features, early, tile)
        return (out, grad_features, grad_weight, grad_bias.reshape(-1))

    return local


def solution(mesh):
    return jax.shard_map(
        build(mesh.shape["col"], mesh.shape["clu"]),
        mesh=mesh,
        in_specs=(
            P("clu", "col"),
            P(None, "col"),
            P("col"),
            P("clu", None),
            P("clu", None),
            P("clu", "col"),
        ),
        out_specs=(P("clu", "col"), P("clu", "col"), P(None, "col"), P("col")),
        check_vma=False,
    )
```

```python
import functools

import jax
import jax.numpy as jnp
from jax import lax
from jax.experimental import pallas as pl
from jax.experimental.pallas import tpu as pltpu
from jax.sharding import PartitionSpec as P

BLOCK = 128
SLOTS = 4
TAIL = 6
GROUP = 2
F32 = jnp.float32
BF16 = jnp.bfloat16
MESH = pl.DeviceIdType.MESH
HBM = pl.BlockSpec(memory_space=pltpu.HBM)
VMEM = pl.BlockSpec(memory_space=pltpu.VMEM)


def stencil_of(adjacency, segment):
    columns = jnp.broadcast_to(segment, (BLOCK, BLOCK))
    links = jnp.where(columns == columns.T, adjacency, 0).astype(F32)
    inverse = 1.0 / (jnp.sum(links, axis=1, keepdims=True) + 1.0)
    row = lax.broadcasted_iota(jnp.int32, (BLOCK, BLOCK), 0)
    column = lax.broadcasted_iota(jnp.int32, (BLOCK, BLOCK), 1)
    return (links + jnp.where(row == column, 2.0, 0.0)).astype(BF16), inverse


def back_through(piece, numbers, blocks):
    width = blocks.shape[1]
    value = None
    for p in numbers:
        block = blocks[pl.ds(pl.multiple_of(p * width, width), width), :]
        term = lax.dot_general(piece(p), block, (((1,), (1,)), ((), ())), preferred_element_type=F32)
        value = term if value is None else value + term
    return value


def scale(value, stencil):
    inverse = 1.0 / (jnp.sum(stencil.astype(F32), axis=1, keepdims=True) - 1.0)
    return (value.astype(BF16).astype(F32) * inverse).astype(BF16)


class cluster_sum:
    PARTS = 4
    BACK = (5, 7, 8, 9)
    rounds = 10
    last = 12

    def __init__(self, total, result, half_in, quarter_in, bias_in, sems, clusters):
        self.result = result
        self.total, self.half_in, self.quarter_in, self.bias_in, self.sems = total, half_in, quarter_in, bias_in, sems
        self.clusters, self.high = clusters, clusters // 2
        self.depth = total.shape[0] - 8
        self.half = self.depth // self.PARTS // 2
        self.quarter = self.half // self.high
        self.me = lax.axis_index("clu")
        self.z, self.x = self.me // 2, lax.rem(self.me, 2)
        self.others = [lax.rem(self.me + d, clusters) for d in range(1, clusters)]
        self.levels = [lax.rem(self.z + d, self.high) for d in range(1, self.high)]

    def rows_of_half(self, c, x):
        return pl.ds(pl.multiple_of(c * 2 * self.half + x * self.half, self.half), self.half)

    def rows_of_quarter(self, c, q):
        start = c * 2 * self.half + self.x * self.half + q * self.quarter
        return pl.ds(pl.multiple_of(start, self.quarter), self.quarter)

    def copy(self, source, target, kind, recv, device):
        return pltpu.make_async_remote_copy(
            src_ref=source, dst_ref=target, send_sem=self.sems[0].at[kind],
            recv_sem=self.sems[1 + kind].at[recv], device_id={"clu": device}, device_id_type=MESH,
        )

    def several(self, rows, kind, recv=0):
        return self.copy(self.total.at[pl.ds(0, rows)], self.result.at[pl.ds(0, rows)], kind, recv, self.others[0])

    def give_half(self, c):
        rows = self.rows_of_half(c, 1 - self.x)
        return self.copy(self.total.at[rows], self.half_in.at[c], 0, c, self.z * 2 + 1 - self.x)

    def give_quarter(self, c, source, target):
        rows = self.rows_of_quarter(c, target)
        return self.copy(
            self.total.at[rows], self.quarter_in.at[c, source], 1, c, target * 2 + self.x
        )

    def return_quarter(self, c, source, target):
        rows = self.rows_of_quarter(c, source)
        return self.copy(
            self.result.at[rows], self.result.at[rows], 2, c, target * 2 + self.x
        )

    def return_half(self, c, x):
        rows = self.rows_of_half(c, x)
        return self.copy(self.result.at[rows], self.result.at[rows], 3, 0, self.z * 2 + 1 - self.x)

    def give_bias(self, source, target):
        return self.copy(
            self.total.at[pl.ds(self.depth, 8)], self.bias_in.at[source], 4, 0, target
        )

    def start(self):
        for c in range(self.PARTS):
            self.give_half(c).start()
        for other in self.others:
            self.give_bias(self.me, other).start()

    def advance(self, k):
        total = self.total
        if k < self.PARTS:
            self.give_half(k).wait_recv()
            total[self.rows_of_half(k, self.x), :] += self.half_in[k]
            for level in self.levels:
                self.give_quarter(k, self.z, level).start()
        c = k - 2
        if 0 <= c < self.PARTS:
            rows = self.rows_of_quarter(c, self.z)
            self.several(len(self.levels) * self.quarter, 1, c).wait_recv()
            value = total[rows, :]
            for level in self.levels:
                value = value + self.quarter_in[c, level]
            self.result[rows, :] = value
            for level in self.levels:
                self.return_quarter(c, self.z, level).start()
        if k in self.BACK:
            c = self.BACK.index(k)
            self.several(len(self.levels) * self.quarter, 2, c).wait_recv()
            self.return_half(c, self.x).start()

    def finish(self):
        halves = self.PARTS * self.half
        quarters = self.PARTS * len(self.levels) * self.quarter
        for kind, rows in enumerate((halves, quarters, quarters, halves, 8 * len(self.others))):
            self.several(rows, kind).wait_send()
        self.several(halves, 3).wait_recv()
        self.several(8 * len(self.others), 4).wait_recv()
        value = self.total[pl.ds(self.depth, 8), :]
        for other in self.others:
            value = value + self.bias_in[other]
        self.result[pl.ds(self.depth, 8), :] = value


def exchange_kernel(
    n, clusters, early, tile, features, adjacency, cotangent, segments, weight, bias,
    activations, scaled, summed_total, sten, mat, blocks_out, grads, *rest,
):
    landing = (None,) + rest[: n - 1]
    pieces = list(rest[n - 1 : 2 * n - 3])
    pieces = pieces[:1] + [activations] + pieces[1:] + [scaled]
    (feat, adj, cot, grad, seg, vec, total, shares, back, load_sem, cot_sem, grad_sem,
     fixed_sem, send_sem, far_in, near_in, grad_out, grad_far, grad_near, back_sem, share_send, share_recv, spread_send, spread_recv,
     block_send, block_recv, half_in, quarter_in, bias_in, sum_sems) = rest[2 * n - 3 :]
    outer = n // 2
    rows, width = features.shape
    depth = mat.shape[0]
    count = rows // tile
    me, cluster = lax.axis_index("col"), lax.axis_index("clu")
    chip, core = me // 2, lax.rem(me, 2)
    sibling = chip * 2 + 1 - core
    part = 2 * width // clusters
    others = [lax.rem(cluster + d, clusters) for d in range(1, clusters)]

    def chip_at(shift):
        return lax.rem(chip + shift + outer, outer) * 2 + core

    def at(k):
        return pl.ds(pl.multiple_of(k * tile, tile), tile)

    def pair(c):
        return pl.ds(pl.multiple_of(c * 2 * tile, 2 * tile), 2 * tile)

    def loads(k):
        slot = lax.rem(k, 2)
        return (
            pltpu.make_async_copy(features.at[at(k)], feat.at[slot], load_sem.at[0, slot]),
            pltpu.make_async_copy(adjacency.at[at(k)], adj.at[slot], load_sem.at[1, slot]),
        )

    def load_cot(k):
        slot = lax.rem(k, 2)
        return pltpu.make_async_copy(cotangent.at[at(k)], cot.at[slot], cot_sem.at[slot])

    def store_grad(k):
        slot = lax.rem(k, 2)
        return pltpu.make_async_copy(grad.at[slot], grads.at[at(k)], grad_sem.at[slot])

    def remote(source, target, send, recv, device, axis="col"):
        return pltpu.make_async_remote_copy(
            src_ref=source, dst_ref=target, send_sem=send, recv_sem=recv,
            device_id={axis: device}, device_id_type=MESH,
        )

    def hop(p, c):
        source = 0 if p % 2 == 0 else p - 1
        device = chip_at(-(p // 2)) if p % 2 == 0 else sibling
        arrival = far_in.at[p // 2 - 1, c] if p % 2 == 0 else near_in.at[c]
        return remote(pieces[source].at[pair(c)], pieces[p].at[pair(c)], send_sem.at[p], arrival, device)

    def grad_hop(p, c):
        rows = pair(c)
        source = grads if p < 2 or p % 2 == 0 else landing[p - 1]
        device = chip_at(-(p // 2)) if p % 2 == 0 else sibling
        arrival = grad_far.at[p // 2 - 1, c] if p % 2 == 0 else grad_near.at[c]
        return remote(source.at[rows], landing[p].at[rows], grad_out.at[p], arrival, device)

    def several(tiles, send, arrival):
        span = pl.ds(0, tiles * tile)
        return remote(grads.at[span], landing[1].at[span], send, arrival, sibling)

    border = early // 2 - 1

    def border_hop(p, i):
        rows, c = at(early - 2 + i), (border, count // 2)[i]
        source = landing[p - 1] if p % 2 else grads
        device = sibling if p % 2 else chip_at(-(p // 2))
        arrival = grad_near.at[c] if p % 2 else grad_far.at[p // 2 - 1, c]
        return remote(source.at[rows], landing[p].at[rows], grad_out.at[p], arrival, device)

    def pass_border(i):
        for p in range(2, n, 2):
            border_hop(p, i).wait_recv()
            border_hop(p + 1, i).start()
        several(outer - 1 + 2 * (1 - i), grad_out.at[0], grad_near.at[(border, count // 2)[i]]).wait_recv()
        for p in range(n):
            load_piece(p, early - 2 + i).start()

    def send_grad(c):
        @pl.when(c == border)
        def _():
            for i in range(2):
                for p in range(2, n, 2):
                    border_hop(p, i).start()

        @pl.when((c < border) | ((core == 1) & (c > border)))
        def _():
            for shift in range(1, outer):
                grad_hop(2 * shift, c).start()

        grad_hop(1, c).start()

    def load_piece(p, k):
        slot = lax.rem(k, 2)
        source = landing[p] if p else grads
        return pltpu.make_async_copy(source.at[at(k)], back.at[slot, pl.ds(p * tile, tile)], back_sem.at[slot])

    def share(shift):
        owner = lax.rem(chip - shift + outer, outer)
        rows = pl.ds(pl.multiple_of(owner * 2 * width + cluster * part, part), part)
        mine = pl.ds(pl.multiple_of(cluster * part, part), part)
        return remote(
            weight.at[rows], shares.at[shift, mine], share_send.at[shift - 1], share_recv.at[shift - 1], chip_at(-shift)
        )

    def spread(shift, source, peer):
        rows = pl.ds(pl.multiple_of(source * part, part), part)
        return remote(
            shares.at[shift, rows], shares.at[shift, rows],
            spread_send.at[shift - 1], spread_recv.at[shift - 1], peer, "clu",
        )

    def all_shares(shift):
        rows = pl.ds(0, len(others) * part)
        return remote(
            shares.at[shift, rows], shares.at[shift, rows], spread_send.at[shift - 1], spread_recv.at[shift - 1], others[0], "clu"
        )

    def block(p):
        half = core if p % 2 == 0 else 1 - core
        if p < 2:
            source = weight.at[pl.ds(pl.multiple_of((chip * 2 + half) * width, width), width)]
        else:
            source = shares.at[p // 2, pl.ds(pl.multiple_of(half * width, width), width)]
        if p % 2 == 0:
            return pltpu.make_async_copy(source, blocks_out.at[p], block_recv.at[p])
        return remote(source, blocks_out.at[p], block_send.at[p], block_recv.at[p], sibling)

    barrier = pltpu.get_barrier_semaphore()
    centre = clusters - 2 + core
    neighbours = [sibling] + [chip_at(shift) for shift in range(1, outer)]

    def greet(axis, peer):
        pl.semaphore_signal(barrier, inc=1, device_id={axis: peer}, device_id_type=MESH)

    for peer in neighbours:
        greet("col", peer)

    for copy in loads(0):
        copy.start()
    fixed = [
        pltpu.make_async_copy(source, target, fixed_sem.at[i])
        for i, (source, target) in enumerate([(segments, seg), (weight, mat), (bias, vec)])
    ]
    for copy in fixed:
        copy.start()
    load_cot(0).start()

    @pl.when(cluster == centre)
    def _():
        pl.semaphore_wait(barrier, len(neighbours) + len(others))
        for peer in others:
            greet("clu", peer)

    @pl.when(cluster != centre)
    def _():
        pl.semaphore_wait(barrier, len(neighbours))

    for shift in range(1, outer):
        share(shift).start()
    pl.when(cluster != centre)(functools.partial(greet, "clu", centre))
    block(0).start()
    block(1).start()
    fixed[0].wait()

    def aggregate_tile(k, carry):
        slot = lax.rem(k, 2)
        for copy in loads(k):
            copy.wait()

        @pl.when(k + 1 < count)
        def _():
            for copy in loads(k + 1):
                copy.start()

        for b in range(tile // BLOCK):
            part = pl.ds(b * BLOCK, BLOCK)
            stencil, inverse = stencil_of(adj[slot, part, :], seg[pl.ds(k * (tile // BLOCK) + b, 1), :])
            summed = jnp.dot(stencil, feat[slot, part, :], preferred_element_type=F32)
            target = pl.ds(pl.multiple_of(k * tile + b * BLOCK, BLOCK), BLOCK)
            sten[target, :] = stencil
            pieces[0][target, :] = (summed * inverse).astype(BF16)

        @pl.when(lax.rem(k, 2) == 1)
        def _():
            for shift in range(1, outer):
                hop(2 * shift, k // 2).start()
            hop(1, k // 2).start()

        return carry

    lax.fori_loop(0, count, aggregate_tile, 0)
    total[...] = jnp.zeros_like(total)
    fixed[1].wait()
    fixed[2].wait()
    blocks = [lax.rem(chip + p // 2, outer) * 2 + (core if p % 2 == 0 else 1 - core) for p in range(n)]

    def forward_tile(k):
        slot = lax.rem(k, 2)
        load_cot(k).wait()

        @pl.when(k + 1 < count)
        def _():
            load_cot(k + 1).start()

        @pl.when(lax.rem(k, 2) == 0)
        def _():
            several(2 * outer, send_sem.at[0], near_in.at[k // 2]).wait_recv()


        @pl.when(k >= 2)
        def _():
            store_grad(k - 2).wait()

        @pl.when((k >= 3) & (lax.rem(k, 2) == 1))
        def _():
            send_grad((k - 3) // 2)

        preact = None
        for p in range(n):
            source = pl.ds(pl.multiple_of(blocks[p] * width, width), width)
            term = jnp.dot(pieces[p][at(k), :], mat[source, :], preferred_element_type=F32)
            preact = term if preact is None else preact + term
        preact = preact + vec[...].astype(F32).reshape(1, width)
        grad_preact = jnp.where(preact > 0.0, cot[slot].astype(F32), 0.0)
        total[pl.ds(depth, 8), :] += jnp.sum(grad_preact.reshape(tile // 8, 8, width), axis=0)
        grad_preact = grad_preact.astype(BF16)
        grad[slot] = grad_preact

        store_grad(k).start()
        for p in range(n):
            target = pl.ds(pl.multiple_of(blocks[p] * width, width), width)
            total[target, :] += lax.dot_general(
                pieces[p][at(k), :], grad_preact, (((0,), (0,)), ((), ())), preferred_element_type=F32
            )
        activations[at(k), :] = jnp.maximum(preact, 0.0).astype(BF16)

    def step(k, carry):
        @pl.when((k < count) & (lax.rem(k, 2) == 0))
        def _():
            for shift in range(1, outer):
                hop(2 * shift, k // 2).wait_recv()
                hop(2 * shift + 1, k // 2).start()

        @pl.when((k == 2) & (cluster != centre))
        def _():
            pl.semaphore_wait(barrier, 1)

        @pl.when(k == 2)
        def _():
            for shift in range(1, outer):
                share(shift).wait_recv()
                for peer in others:
                    spread(shift, cluster, peer).start()

        @pl.when(k == 6)
        def _():
            for shift in range(1, outer):
                all_shares(shift).wait_recv()
                block(2 * shift).start()
                block(2 * shift + 1).start()

        @pl.when(k >= 1)
        def _():
            forward_tile(k - 1)

        return carry

    lax.fori_loop(0, count + 1, step, 0)
    sums = cluster_sum(total, summed_total, half_in, quarter_in, bias_in, sum_sems, clusters)
    sums.start()
    for k in (count - 2, count - 1):
        store_grad(k).wait()
    send_grad(count // 2 - 1)
    for p in range(1, n):
        several(count, send_sem.at[p], near_in.at[0]).wait_send()
    for p in range(1, n, 2):
        block(p).wait_send()
    for shift in range(1, outer):
        share(shift).wait_send()
        all_shares(shift).wait_send()
    for p in range(n):
        if p % 2:
            block(p).wait_recv()
        else:
            block(p).wait()
    copies = [
        pltpu.make_async_copy(blocks_out.at[p], mat.at[pl.ds(p * width, width)], block_send.at[p - p % 2])
        for p in range(0, n, 2)
    ] + [
        pltpu.make_async_copy(blocks_out.at[p], mat.at[pl.ds(p * width, width)], block_recv.at[p])
        for p in range(1, n, 2)
    ]
    for copy in copies:
        copy.start()
    for copy in copies:
        copy.wait()

    def backward_tile(k):
        slot = lax.rem(k, 2)
        pltpu.make_async_copy(grads.at[pl.ds(0, n * tile)], back.at[slot], back_sem.at[slot]).wait()
        scaled[at(k), :] = scale(back_through(lambda p: back[slot, pl.ds(p * tile, tile), :], range(n), mat), sten[at(k), :])

    def moment(r):
        return max(r * 512 // tile, 0)

    def back_step(k, carry):
        @pl.when(k >= 1)
        def _():
            backward_tile(k - 1)

        for i in range(2):
            pl.when(k == early - 2 + i)(functools.partial(pass_border, i))

        @pl.when((k < early - 2) & (lax.rem(k, 2) == 0))
        def _():
            for shift in range(1, outer):
                grad_hop(2 * shift, k // 2).wait_recv()
                grad_hop(2 * shift + 1, k // 2).start()
            several(2 * outer, grad_out.at[0], grad_near.at[k // 2]).wait_recv()
            for p in range(n):
                load_piece(p, k).start()
                load_piece(p, k + 1).start()

        for r in range(sums.rounds):
            if moment(r) <= early:
                pl.when(k == moment(r))(functools.partial(sums.advance, r))
        if moment(sums.last) <= early:
            pl.when(k == moment(sums.last))(sums.finish)
        return carry

    lax.fori_loop(0, early + 1, back_step, 0)
    for r in range(sums.rounds):
        if moment(r) > early:
            sums.advance(r)
    if moment(sums.last) > early:
        sums.finish()
    def late_step(c, carry):
        several(2, grad_out.at[0], grad_near.at[c]).wait_recv()

        @pl.when(core == 1)
        def _():
            for shift in range(1, outer):
                grad_hop(2 * shift, c).wait_recv()

        return carry

    for p in range(3, n, 2):
        several(early, grad_out.at[p], grad_near.at[0]).wait_send()
    several(count, grad_out.at[1], grad_near.at[0]).wait_send()
    lax.fori_loop(early // 2, count // 2, late_step, 0)

    @pl.when(core == 0)
    def _():
        for p in range(2, n, 2):
            several(early, grad_out.at[p], grad_near.at[0]).wait_send()

    @pl.when(core == 1)
    def _():
        for p in range(2, n, 2):
            several(count, grad_out.at[p], grad_near.at[0]).wait_send()


def exchange(features, adjacency, cotangent, segments, weight, bias, n, clusters, early, tile):
    rows, width = features.shape
    depth = weight.shape[0]
    count, outer = rows // tile, n // 2
    parts, high = cluster_sum.PARTS, clusters // 2
    dma = pltpu.SemaphoreType.DMA
    array = jax.ShapeDtypeStruct
    return pl.pallas_call(
        functools.partial(exchange_kernel, n, clusters, early, tile),
        in_specs=[HBM] * 6,
        out_specs=[VMEM] * 5 + [HBM] * (n + 1),
        out_shape=[
            pltpu.VMEM((rows, width), BF16),
            pltpu.VMEM((rows, width), BF16),
            pltpu.VMEM((depth + 8, width), F32),
            pltpu.VMEM((rows, BLOCK), BF16),
            pltpu.VMEM((depth, width), BF16),
            array((n, width, width), BF16),
        ]
        + [array((rows, width), BF16)] * n,
        scratch_shapes=[pltpu.VMEM((rows, width), BF16)] * (n - 2)
        + [
            pltpu.VMEM((2, tile, width), BF16),
            pltpu.VMEM((2, tile, BLOCK), jnp.int32),
            pltpu.VMEM((2, tile, width), BF16),
            pltpu.VMEM((2, tile, width), BF16),
            pltpu.VMEM(segments.shape, jnp.int32),
            pltpu.VMEM((width,), BF16),
            pltpu.VMEM((depth + 8, width), F32),
            pltpu.VMEM((outer, 2 * width, width), BF16),
            pltpu.VMEM((2, n * tile, width), BF16),
            dma((2, 2)),
            dma((2,)),
            dma((2,)),
            dma((3,)),
            dma((n,)),
            dma((outer - 1, count // 2)),
            dma((count // 2,)),
            dma((n,)),
            dma((outer - 1, count // 2 + 1)),
            dma((count // 2 + 1,)),
            dma((2,)),
            dma((outer - 1,)),
            dma((outer - 1,)),
            dma((outer - 1,)),
            dma((outer - 1,)),
            dma((n,)),
            dma((n,)),
            pltpu.VMEM((parts, depth // parts // 2, width), F32),
            pltpu.VMEM((parts, high, depth // parts // 2 // high, width), F32),
            pltpu.VMEM((clusters, 8, width), F32),
            [dma((5,)), dma((parts,)), dma((parts,)), dma((parts,)), dma((1,)), dma((1,))],
        ],
        compiler_params=pltpu.CompilerParams(
            collective_id=0, has_side_effects=True, vmem_limit_bytes=38 << 20
        ),
    )(*[pltpu.with_memory_space_constraint(x, pltpu.HBM) for x in (features, adjacency, cotangent, segments, weight, bias)])


def stencil_rows(stencil, scaled, slots, slot, first, start, span):
    for b in range(span // BLOCK):
        source = pl.multiple_of(start + b * BLOCK, BLOCK)
        slots[slot, pl.ds(b * BLOCK, BLOCK), :] = jnp.dot(
            stencil[pl.ds(first + source, BLOCK), :], scaled[pl.ds(source, BLOCK), :], preferred_element_type=F32
        )


def finish_kernel(
    early, span, activations, scaled, total, stencil,
    grad_features, out, grad_weight, grad_bias, slots, row, slot_sem, fixed_sem,
):
    depth = total.shape[0] - 8
    count = early // span
    row[...] = jnp.sum(total[pl.ds(depth, 8), :], axis=0, keepdims=True)
    fixed = [
        pltpu.make_async_copy(activations, out, fixed_sem.at[0]),
        pltpu.make_async_copy(total.at[pl.ds(0, depth)], grad_weight, fixed_sem.at[1]),
        pltpu.make_async_copy(row, grad_bias, fixed_sem.at[2]),
    ]
    for copy in fixed:
        copy.start()

    def store(k):
        slot = lax.rem(k, SLOTS)
        target = pl.ds(pl.multiple_of(k * span, span), span)
        return pltpu.make_async_copy(slots.at[slot], grad_features.at[target], slot_sem.at[slot])

    def step(k, carry):
        @pl.when(k >= SLOTS)
        def _():
            store(k - SLOTS).wait()

        stencil_rows(stencil, scaled, slots, lax.rem(k, SLOTS), 0, k * span, span)
        store(k).start()
        return carry

    lax.fori_loop(0, count, step, 0)
    for k in range(max(count - SLOTS, 0), count):
        store(k).wait()
    for copy in fixed:
        copy.wait()


def finish(activations, scaled, total, stencil, early, tile):
    rows, width = scaled.shape
    depth = total.shape[0] - 8
    dma = pltpu.SemaphoreType.DMA
    return pl.pallas_call(
        functools.partial(finish_kernel, early * tile, 2 * tile),
        in_specs=[VMEM] * 4,
        out_specs=[HBM] * 4,
        out_shape=[
            jax.ShapeDtypeStruct((rows, width), F32),
            jax.ShapeDtypeStruct((rows, width), BF16),
            jax.ShapeDtypeStruct((depth, width), F32),
            jax.ShapeDtypeStruct((1, width), F32),
        ],
        scratch_shapes=[
            pltpu.VMEM((SLOTS, 2 * tile, width), F32),
            pltpu.VMEM((1, width), F32),
            dma((SLOTS,)),
            dma((3,)),
        ],
        cost_estimate=pl.CostEstimate(
            flops=2 * rows * BLOCK * width, bytes_accessed=6 * rows * width + 4 * depth * width, transcendentals=0
        ),
        compiler_params=pltpu.CompilerParams(vmem_limit_bytes=12 << 20),
    )(activations, scaled, total, stencil)


def late_kernel(n, early, tile, *refs):
    grads, landing = refs[0], (None,) + refs[1:n]
    sten, mat, scaled, pieces, load_sem, far_out, far_in, near_out, near_in = refs[n + 1 :]
    outer = n // 2
    rows, width = grads.shape
    late = rows // tile - early
    kept = pl.ds(early * tile, late * tile)
    me = lax.axis_index("col")
    chip, core = me // 2, lax.rem(me, 2)
    sibling = chip * 2 + 1 - core

    def chip_at(shift):
        return lax.rem(chip + shift + outer, outer) * 2 + core

    def at(j):
        return pl.ds(pl.multiple_of(j * tile, tile), tile)

    def remote(source, target, send, recv, device):
        return pltpu.make_async_remote_copy(
            src_ref=source, dst_ref=target, send_sem=send, recv_sem=recv,
            device_id={"col": device}, device_id_type=MESH,
        )

    def load(p, part):
        source = landing[p] if p else grads
        first, size = ((0, 2 * tile), (2 * tile, (late - 2) * tile))[part]
        here = source.at[pl.ds(early * tile + first, size)]
        return pltpu.make_async_copy(here, pieces.at[p, pl.ds(first, size)], load_sem.at[part, p])

    def far(p, j):
        source = grads.at[pl.ds(pl.multiple_of((early + j) * tile, tile), tile)]
        return remote(source, pieces.at[p, at(j)], far_out.at[p], far_in.at[p // 2 - 1, j], chip_at(-(p // 2)))

    def near(p, j):
        return remote(pieces.at[p - 1, at(j)], pieces.at[p, at(j)], near_out.at[p], near_in.at[p // 2 - 1, j], sibling)

    barrier = pltpu.get_barrier_semaphore()

    @pl.when(core == 0)
    def _():
        for shift in range(1, outer):
            pl.semaphore_signal(barrier, inc=1, device_id={"col": chip_at(shift)}, device_id_type=MESH)
        pl.semaphore_wait(barrier, outer - 1)
        for j in range(late):
            for p in range(2, n, 2):
                far(p, j).start()
        pl.semaphore_signal(barrier, inc=1, device_id={"col": sibling}, device_id_type=MESH)
        for part in range(2):
            for p in range(2):
                load(p, part).start()
        pl.semaphore_wait(barrier, 1)

    @pl.when(core == 1)
    def _():
        for part in range(2):
            for p in range(n):
                if p < 2 or p % 2 == 0:
                    load(p, part).start()
        pl.semaphore_wait(barrier, 1)
        pl.semaphore_signal(barrier, inc=1, device_id={"col": sibling}, device_id_type=MESH)
        for part in range(2):
            for p in range(2, n, 2):
                load(p, part).wait()
            for j in ((0, 1), range(2, late))[part]:
                for p in range(3, n, 2):
                    near(p, j).start()

    def loaded(part):
        for p in range(2):
            load(p, part).wait()

    def take(j):
        @pl.when(core == 0)
        def _():
            for p in range(2, n, 2):
                far(p, j).wait_recv()
                near(p + 1, j).start()

    def wait_near(j):
        for p in range(3, n, 2):
            near(p, j).wait_recv()

    def products(j, size, numbers):
        rows = pl.ds(pl.multiple_of(j * tile, tile), size * tile)
        return back_through(lambda p: pieces[p, rows, :], numbers, mat)

    def store(j, size, value):
        rows = pl.ds(pl.multiple_of((early + j) * tile, tile), size * tile)
        scaled[pl.ds(pl.multiple_of(j * tile, tile), size * tile), :] = scale(value, sten[rows, :])

    def step(g, carry):
        for j in range(GROUP):
            take(GROUP * g + j)
        for j in range(GROUP):
            wait_near(GROUP * g + j)
        store(GROUP * g, GROUP, products(GROUP * g, GROUP, range(n)))
        return carry

    loaded(0)
    lax.fori_loop(0, 2 // GROUP, step, 0)
    loaded(1)
    lax.fori_loop(2 // GROUP, (late - 2) // GROUP, step, 0)
    last = late - 1
    take(last - 1)
    wait_near(last - 1)
    store(last - 1, 1, products(last - 1, 1, range(n)))
    first = [0, 1] + [2 * shift + 1 - core for shift in range(1, outer)]

    @pl.when(core == 0)
    def _():
        wait_near(last)

    value = products(last, 1, first)
    take(last)

    @pl.when(core == 1)
    def _():
        wait_near(last)

    store(last, 1, value + products(last, 1, [2 * shift + core for shift in range(1, outer)]))

    @pl.when(core == 0)
    def _():
        for p in range(2, n, 2):
            remote(grads.at[kept], pieces.at[p], far_out.at[p], far_in.at[p // 2 - 1, 0], chip_at(-(p // 2))).wait_send()

    for p in range(3, n, 2):
        remote(pieces.at[p - 1], pieces.at[p], near_out.at[p], near_in.at[p // 2 - 1, 0], sibling).wait_send()


def exchange_late(grads, landing, earlier, stencil, blocks, n, early, tile):
    rows, width = grads.shape
    late, outer = rows // tile - early, n // 2
    dma = pltpu.SemaphoreType.DMA
    far = [pltpu.with_memory_space_constraint(x, pltpu.HBM) for x in (grads, *landing, earlier)]
    return pl.pallas_call(
        functools.partial(late_kernel, n, early, tile),
        in_specs=[HBM] * (n + 1) + [VMEM] * 2,
        out_specs=VMEM,
        out_shape=pltpu.VMEM((late * tile, width), BF16),
        scratch_shapes=[
            pltpu.VMEM((n, late * tile, width), BF16),
            dma((2, n)),
            dma((n,)),
            dma((outer - 1, late)),
            dma((n,)),
            dma((outer - 1, late)),
        ],
        compiler_params=pltpu.CompilerParams(
            collective_id=1, has_side_effects=True, vmem_limit_bytes=20 << 20
        ),
    )(*far, stencil, blocks)


def finish_late_kernel(first, span, scaled, stencil, _, grad_features, slots, sem):
    count = scaled.shape[0] // span

    def store(k):
        return pltpu.make_async_copy(slots.at[k], grad_features.at[pl.ds(first + k * span, span)], sem.at[k])

    for k in range(count):
        stencil_rows(stencil, scaled, slots, k, first, k * span, span)
        store(k).start()
    for k in range(count):
        store(k).wait()


def finish_late(scaled, stencil, grad_features, early, tile):
    late, width = scaled.shape
    span = tile
    return pl.pallas_call(
        functools.partial(finish_late_kernel, early * tile, span),
        in_specs=[VMEM] * 2 + [HBM],
        out_specs=HBM,
        out_shape=jax.ShapeDtypeStruct(grad_features.shape, F32),
        input_output_aliases={2: 0},
        scratch_shapes=[pltpu.VMEM((late // span, span, width), F32), pltpu.SemaphoreType.DMA((late // span,))],
        cost_estimate=pl.CostEstimate(
            flops=2 * late * BLOCK * width, bytes_accessed=4 * late * width, transcendentals=0
        ),
        compiler_params=pltpu.CompilerParams(vmem_limit_bytes=12 << 20),
    )(scaled, stencil, grad_features)


def build(n, clusters):
    def local(features, weight, bias, adjacency, segments, cotangent):
        tile = 256 if n <= 4 else 512
        early = features.shape[0] // tile - TAIL
        activations, scaled, total, stencil, blocks, _, grads, *landing = exchange(
            features, adjacency, cotangent, segments, weight, bias, n, clusters, early, tile
        )
        grad_features, out, grad_weight, grad_bias = finish(activations, scaled, total, stencil, early, tile)
        scaled = exchange_late(grads, landing, grad_bias, stencil, blocks, n, early, tile)
        grad_features = finish_late(scaled, stencil, grad_features, early, tile)
        return (out, grad_features, grad_weight, grad_bias.reshape(-1))

    return local


def solution(mesh):
    return jax.shard_map(
        build(mesh.shape["col"], mesh.shape["clu"]),
        mesh=mesh,
        in_specs=(
            P("clu", "col"),
            P(None, "col"),
            P("col"),
            P("clu", None),
            P("clu", None),
            P("clu", "col"),
        ),
        out_specs=(P("clu", "col"), P("clu", "col"), P(None, "col"), P("col")),
        check_vma=False,
    )
```

```python
import functools

import jax
import jax.numpy as jnp
from jax import lax
from jax.experimental import pallas as pl
from jax.experimental.pallas import tpu as pltpu
from jax.sharding import PartitionSpec as P

BLOCK = 128
SLOTS = 4
TAIL = 6
GROUP = 1
F32 = jnp.float32
BF16 = jnp.bfloat16
MESH = pl.DeviceIdType.MESH
HBM = pl.BlockSpec(memory_space=pltpu.HBM)
VMEM = pl.BlockSpec(memory_space=pltpu.VMEM)


def stencil_of(adjacency, segment):
    columns = jnp.broadcast_to(segment, (BLOCK, BLOCK))
    links = jnp.where(columns == columns.T, adjacency, 0).astype(F32)
    inverse = 1.0 / (jnp.sum(links, axis=1, keepdims=True) + 1.0)
    row = lax.broadcasted_iota(jnp.int32, (BLOCK, BLOCK), 0)
    column = lax.broadcasted_iota(jnp.int32, (BLOCK, BLOCK), 1)
    return (links + jnp.where(row == column, 2.0, 0.0)).astype(BF16), inverse


def back_through(piece, numbers, blocks):
    width = blocks.shape[1]
    value = None
    for p in numbers:
        block = blocks[pl.ds(pl.multiple_of(p * width, width), width), :]
        term = lax.dot_general(piece(p), block, (((1,), (1,)), ((), ())), preferred_element_type=F32)
        value = term if value is None else value + term
    return value


def scale(value, stencil):
    inverse = 1.0 / (jnp.sum(stencil.astype(F32), axis=1, keepdims=True) - 1.0)
    return (value.astype(BF16).astype(F32) * inverse).astype(BF16)


class cluster_sum:
    PARTS = 4
    BACK = (5, 7, 8, 9)
    rounds = 10
    last = 12

    def __init__(self, total, result, half_in, quarter_in, bias_in, sems, clusters):
        self.result = result
        self.total, self.half_in, self.quarter_in, self.bias_in, self.sems = total, half_in, quarter_in, bias_in, sems
        self.clusters, self.high = clusters, clusters // 2
        self.depth = total.shape[0] - 8
        self.half = self.depth // self.PARTS // 2
        self.quarter = self.half // self.high
        self.me = lax.axis_index("clu")
        self.z, self.x = self.me // 2, lax.rem(self.me, 2)
        self.others = [lax.rem(self.me + d, clusters) for d in range(1, clusters)]
        self.levels = [lax.rem(self.z + d, self.high) for d in range(1, self.high)]

    def rows_of_half(self, c, x):
        return pl.ds(pl.multiple_of(c * 2 * self.half + x * self.half, self.half), self.half)

    def rows_of_quarter(self, c, q):
        start = c * 2 * self.half + self.x * self.half + q * self.quarter
        return pl.ds(pl.multiple_of(start, self.quarter), self.quarter)

    def copy(self, source, target, kind, recv, device):
        return pltpu.make_async_remote_copy(
            src_ref=source, dst_ref=target, send_sem=self.sems[0].at[kind],
            recv_sem=self.sems[1 + kind].at[recv], device_id={"clu": device}, device_id_type=MESH,
        )

    def several(self, rows, kind, recv=0):
        return self.copy(self.total.at[pl.ds(0, rows)], self.result.at[pl.ds(0, rows)], kind, recv, self.others[0])

    def give_half(self, c):
        rows = self.rows_of_half(c, 1 - self.x)
        return self.copy(self.total.at[rows], self.half_in.at[c], 0, c, self.z * 2 + 1 - self.x)

    def give_quarter(self, c, source, target):
        rows = self.rows_of_quarter(c, target)
        return self.copy(
            self.total.at[rows], self.quarter_in.at[c, source], 1, c, target * 2 + self.x
        )

    def return_quarter(self, c, source, target):
        rows = self.rows_of_quarter(c, source)
        return self.copy(
            self.result.at[rows], self.result.at[rows], 2, c, target * 2 + self.x
        )

    def return_half(self, c, x):
        rows = self.rows_of_half(c, x)
        return self.copy(self.result.at[rows], self.result.at[rows], 3, 0, self.z * 2 + 1 - self.x)

    def give_bias(self, source, target):
        return self.copy(
            self.total.at[pl.ds(self.depth, 8)], self.bias_in.at[source], 4, 0, target
        )

    def start(self):
        for c in range(self.PARTS):
            self.give_half(c).start()
        for other in self.others:
            self.give_bias(self.me, other).start()

    def advance(self, k):
        total = self.total
        if k < self.PARTS:
            self.give_half(k).wait_recv()
            total[self.rows_of_half(k, self.x), :] += self.half_in[k]
            for level in self.levels:
                self.give_quarter(k, self.z, level).start()
        c = k - 2
        if 0 <= c < self.PARTS:
            rows = self.rows_of_quarter(c, self.z)
            self.several(len(self.levels) * self.quarter, 1, c).wait_recv()
            value = total[rows, :]
            for level in self.levels:
                value = value + self.quarter_in[c, level]
            self.result[rows, :] = value
            for level in self.levels:
                self.return_quarter(c, self.z, level).start()
        if k in self.BACK:
            c = self.BACK.index(k)
            self.several(len(self.levels) * self.quarter, 2, c).wait_recv()
            self.return_half(c, self.x).start()

    def finish(self):
        halves = self.PARTS * self.half
        quarters = self.PARTS * len(self.levels) * self.quarter
        for kind, rows in enumerate((halves, quarters, quarters, halves, 8 * len(self.others))):
            self.several(rows, kind).wait_send()
        self.several(halves, 3).wait_recv()
        self.several(8 * len(self.others), 4).wait_recv()
        value = self.total[pl.ds(self.depth, 8), :]
        for other in self.others:
            value = value + self.bias_in[other]
        self.result[pl.ds(self.depth, 8), :] = value


def exchange_kernel(
    n, clusters, early, tile, features, adjacency, cotangent, segments, weight, bias,
    activations, scaled, summed_total, sten, mat, blocks_out, grads, *rest,
):
    landing = (None,) + rest[: n - 1]
    pieces = list(rest[n - 1 : 2 * n - 3])
    pieces = pieces[:1] + [activations] + pieces[1:] + [scaled]
    (feat, adj, cot, grad, seg, vec, total, shares, back, load_sem, cot_sem, grad_sem,
     fixed_sem, send_sem, far_in, near_in, grad_out, grad_far, grad_near, back_sem, share_send, share_recv, spread_send, spread_recv,
     block_send, block_recv, half_in, quarter_in, bias_in, sum_sems) = rest[2 * n - 3 :]
    outer = n // 2
    rows, width = features.shape
    depth = mat.shape[0]
    count = rows // tile
    me, cluster = lax.axis_index("col"), lax.axis_index("clu")
    chip, core = me // 2, lax.rem(me, 2)
    sibling = chip * 2 + 1 - core
    part = 2 * width // clusters
    others = [lax.rem(cluster + d, clusters) for d in range(1, clusters)]

    def chip_at(shift):
        return lax.rem(chip + shift + outer, outer) * 2 + core

    def at(k):
        return pl.ds(pl.multiple_of(k * tile, tile), tile)

    def pair(c):
        return pl.ds(pl.multiple_of(c * 2 * tile, 2 * tile), 2 * tile)

    def loads(k):
        slot = lax.rem(k, 2)
        return (
            pltpu.make_async_copy(features.at[at(k)], feat.at[slot], load_sem.at[0, slot]),
            pltpu.make_async_copy(adjacency.at[at(k)], adj.at[slot], load_sem.at[1, slot]),
        )

    def load_cot(k):
        slot = lax.rem(k, 2)
        return pltpu.make_async_copy(cotangent.at[at(k)], cot.at[slot], cot_sem.at[slot])

    def store_grad(k):
        slot = lax.rem(k, 2)
        return pltpu.make_async_copy(grad.at[slot], grads.at[at(k)], grad_sem.at[slot])

    def remote(source, target, send, recv, device, axis="col"):
        return pltpu.make_async_remote_copy(
            src_ref=source, dst_ref=target, send_sem=send, recv_sem=recv,
            device_id={axis: device}, device_id_type=MESH,
        )

    def hop(p, c):
        source = 0 if p % 2 == 0 else p - 1
        device = chip_at(-(p // 2)) if p % 2 == 0 else sibling
        arrival = far_in.at[p // 2 - 1, c] if p % 2 == 0 else near_in.at[c]
        return remote(pieces[source].at[pair(c)], pieces[p].at[pair(c)], send_sem.at[p], arrival, device)

    def grad_hop(p, c):
        rows = pair(c)
        source = grads if p < 2 or p % 2 == 0 else landing[p - 1]
        device = chip_at(-(p // 2)) if p % 2 == 0 else sibling
        arrival = grad_far.at[p // 2 - 1, c] if p % 2 == 0 else grad_near.at[c]
        return remote(source.at[rows], landing[p].at[rows], grad_out.at[p], arrival, device)

    def several(tiles, send, arrival):
        span = pl.ds(0, tiles * tile)
        return remote(grads.at[span], landing[1].at[span], send, arrival, sibling)

    border = early // 2 - 1

    def border_hop(p, i):
        rows, c = at(early - 2 + i), (border, count // 2)[i]
        source = landing[p - 1] if p % 2 else grads
        device = sibling if p % 2 else chip_at(-(p // 2))
        arrival = grad_near.at[c] if p % 2 else grad_far.at[p // 2 - 1, c]
        return remote(source.at[rows], landing[p].at[rows], grad_out.at[p], arrival, device)

    def pass_border(i):
        for p in range(2, n, 2):
            border_hop(p, i).wait_recv()
            border_hop(p + 1, i).start()
        several(outer - 1 + 2 * (1 - i), grad_out.at[0], grad_near.at[(border, count // 2)[i]]).wait_recv()
        for p in range(n):
            load_piece(p, early - 2 + i).start()

    def send_grad(c):
        @pl.when(c == border)
        def _():
            for i in range(2):
                for p in range(2, n, 2):
                    border_hop(p, i).start()

        @pl.when((c < border) | ((core == 1) & (c > border)))
        def _():
            for shift in range(1, outer):
                grad_hop(2 * shift, c).start()

        grad_hop(1, c).start()

    def load_piece(p, k):
        slot = lax.rem(k, 2)
        source = landing[p] if p else grads
        return pltpu.make_async_copy(source.at[at(k)], back.at[slot, p], back_sem.at[slot, p])

    def share(shift):
        owner = lax.rem(chip - shift + outer, outer)
        rows = pl.ds(pl.multiple_of(owner * 2 * width + cluster * part, part), part)
        mine = pl.ds(pl.multiple_of(cluster * part, part), part)
        return remote(
            weight.at[rows], shares.at[shift, mine], share_send.at[shift], share_recv.at[shift], chip_at(-shift)
        )

    def spread(shift, source, peer):
        rows = pl.ds(pl.multiple_of(source * part, part), part)
        return remote(
            shares.at[shift, rows], shares.at[shift, rows],
            spread_send.at[shift], spread_recv.at[shift], peer, "clu",
        )

    def all_shares(shift):
        rows = pl.ds(0, len(others) * part)
        return remote(
            shares.at[shift, rows], shares.at[shift, rows], spread_send.at[shift], spread_recv.at[shift], others[0], "clu"
        )

    def block(p):
        half = core if p % 2 == 0 else 1 - core
        if p < 2:
            source = weight.at[pl.ds(pl.multiple_of((chip * 2 + half) * width, width), width)]
        else:
            source = shares.at[p // 2, pl.ds(pl.multiple_of(half * width, width), width)]
        if p % 2 == 0:
            return pltpu.make_async_copy(source, blocks_out.at[p], block_recv.at[p])
        return remote(source, blocks_out.at[p], block_send.at[p], block_recv.at[p], sibling)

    barrier = pltpu.get_barrier_semaphore()
    centre = clusters - 2 + core
    neighbours = [sibling] + [chip_at(shift) for shift in range(1, outer)]

    def greet(axis, peer):
        pl.semaphore_signal(barrier, inc=1, device_id={axis: peer}, device_id_type=MESH)

    for peer in neighbours:
        greet("col", peer)

    for copy in loads(0):
        copy.start()
    fixed = [
        pltpu.make_async_copy(source, target, fixed_sem.at[i])
        for i, (source, target) in enumerate([(segments, seg), (weight, mat), (bias, vec)])
    ]
    for copy in fixed:
        copy.start()
    load_cot(0).start()

    @pl.when(cluster == centre)
    def _():
        pl.semaphore_wait(barrier, len(neighbours) + len(others))
        for peer in others:
            greet("clu", peer)

    @pl.when(cluster != centre)
    def _():
        pl.semaphore_wait(barrier, len(neighbours))

    for shift in range(1, outer):
        share(shift).start()
    pl.when(cluster != centre)(functools.partial(greet, "clu", centre))
    block(0).start()
    block(1).start()
    fixed[0].wait()

    def aggregate_tile(k, carry):
        slot = lax.rem(k, 2)
        for copy in loads(k):
            copy.wait()

        @pl.when(k + 1 < count)
        def _():
            for copy in loads(k + 1):
                copy.start()

        for b in range(tile // BLOCK):
            part = pl.ds(b * BLOCK, BLOCK)
            stencil, inverse = stencil_of(adj[slot, part, :], seg[pl.ds(k * (tile // BLOCK) + b, 1), :])
            summed = jnp.dot(stencil, feat[slot, part, :], preferred_element_type=F32)
            target = pl.ds(pl.multiple_of(k * tile + b * BLOCK, BLOCK), BLOCK)
            sten[target, :] = stencil
            pieces[0][target, :] = (summed * inverse).astype(BF16)

        @pl.when(lax.rem(k, 2) == 1)
        def _():
            for shift in range(1, outer):
                hop(2 * shift, k // 2).start()
            hop(1, k // 2).start()

        return carry

    lax.fori_loop(0, count, aggregate_tile, 0)
    total[...] = jnp.zeros_like(total)
    fixed[1].wait()
    fixed[2].wait()
    blocks = [lax.rem(chip + p // 2, outer) * 2 + (core if p % 2 == 0 else 1 - core) for p in range(n)]

    def forward_tile(k):
        slot = lax.rem(k, 2)
        load_cot(k).wait()

        @pl.when(k + 1 < count)
        def _():
            load_cot(k + 1).start()

        @pl.when(lax.rem(k, 2) == 0)
        def _():
            several(2 * outer, send_sem.at[0], near_in.at[k // 2]).wait_recv()


        @pl.when(k >= 2)
        def _():
            store_grad(k - 2).wait()

        @pl.when((k >= 3) & (lax.rem(k, 2) == 1))
        def _():
            send_grad((k - 3) // 2)

        preact = None
        for p in range(n):
            source = pl.ds(pl.multiple_of(blocks[p] * width, width), width)
            term = jnp.dot(pieces[p][at(k), :], mat[source, :], preferred_element_type=F32)
            preact = term if preact is None else preact + term
        preact = preact + vec[...].astype(F32).reshape(1, width)
        grad_preact = jnp.where(preact > 0.0, cot[slot].astype(F32), 0.0)
        total[pl.ds(depth, 8), :] += jnp.sum(grad_preact.reshape(tile // 8, 8, width), axis=0)
        grad_preact = grad_preact.astype(BF16)
        grad[slot] = grad_preact

        store_grad(k).start()
        for p in range(n):
            target = pl.ds(pl.multiple_of(blocks[p] * width, width), width)
            total[target, :] += lax.dot_general(
                pieces[p][at(k), :], grad_preact, (((0,), (0,)), ((), ())), preferred_element_type=F32
            )
        activations[at(k), :] = jnp.maximum(preact, 0.0).astype(BF16)

    def step(k, carry):
        @pl.when((k < count) & (lax.rem(k, 2) == 0))
        def _():
            for shift in range(1, outer):
                hop(2 * shift, k // 2).wait_recv()
                hop(2 * shift + 1, k // 2).start()

        @pl.when((k == 2) & (cluster != centre))
        def _():
            pl.semaphore_wait(barrier, 1)

        @pl.when(k == 2)
        def _():
            for shift in range(1, outer):
                share(shift).wait_recv()
                for peer in others:
                    spread(shift, cluster, peer).start()

        @pl.when(k == 6)
        def _():
            for shift in range(1, outer):
                all_shares(shift).wait_recv()
                block(2 * shift).start()
                block(2 * shift + 1).start()

        @pl.when(k >= 1)
        def _():
            forward_tile(k - 1)

        return carry

    lax.fori_loop(0, count + 1, step, 0)
    sums = cluster_sum(total, summed_total, half_in, quarter_in, bias_in, sum_sems, clusters)
    sums.start()
    for k in (count - 2, count - 1):
        store_grad(k).wait()
    send_grad(count // 2 - 1)
    for p in range(1, n):
        several(count, send_sem.at[p], near_in.at[0]).wait_send()
    for p in range(1, n, 2):
        block(p).wait_send()
    for shift in range(1, outer):
        share(shift).wait_send()
        all_shares(shift).wait_send()
    for p in range(n):
        if p % 2:
            block(p).wait_recv()
        else:
            block(p).wait()
    copies = [
        pltpu.make_async_copy(blocks_out.at[p], mat.at[pl.ds(p * width, width)], block_send.at[p - p % 2])
        for p in range(0, n, 2)
    ] + [
        pltpu.make_async_copy(blocks_out.at[p], mat.at[pl.ds(p * width, width)], block_recv.at[p])
        for p in range(1, n, 2)
    ]
    for copy in copies:
        copy.start()
    for copy in copies:
        copy.wait()

    def backward_tile(k):
        slot = lax.rem(k, 2)
        for p in range(n):
            load_piece(p, k).wait()
        scaled[at(k), :] = scale(back_through(lambda p: back[slot, p], range(n), mat), sten[at(k), :])

    def moment(r):
        return max(r * 512 // tile, 0)

    def back_step(k, carry):
        @pl.when(k >= 1)
        def _():
            backward_tile(k - 1)

        for i in range(2):
            pl.when(k == early - 2 + i)(functools.partial(pass_border, i))

        @pl.when((k < early - 2) & (lax.rem(k, 2) == 0))
        def _():
            for shift in range(1, outer):
                grad_hop(2 * shift, k // 2).wait_recv()
                grad_hop(2 * shift + 1, k // 2).start()
            several(2 * outer, grad_out.at[0], grad_near.at[k // 2]).wait_recv()
            for p in range(n):
                load_piece(p, k).start()
                load_piece(p, k + 1).start()

        for r in range(sums.rounds):
            if moment(r) <= early:
                pl.when(k == moment(r))(functools.partial(sums.advance, r))
        if moment(sums.last) <= early:
            pl.when(k == moment(sums.last))(sums.finish)
        return carry

    lax.fori_loop(0, early + 1, back_step, 0)
    for r in range(sums.rounds):
        if moment(r) > early:
            sums.advance(r)
    if moment(sums.last) > early:
        sums.finish()
    def late_step(c, carry):
        several(2, grad_out.at[0], grad_near.at[c]).wait_recv()

        @pl.when(core == 1)
        def _():
            for shift in range(1, outer):
                grad_hop(2 * shift, c).wait_recv()

        return carry

    for p in range(3, n, 2):
        several(early, grad_out.at[p], grad_near.at[0]).wait_send()
    several(count, grad_out.at[1], grad_near.at[0]).wait_send()
    lax.fori_loop(early // 2, count // 2, late_step, 0)

    @pl.when(core == 0)
    def _():
        for p in range(2, n, 2):
            several(early, grad_out.at[p], grad_near.at[0]).wait_send()

    @pl.when(core == 1)
    def _():
        for p in range(2, n, 2):
            several(count, grad_out.at[p], grad_near.at[0]).wait_send()


def exchange(features, adjacency, cotangent, segments, weight, bias, n, clusters, early, tile):
    rows, width = features.shape
    depth = weight.shape[0]
    count, outer = rows // tile, n // 2
    parts, high = cluster_sum.PARTS, clusters // 2
    dma = pltpu.SemaphoreType.DMA
    array = jax.ShapeDtypeStruct
    return pl.pallas_call(
        functools.partial(exchange_kernel, n, clusters, early, tile),
        in_specs=[HBM] * 6,
        out_specs=[VMEM] * 5 + [HBM] * (n + 1),
        out_shape=[
            pltpu.VMEM((rows, width), BF16),
            pltpu.VMEM((rows, width), BF16),
            pltpu.VMEM((depth + 8, width), F32),
            pltpu.VMEM((rows, BLOCK), BF16),
            pltpu.VMEM((depth, width), BF16),
            array((n, width, width), BF16),
        ]
        + [array((rows, width), BF16)] * n,
        scratch_shapes=[pltpu.VMEM((rows, width), BF16)] * (n - 2)
        + [
            pltpu.VMEM((2, tile, width), BF16),
            pltpu.VMEM((2, tile, BLOCK), jnp.int32),
            pltpu.VMEM((2, tile, width), BF16),
            pltpu.VMEM((2, tile, width), BF16),
            pltpu.VMEM(segments.shape, jnp.int32),
            pltpu.VMEM((width,), BF16),
            pltpu.VMEM((depth + 8, width), F32),
            pltpu.VMEM((outer, 2 * width, width), BF16),
            pltpu.VMEM((2, n, tile, width), BF16),
            dma((2, 2)),
            dma((2,)),
            dma((2,)),
            dma((3,)),
            dma((n,)),
            dma((outer - 1, count // 2)),
            dma((count // 2,)),
            dma((n,)),
            dma((outer - 1, count // 2 + 1)),
            dma((count // 2 + 1,)),
            dma((2, n)),
            dma((outer,)),
            dma((outer,)),
            dma((outer,)),
            dma((outer,)),
            dma((n,)),
            dma((n,)),
            pltpu.VMEM((parts, depth // parts // 2, width), F32),
            pltpu.VMEM((parts, high, depth // parts // 2 // high, width), F32),
            pltpu.VMEM((clusters, 8, width), F32),
            [dma((5,)), dma((parts,)), dma((parts,)), dma((parts,)), dma((1,)), dma((1,))],
        ],
        compiler_params=pltpu.CompilerParams(
            collective_id=0, has_side_effects=True, vmem_limit_bytes=38 << 20
        ),
    )(*[pltpu.with_memory_space_constraint(x, pltpu.HBM) for x in (features, adjacency, cotangent, segments, weight, bias)])


def stencil_rows(stencil, scaled, slots, slot, first, start, span):
    for b in range(span // BLOCK):
        source = pl.multiple_of(start + b * BLOCK, BLOCK)
        slots[slot, pl.ds(b * BLOCK, BLOCK), :] = jnp.dot(
            stencil[pl.ds(first + source, BLOCK), :], scaled[pl.ds(source, BLOCK), :], preferred_element_type=F32
        )


def finish_kernel(
    early, span, activations, scaled, total, stencil,
    grad_features, out, grad_weight, grad_bias, slots, row, slot_sem, fixed_sem,
):
    depth = total.shape[0] - 8
    count = early // span
    row[...] = jnp.sum(total[pl.ds(depth, 8), :], axis=0, keepdims=True)
    fixed = [
        pltpu.make_async_copy(activations, out, fixed_sem.at[0]),
        pltpu.make_async_copy(total.at[pl.ds(0, depth)], grad_weight, fixed_sem.at[1]),
        pltpu.make_async_copy(row, grad_bias, fixed_sem.at[2]),
    ]
    for copy in fixed:
        copy.start()

    def store(k):
        slot = lax.rem(k, SLOTS)
        target = pl.ds(pl.multiple_of(k * span, span), span)
        return pltpu.make_async_copy(slots.at[slot], grad_features.at[target], slot_sem.at[slot])

    def step(k, carry):
        @pl.when(k >= SLOTS)
        def _():
            store(k - SLOTS).wait()

        stencil_rows(stencil, scaled, slots, lax.rem(k, SLOTS), 0, k * span, span)
        store(k).start()
        return carry

    lax.fori_loop(0, count, step, 0)
    for k in range(max(count - SLOTS, 0), count):
        store(k).wait()
    for copy in fixed:
        copy.wait()


def finish(activations, scaled, total, stencil, early, tile):
    rows, width = scaled.shape
    depth = total.shape[0] - 8
    dma = pltpu.SemaphoreType.DMA
    return pl.pallas_call(
        functools.partial(finish_kernel, early * tile, 2 * tile),
        in_specs=[VMEM] * 4,
        out_specs=[HBM] * 4,
        out_shape=[
            jax.ShapeDtypeStruct((rows, width), F32),
            jax.ShapeDtypeStruct((rows, width), BF16),
            jax.ShapeDtypeStruct((depth, width), F32),
            jax.ShapeDtypeStruct((1, width), F32),
        ],
        scratch_shapes=[
            pltpu.VMEM((SLOTS, 2 * tile, width), F32),
            pltpu.VMEM((1, width), F32),
            dma((SLOTS,)),
            dma((3,)),
        ],
        cost_estimate=pl.CostEstimate(
            flops=2 * rows * BLOCK * width, bytes_accessed=6 * rows * width + 4 * depth * width, transcendentals=0
        ),
        compiler_params=pltpu.CompilerParams(vmem_limit_bytes=12 << 20),
    )(activations, scaled, total, stencil)


def late_kernel(n, early, tile, *refs):
    grads, landing = refs[0], (None,) + refs[1:n]
    sten, mat, scaled, pieces, load_sem, far_out, far_in, near_out, near_in = refs[n + 1 :]
    outer = n // 2
    rows, width = grads.shape
    late = rows // tile - early
    kept = pl.ds(early * tile, late * tile)
    me = lax.axis_index("col")
    chip, core = me // 2, lax.rem(me, 2)
    sibling = chip * 2 + 1 - core

    def chip_at(shift):
        return lax.rem(chip + shift + outer, outer) * 2 + core

    def at(j):
        return pl.ds(pl.multiple_of(j * tile, tile), tile)

    def remote(source, target, send, recv, device):
        return pltpu.make_async_remote_copy(
            src_ref=source, dst_ref=target, send_sem=send, recv_sem=recv,
            device_id={"col": device}, device_id_type=MESH,
        )

    def load(p, part):
        source = landing[p] if p else grads
        first, size = ((0, 2 * tile), (2 * tile, (late - 2) * tile))[part]
        here = source.at[pl.ds(early * tile + first, size)]
        return pltpu.make_async_copy(here, pieces.at[p, pl.ds(first, size)], load_sem.at[part, p])

    def far(p, j):
        source = grads.at[pl.ds(pl.multiple_of((early + j) * tile, tile), tile)]
        return remote(source, pieces.at[p, at(j)], far_out.at[p], far_in.at[p // 2 - 1, j], chip_at(-(p // 2)))

    def near(p, j):
        return remote(pieces.at[p - 1, at(j)], pieces.at[p, at(j)], near_out.at[p], near_in.at[p // 2 - 1, j], sibling)

    barrier = pltpu.get_barrier_semaphore()

    @pl.when(core == 0)
    def _():
        for shift in range(1, outer):
            pl.semaphore_signal(barrier, inc=1, device_id={"col": chip_at(shift)}, device_id_type=MESH)
        pl.semaphore_wait(barrier, outer - 1)
        for j in range(late):
            for p in range(2, n, 2):
                far(p, j).start()
        pl.semaphore_signal(barrier, inc=1, device_id={"col": sibling}, device_id_type=MESH)
        for part in range(2):
            for p in range(2):
                load(p, part).start()
        pl.semaphore_wait(barrier, 1)

    @pl.when(core == 1)
    def _():
        for part in range(2):
            for p in range(n):
                if p < 2 or p % 2 == 0:
                    load(p, part).start()
        pl.semaphore_wait(barrier, 1)
        pl.semaphore_signal(barrier, inc=1, device_id={"col": sibling}, device_id_type=MESH)
        for part in range(2):
            for p in range(2, n, 2):
                load(p, part).wait()
            for j in ((0, 1), range(2, late))[part]:
                for p in range(3, n, 2):
                    near(p, j).start()

    def loaded(part):
        for p in range(2):
            load(p, part).wait()

    def take(j):
        @pl.when(core == 0)
        def _():
            for p in range(2, n, 2):
                far(p, j).wait_recv()
                near(p + 1, j).start()

    def wait_near(j):
        for p in range(3, n, 2):
            near(p, j).wait_recv()

    def products(j, size, numbers):
        rows = pl.ds(pl.multiple_of(j * tile, tile), size * tile)
        return back_through(lambda p: pieces[p, rows, :], numbers, mat)

    def store(j, size, value):
        rows = pl.ds(pl.multiple_of((early + j) * tile, tile), size * tile)
        scaled[pl.ds(pl.multiple_of(j * tile, tile), size * tile), :] = scale(value, sten[rows, :])

    def step(g, carry):
        for j in range(GROUP):
            take(GROUP * g + j)
        for j in range(GROUP):
            wait_near(GROUP * g + j)
        store(GROUP * g, GROUP, products(GROUP * g, GROUP, range(n)))
        return carry

    loaded(0)
    lax.fori_loop(0, 2 // GROUP, step, 0)
    loaded(1)
    lax.fori_loop(2 // GROUP, (late - 2) // GROUP, step, 0)
    last = late - 1
    take(last - 1)
    wait_near(last - 1)
    store(last - 1, 1, products(last - 1, 1, range(n)))
    first = [0, 1] + [2 * shift + 1 - core for shift in range(1, outer)]

    @pl.when(core == 0)
    def _():
        wait_near(last)

    value = products(last, 1, first)
    take(last)

    @pl.when(core == 1)
    def _():
        wait_near(last)

    store(last, 1, value + products(last, 1, [2 * shift + core for shift in range(1, outer)]))

    @pl.when(core == 0)
    def _():
        for p in range(2, n, 2):
            remote(grads.at[kept], pieces.at[p], far_out.at[p], far_in.at[p // 2 - 1, 0], chip_at(-(p // 2))).wait_send()

    for p in range(3, n, 2):
        remote(pieces.at[p - 1], pieces.at[p], near_out.at[p], near_in.at[p // 2 - 1, 0], sibling).wait_send()


def exchange_late(grads, landing, earlier, stencil, blocks, n, early, tile):
    rows, width = grads.shape
    late, outer = rows // tile - early, n // 2
    dma = pltpu.SemaphoreType.DMA
    far = [pltpu.with_memory_space_constraint(x, pltpu.HBM) for x in (grads, *landing, earlier)]
    return pl.pallas_call(
        functools.partial(late_kernel, n, early, tile),
        in_specs=[HBM] * (n + 1) + [VMEM] * 2,
        out_specs=VMEM,
        out_shape=pltpu.VMEM((late * tile, width), BF16),
        scratch_shapes=[
            pltpu.VMEM((n, late * tile, width), BF16),
            dma((2, n)),
            dma((n,)),
            dma((outer - 1, late)),
            dma((n,)),
            dma((outer - 1, late)),
        ],
        compiler_params=pltpu.CompilerParams(
            collective_id=1, has_side_effects=True, vmem_limit_bytes=20 << 20
        ),
    )(*far, stencil, blocks)


def finish_late_kernel(first, span, scaled, stencil, _, grad_features, slots, sem):
    count = scaled.shape[0] // span

    def store(k):
        return pltpu.make_async_copy(slots.at[k], grad_features.at[pl.ds(first + k * span, span)], sem.at[k])

    for k in range(count):
        stencil_rows(stencil, scaled, slots, k, first, k * span, span)
        store(k).start()
    for k in range(count):
        store(k).wait()


def finish_late(scaled, stencil, grad_features, early, tile):
    late, width = scaled.shape
    span = tile
    return pl.pallas_call(
        functools.partial(finish_late_kernel, early * tile, span),
        in_specs=[VMEM] * 2 + [HBM],
        out_specs=HBM,
        out_shape=jax.ShapeDtypeStruct(grad_features.shape, F32),
        input_output_aliases={2: 0},
        scratch_shapes=[pltpu.VMEM((late // span, span, width), F32), pltpu.SemaphoreType.DMA((late // span,))],
        cost_estimate=pl.CostEstimate(
            flops=2 * late * BLOCK * width, bytes_accessed=4 * late * width, transcendentals=0
        ),
        compiler_params=pltpu.CompilerParams(vmem_limit_bytes=12 << 20),
    )(scaled, stencil, grad_features)


def build(n, clusters):
    def local(features, weight, bias, adjacency, segments, cotangent):
        tile = 256 if n <= 4 else 512
        early = features.shape[0] // tile - TAIL
        activations, scaled, total, stencil, blocks, _, grads, *landing = exchange(
            features, adjacency, cotangent, segments, weight, bias, n, clusters, early, tile
        )
        grad_features, out, grad_weight, grad_bias = finish(activations, scaled, total, stencil, early, tile)
        scaled = exchange_late(grads, landing, grad_bias, stencil, blocks, n, early, tile)
        grad_features = finish_late(scaled, stencil, grad_features, early, tile)
        return (out, grad_features, grad_weight, grad_bias.reshape(-1))

    return local


def solution(mesh):
    return jax.shard_map(
        build(mesh.shape["col"], mesh.shape["clu"]),
        mesh=mesh,
        in_specs=(
            P("clu", "col"),
            P(None, "col"),
            P("col"),
            P("clu", None),
            P("clu", None),
            P("clu", "col"),
        ),
        out_specs=(P("clu", "col"), P("clu", "col"), P(None, "col"), P("col")),
        check_vma=False,
    )
```
